32 devices in a mesh: grp: 4 (over x, core), seq: 4 (over z), tp: 2 (over y).
Axes of the slice: x: 2, y: 2, z: 4, core: 2. Of those that a mesh axis runs over, the one named last changes fastest.
Arguments:
- prompt_in: bfloat16 [4, 1536, 768], P('grp', 'seq'), may hold values from -6 to 6
- cont_in: bfloat16 [4, 4, 512, 768], P('grp', 'seq'), may hold values from -6 to 6
- prompt_cot: bfloat16 [4, 1536, 768], P('grp', 'seq'), may hold values from -6 to 6
- cont_cot: bfloat16 [4, 4, 512, 768], P('grp', 'seq'), may hold values from -6 to 6
- prompt_len: int32 [4, 4], P('grp', 'seq'), may hold values from 1 to 1536, as said below
- qkv_weight: bfloat16 [3, 768, 768], P(None, None, 'tp'), may hold values from -0.3125 to 0.3125
- out_weight: bfloat16 [768, 768], P('tp'), may hold values from -1.25 to 1.25
- ffn_in: bfloat16 [768, 3072], P(None, 'tp'), may hold values from -0.21875 to 0.21875
- ffn_out: bfloat16 [3072, 768], P('tp'), may hold values from -0.109375 to 0.109375
- norm_gain: bfloat16 [2, 768], replicated, may hold values from 0.5 to 1.5
- norm_shift: bfloat16 [2, 768], replicated, may hold values from -1.5 to 1.5
Outputs:
- prompt_out: bfloat16 [4, 1536, 768], P('grp', 'seq')
- cont_out: bfloat16 [4, 4, 512, 768], P('grp', 'seq')
- prompt_grad: bfloat16 [4, 1536, 768], P('grp', 'seq')
- cont_grad: bfloat16 [4, 4, 512, 768], P('grp', 'seq')
- qkv_weight_grad: float32 [3, 768, 768], P(None, 'seq', 'tp')
- out_weight_grad: float32 [768, 768], P('tp', 'seq')
- ffn_in_grad: float32 [768, 3072], P('seq', 'tp')
- ffn_out_grad: float32 [3072, 768], P('tp', 'seq')
- norm_gain_grad: float32 [2, 768], P(None, ('seq', 'tp'))
- norm_shift_grad: float32 [2, 768], P(None, ('seq', 'tp'))
The draws below stay inside these ranges and needn't reach their ends.
Inputs may be any that keep to these rules, and one draw needn't show every extreme that they name: prompt_len[g, c] counts the leading prompt tokens of group g that continuation c sees; in every group some continuation sees all 1536.
All inputs are finite; a program needn't handle non-finite values.
Results may differ from the reference program's by a relative error of at most 0.02.
Values may be sent and summed in bfloat16 or wider, within the bound.
No kernel may reach another device: no remote copies, remote signals or barrier semaphores. Data moves between devices by JAX's collectives and lax.ppermute only.
A program may use at most 256 MiB of HBM per device.

```python
import jax
import jax.numpy as jnp
from jax import lax

D = 768
HEADS = 12
HEAD = 64
FF = 3072
BLK = 512
GROUPS = 4
CONTS = 4
PROMPT = 1536


def draw_prompt_len(key, part):
    first_key, second_key = jax.random.split(jax.random.fold_in(key, 11))
    lengths = jax.random.randint(first_key, (GROUPS, CONTS), 1, PROMPT + 1)
    chosen = jax.random.randint(second_key, (GROUPS, 1), 0, CONTS)
    columns = jnp.arange(CONTS, dtype=jnp.int32)[None, :]
    return jnp.where(columns == chosen, PROMPT, lengths).astype(jnp.int32)


def block_scale(key, extent, pieces, smallest, high):
    def one(axis_at, blocks):
        steps = jax.random.uniform(jax.random.fold_in(jax.random.fold_in(key, 6), axis_at), (blocks,), jnp.float32, smallest / len(pieces), high / len(pieces))
        return jnp.repeat(jnp.exp(steps), extent[axis_at] // blocks).reshape((-1,) + (1,) * (len(extent) - axis_at - 1))

    loudness = one(*pieces[0])
    for cut in pieces[1:]:
        loudness = loudness * one(*cut)
    return loudness


def scatter_about(key, shape, spread, reach, cuts=(), held_as=jnp.bfloat16):
    array = spread * jax.random.normal(key, shape, jnp.float32)
    if cuts:
        array = array * block_scale(key, shape, cuts, -0.22, 0.18)
    return jnp.clip(array, -reach, reach).astype(held_as)


def setup_inputs(seed: int = 0) -> dict:
    splits = jax.random.split(jax.random.key(seed), 12)
    prompt_in = scatter_about(splits[0], (GROUPS, PROMPT, D), 1.0, 6.0, ((0, 4), (1, 4)))
    cont_in = scatter_about(splits[1], (GROUPS, CONTS, BLK, D), 1.0, 6.0, ((0, 4), (1, 4)))
    prompt_cot = scatter_about(splits[2], (GROUPS, PROMPT, D), 1.0, 6.0, ((0, 4), (1, 4)))
    cont_cot = scatter_about(splits[3], (GROUPS, CONTS, BLK, D), 1.0, 6.0, ((0, 4), (1, 4)))
    prompt_len = draw_prompt_len(jax.random.fold_in(splits[11], 71), 0)
    qkv_weight = scatter_about(splits[5], (3, D, D), (D // 2) ** -0.5, 0.3125, ((2, 2),))
    out_weight = scatter_about(splits[6], (D, D), (max(D // 32, 1)) ** -0.5, 1.25, ((0, 2),))
    ffn_in = scatter_about(splits[7], (D, FF), D ** -0.5, 0.21875, ((1, 2),))
    ffn_out = scatter_about(splits[8], (FF, D), FF ** -0.5, 0.109375, ((0, 2),))
    norm_gain = jnp.clip(1.0 + 0.1 * jax.random.normal(splits[9], (2, D), jnp.float32), 0.5, 1.5).astype(jnp.bfloat16)
    norm_shift = scatter_about(splits[10], (2, D), 0.3, 1.5)
    return dict(prompt_in=prompt_in, cont_in=cont_in, prompt_cot=prompt_cot, cont_cot=cont_cot, prompt_len=prompt_len, qkv_weight=qkv_weight, out_weight=out_weight, ffn_in=ffn_in, ffn_out=ffn_out, norm_gain=norm_gain, norm_shift=norm_shift)


norm_eps = 1e-05
hidden_value = -1e+30

@jax.custom_vjp
def low(v):
    return lax.optimization_barrier(v.astype(jnp.bfloat16)).astype(jnp.float32)

@jax.custom_vjp
def low_back(v):
    return v

def low_keep(v):
    return (low(v), None)

def low_pass(kept, grad):
    return (grad,)

def back_keep(v):
    return (v, None)

def back_low(kept, grad):
    return (low(grad),)
low.defvjp(low_keep, low_pass)
low_back.defvjp(back_keep, back_low)

def layer_norm(tokens, gain, shift):
    mean = lax.optimization_barrier(jnp.mean(tokens, axis=-1, keepdims=True))
    centred = tokens - mean
    variance = lax.optimization_barrier(jnp.mean(centred * centred, axis=-1, keepdims=True))
    return centred * lax.rsqrt(variance + norm_eps) * gain + shift

def attend(queries, keys, values, limit):
    scores = jnp.einsum('rhe,khe->hrk', queries, keys, precision=lax.Precision.HIGHEST) * HEAD ** (-0.5)
    scores = low_back(scores)
    position = jnp.arange(keys.shape[0], dtype=jnp.int32)
    visible = (position < limit) | (position >= PROMPT)
    scores = jnp.where(visible[None, None, :], scores, hidden_value)
    largest = lax.optimization_barrier(jnp.max(scores, axis=-1, keepdims=True))
    weights = jnp.exp(scores - largest)
    probs = low(weights / lax.optimization_barrier(jnp.sum(weights, axis=-1, keepdims=True)))
    return jnp.einsum('hrk,khe->rhe', probs, values, precision=lax.Precision.HIGHEST)

def checked_attend(queries, keys, values, limit):
    return jax.checkpoint(attend)(queries, keys, values, limit)

def group_layer(prompt_x, cont_x, lens, qkv_w, out_w, in_w, down_w, gain, shift):
    tokens = jnp.concatenate([prompt_x, cont_x.reshape(-1, D)], axis=0)
    count = tokens.shape[0]
    normed = low(layer_norm(tokens, gain[0], shift[0]))
    projected = jnp.einsum('nd,cde->cne', normed, qkv_w, precision=lax.Precision.HIGHEST)
    projected = low_back(low(projected))
    heads = projected.reshape(3, count, HEADS, HEAD)
    queries, keys, values = (heads[0], heads[1], heads[2])
    shared_keys = keys[:PROMPT]
    shared_values = values[:PROMPT]
    prompt_limit = jnp.int32(PROMPT)

    def prompt_block(block_queries):
        return checked_attend(block_queries, shared_keys, shared_values, prompt_limit)
    prompt_att = lax.map(prompt_block, queries[:PROMPT].reshape(PROMPT // BLK, BLK, HEADS, HEAD))

    def cont_block(items):
        block_queries, block_keys, block_values, limit = items
        all_keys = jnp.concatenate([shared_keys, block_keys], axis=0)
        all_values = jnp.concatenate([shared_values, block_values], axis=0)
        return checked_attend(block_queries, all_keys, all_values, limit)
    cont_att = lax.map(cont_block, (queries[PROMPT:].reshape(-1, BLK, HEADS, HEAD), keys[PROMPT:].reshape(-1, BLK, HEADS, HEAD), values[PROMPT:].reshape(-1, BLK, HEADS, HEAD), lens.astype(jnp.int32)))
    attended = jnp.concatenate([prompt_att.reshape(PROMPT, D), cont_att.reshape(-1, D)], axis=0)
    attended = low_back(low(attended))
    mixed = low_back(jnp.dot(attended, out_w, precision=lax.Precision.HIGHEST))
    resid = tokens + mixed
    normed_two = low(layer_norm(resid, gain[1], shift[1]))
    upper = low_back(jnp.dot(normed_two, in_w, precision=lax.Precision.HIGHEST))
    activated = low(jax.nn.gelu(upper, approximate=False))
    result = resid + jnp.dot(activated, down_w, precision=lax.Precision.HIGHEST)
    return (result[:PROMPT], result[PROMPT:].reshape(cont_x.shape))

def reference(prompt_in, cont_in, prompt_cot, cont_cot, prompt_len, qkv_weight, out_weight, ffn_in, ffn_out, norm_gain, norm_shift):
    floats = [a.astype(jnp.float32) for a in (prompt_in, cont_in, qkv_weight, out_weight, ffn_in, ffn_out, norm_gain, norm_shift)]

    def forward(prompt_x, cont_x, qkv_w, out_w, in_w, down_w, gain, shift):

        def one_group(items):
            return jax.checkpoint(group_layer)(items[0], items[1], items[2], qkv_w, out_w, in_w, down_w, gain, shift)
        return lax.map(one_group, (prompt_x, cont_x, prompt_len))
    outputs, pullback = jax.vjp(forward, *floats)
    grads = pullback((prompt_cot.astype(jnp.float32), cont_cot.astype(jnp.float32)))
    return (outputs[0].astype(jnp.bfloat16), outputs[1].astype(jnp.bfloat16), grads[0].astype(jnp.bfloat16), grads[1].astype(jnp.bfloat16), grads[2], grads[3], grads[4], grads[5], grads[6], grads[7])
```

```python
import jax
import jax.numpy as jnp
from jax import lax
from jax.sharding import PartitionSpec as P

HEAD = 64
CORES = 2
norm_eps = 1e-05
hidden_value = -1e30
BF = jnp.bfloat16
F32 = jnp.float32


def pick(array, index, axis):
    return lax.dynamic_index_in_dim(array, index, axis, keepdims=False)


def shift_perm(count, step):
    return [(j, (j + step) % count) for j in range(count)]


def group_perm(count, core_flip, step):
    chips = count // CORES
    return [
        (x * CORES + c, ((x + step) % chips) * CORES + (c ^ core_flip))
        for x in range(chips)
        for c in range(CORES)
    ]


def tp_sum(part):
    low = lax.optimization_barrier(part.astype(BF))
    other = lax.ppermute(low, "tp", shift_perm(lax.axis_size("tp"), 1))
    return low.astype(F32) + other.astype(F32)


def spread_sum(grad):
    seq_n = lax.axis_size("seq")
    grp_n = lax.axis_size("grp")
    chips = grp_n // CORES
    seq_i = lax.axis_index("seq")
    grp_i = lax.axis_index("grp")
    core_i = grp_i % CORES
    chip_i = grp_i // CORES
    rows = grad.shape[0] // (seq_n * grp_n)
    width = grad.shape[1]
    low = grad.astype(BF).reshape(seq_n, CORES, chips, rows, width)
    got = lax.ppermute(pick(low, 1 - core_i, 1), "grp", group_perm(grp_n, 1, 0))
    half = (pick(low, core_i, 1).astype(F32) + got.astype(F32)).astype(BF)
    total = pick(half, chip_i, 1).astype(F32)
    for step in range(1, chips):
        sent = pick(half, (chip_i + step) % chips, 1)
        total += lax.ppermute(sent, "grp", group_perm(grp_n, 0, step)).astype(F32)
    part = total.astype(BF)
    total = pick(part, seq_i, 0).astype(F32)
    for step in range(1, seq_n):
        sent = pick(part, (seq_i + step) % seq_n, 0)
        total += lax.ppermute(sent, "seq", shift_perm(seq_n, step)).astype(F32)
    mine = lax.optimization_barrier(total.astype(BF))
    line = jnp.zeros((chips, rows, width), BF)
    line = lax.dynamic_update_index_in_dim(line, mine, chip_i, 0)
    for step in range(1, chips):
        came = lax.ppermute(mine, "grp", group_perm(grp_n, 0, step))
        line = lax.dynamic_update_index_in_dim(line, came, (chip_i - step) % chips, 0)
    other = lax.ppermute(line, "grp", group_perm(grp_n, 1, 0))
    first = core_i == 0
    both = jnp.stack([jnp.where(first, line, other), jnp.where(first, other, line)])
    return both.reshape(CORES * chips * rows, width).astype(F32)


def norm_parts(tokens):
    mean = jnp.mean(tokens, axis=-1, keepdims=True)
    centred = tokens - mean
    variance = jnp.mean(centred * centred, axis=-1, keepdims=True)
    inv = lax.rsqrt(variance + norm_eps)
    return centred * inv, inv


def norm_back(normed, inv, upstream, gain):
    scaled = upstream * gain
    mean = jnp.mean(scaled, axis=-1, keepdims=True)
    inner = jnp.mean(scaled * normed, axis=-1, keepdims=True)
    return inv * (scaled - mean - normed * inner)


def exact_gelu(upper):
    return jax.nn.gelu(upper, approximate=False)


def body(
    prompt_in,
    cont_in,
    prompt_cot,
    cont_cot,
    prompt_len,
    qkv_weight,
    out_weight,
    ffn_in,
    ffn_out,
    norm_gain,
    norm_shift,
):
    prompt_rows = prompt_in.shape[1]
    width = prompt_in.shape[2]
    local_width = qkv_weight.shape[2]
    local_heads = local_width // HEAD
    scale = HEAD ** (-0.5)
    seq_n = lax.axis_size("seq")
    seq_i = lax.axis_index("seq")
    tp_n = lax.axis_size("tp")
    tokens = jnp.concatenate([prompt_in[0], cont_in[0, 0]], axis=0).astype(F32)
    row_count = tokens.shape[0]
    gains = norm_gain.astype(F32)
    shifts = norm_shift.astype(F32)
    normed_one, inv_one = norm_parts(tokens)
    first_low = (normed_one * gains[0] + shifts[0]).astype(BF)
    projected = jnp.einsum(
        "nd,cde->cne", first_low, qkv_weight, preferred_element_type=F32
    ).astype(BF)
    own_kv = projected[1:3, :prompt_rows]
    blocks = [own_kv]
    places = [seq_i]
    for step in range(1, seq_n):
        blocks.append(lax.ppermute(own_kv, "seq", shift_perm(seq_n, step)))
        places.append((seq_i - step) % seq_n)
    prompt_keys = seq_n * prompt_rows

    def split_heads(matrix):
        return matrix.reshape(matrix.shape[0], local_heads, HEAD).transpose(1, 0, 2)

    def join_heads(stacked):
        return stacked.transpose(1, 0, 2).reshape(stacked.shape[1], local_width)

    keyvals = jnp.concatenate(blocks + [projected[1:3, prompt_rows:]], axis=1)
    key_count = keyvals.shape[1]
    inside = jnp.arange(prompt_rows, dtype=jnp.int32)
    position = (jnp.stack(places)[:, None] * prompt_rows + inside[None, :]).reshape(-1)
    position = jnp.concatenate(
        [position, jnp.full((key_count - prompt_keys,), prompt_keys, jnp.int32)]
    )[None, :]
    row_index = jnp.arange(row_count, dtype=jnp.int32)[:, None]
    limit = jnp.where(row_index < prompt_rows, prompt_keys, prompt_len[0, 0])
    visible = (position < limit) | (position >= prompt_keys) & (row_index >= prompt_rows)
    head_queries = split_heads(projected[0])
    nothing = jnp.zeros((), F32)

    def head_scores(queries, keys):
        scores = jnp.einsum("ne,ke->nk", queries, keys, preferred_element_type=F32) * scale
        return jnp.where(visible, scores, hidden_value)

    def forward_head(carry, pieces):
        queries, keys, values = pieces
        scores = head_scores(queries, keys)
        largest = jnp.max(scores, axis=-1, keepdims=True)
        weights = jnp.exp(scores - largest)
        summed = jnp.sum(weights, axis=-1, keepdims=True)
        probs = (weights / summed).astype(BF)
        output = jnp.dot(probs, values, preferred_element_type=F32)
        return (carry, (output, largest[:, 0] + jnp.log(summed[:, 0])))

    _, (head_out, log_sums) = lax.scan(
        forward_head, nothing, (head_queries, split_heads(keyvals[0]), split_heads(keyvals[1]))
    )
    attended = join_heads(head_out).astype(BF)
    resid = tokens + tp_sum(jnp.dot(attended, out_weight, preferred_element_type=F32))
    normed_two, inv_two = norm_parts(resid)
    second_low = (normed_two * gains[1] + shifts[1]).astype(BF)
    upper = jnp.dot(second_low, ffn_in, preferred_element_type=F32)
    activated, gelu_pull = jax.vjp(exact_gelu, upper)
    act_low = activated.astype(BF)
    cotangent = jnp.concatenate([prompt_cot[0], cont_cot[0, 0]], axis=0)
    act_grad = jnp.einsum("nd,fd->nf", cotangent, ffn_out, preferred_element_type=F32)
    upper_grad = gelu_pull(act_grad)[0].astype(BF)
    second_terms = jnp.einsum("nf,df->nd", upper_grad, ffn_in, preferred_element_type=F32)
    second_grad = tp_sum(second_terms)
    in_grad = jnp.einsum("nd,nf->df", second_low, upper_grad, preferred_element_type=F32)
    down_grad = jnp.einsum("nd,nf->df", cotangent, act_low, preferred_element_type=F32)
    in_sum = spread_sum(in_grad)
    down_sum = spread_sum(down_grad)
    ffn_terms = jnp.dot(act_low, ffn_out, preferred_element_type=F32)
    result = (resid + tp_sum(ffn_terms)).astype(BF)
    prompt_out = result[:prompt_rows][None]
    cont_out = result[prompt_rows:][None, None]
    resid_grad = cotangent.astype(F32) + norm_back(normed_two, inv_two, second_grad, gains[1])
    mixed_low = resid_grad.astype(BF)
    mixing_grad = jnp.einsum("nd,ne->de", mixed_low, attended, preferred_element_type=F32)
    mixing_sum = spread_sum(mixing_grad)
    attended_grad = jnp.einsum("nd,ed->ne", mixed_low, out_weight, preferred_element_type=F32).astype(
        BF
    )

    def backward_head(carry, pieces):
        queries, keys, values, log_sum, head_grad = pieces
        scores = head_scores(queries, keys)
        probs = jnp.exp(scores - log_sum[:, None])
        prob_grad = jnp.einsum("ne,ke->nk", head_grad, values, preferred_element_type=F32)
        inner = jnp.sum(probs * prob_grad, axis=-1, keepdims=True)
        score_grad = (probs * (prob_grad - inner)).astype(BF)
        query_grad = jnp.dot(score_grad, keys, preferred_element_type=F32) * scale
        key_grad = jnp.einsum("nk,ne->ke", score_grad, queries, preferred_element_type=F32) * scale
        value_grad = jnp.einsum(
            "nk,ne->ke", probs.astype(BF), head_grad, preferred_element_type=F32
        )
        return (carry, (query_grad, key_grad, value_grad))

    _, (query_grads, key_grads, value_grads) = lax.scan(
        backward_head,
        nothing,
        (
            head_queries,
            split_heads(keyvals[0]),
            split_heads(keyvals[1]),
            log_sums,
            split_heads(attended_grad),
        ),
    )
    query_grad = join_heads(query_grads)
    keyval_grad = jnp.stack([join_heads(key_grads), join_heads(value_grads)])
    shared = keyval_grad[:, :prompt_rows]
    for step in range(1, seq_n):
        block = keyval_grad[:, step * prompt_rows : (step + 1) * prompt_rows].astype(BF)
        shared += lax.ppermute(block, "seq", shift_perm(seq_n, -step)).astype(F32)
    full = jnp.concatenate([shared, keyval_grad[:, prompt_keys:]], axis=1)
    proj_grad = jnp.concatenate([query_grad[None], full]).astype(BF)
    first_terms = jnp.einsum("cne,cde->nd", proj_grad, qkv_weight, preferred_element_type=F32)
    first_grad = tp_sum(first_terms)
    qkv_grad = jnp.einsum("nd,cne->dce", first_low, proj_grad, preferred_element_type=F32)
    qkv_sum = spread_sum(qkv_grad.reshape(width, 3 * local_width))
    token_grad = resid_grad + norm_back(normed_one, inv_one, first_grad, gains[0])
    prompt_grad = token_grad[:prompt_rows].astype(BF)[None]
    cont_grad = token_grad[prompt_rows:].astype(BF)[None, None]
    norm_rows = jnp.stack(
        [
            jnp.sum(first_grad * normed_one, axis=0),
            jnp.sum(second_grad * normed_two, axis=0),
            jnp.sum(first_grad, axis=0),
            jnp.sum(second_grad, axis=0),
        ]
    )
    norm_blocks = norm_rows.reshape(4, seq_n, tp_n, -1)
    norm_own = pick(norm_blocks, lax.axis_index("tp"), 2)
    total = pick(norm_own, seq_i, 1)
    for step in range(1, seq_n):
        sent = pick(norm_own, (seq_i + step) % seq_n, 1)
        total += lax.ppermute(sent, "seq", shift_perm(seq_n, step))
    grp_n = lax.axis_size("grp")
    part = total
    for step in range(1, grp_n // CORES):
        total += lax.ppermute(part, "grp", group_perm(grp_n, 0, step))
    total = lax.optimization_barrier(total)
    total = total + lax.ppermute(total, "grp", group_perm(grp_n, 1, 0))
    seq_rows = width // seq_n
    return (
        prompt_out,
        cont_out,
        prompt_grad,
        cont_grad,
        qkv_sum.reshape(seq_rows, 3, local_width).transpose(1, 0, 2),
        mixing_sum.T,
        in_sum,
        down_sum.T,
        total[:2],
        total[2:],
    )


def solution(mesh):
    placed = (
        P("grp", "seq", None),
        P("grp", "seq", None, None),
        P("grp", "seq", None),
        P("grp", "seq", None, None),
        P("grp", "seq"),
        P(None, None, "tp"),
        P("tp", None),
        P(None, "tp"),
        P("tp", None),
        P(),
        P(),
    )
    return jax.shard_map(
        body,
        mesh=mesh,
        in_specs=placed,
        out_specs=(
            P("grp", "seq", None),
            P("grp", "seq", None, None),
            P("grp", "seq", None),
            P("grp", "seq", None, None),
            P(None, "seq", "tp"),
            P("tp", "seq"),
            P("seq", "tp"),
            P("tp", "seq"),
            P(None, ("seq", "tp")),
            P(None, ("seq", "tp")),
        ),
        check_vma=False,
    )
```

```python
import functools

import jax
import jax.numpy as jnp
from jax import lax
from jax.experimental import pallas as pl
from jax.experimental.pallas import tpu as pltpu
from jax.sharding import PartitionSpec as P

HEAD = 64
CORES = 2
LANES = 128
norm_eps = 1e-05
hidden_value = -1e30
BF = jnp.bfloat16
F32 = jnp.float32
BUDGET = 56 * 1024 * 1024


def nt(left, right):
    return lax.dot_general(left, right, (((1,), (1,)), ((), ())), preferred_element_type=F32)


def tn(left, right):
    return lax.dot_general(left, right, (((0,), (0,)), ((), ())), preferred_element_type=F32)


def nn(left, right):
    return lax.dot_general(left, right, (((1,), (0,)), ((), ())), preferred_element_type=F32)


def one_head(pair, which, factor=None):
    lane = lax.broadcasted_iota(jnp.int32, pair.shape, 1)
    wide = pair.astype(F32)
    if factor is not None:
        wide = wide * factor
    return jnp.where((lane // HEAD) == which, wide, 0.0).astype(BF)


def attend_kernel(*refs, masked, prompt_rows):
    if masked:
        q_ref, ko_ref, vo_ref, kf_ref, vf_ref, bo_ref, bf_ref, out_ref, log_ref = refs
    else:
        q_ref, ko_ref, vo_ref, kf_ref, vf_ref, out_ref, log_ref = refs
    queries = q_ref[0]
    rows = queries.shape[0]
    own_keys = ko_ref.shape[1] if masked else prompt_rows
    near_values = vo_ref[0, :own_keys]
    far_values = vf_ref[0]
    outs = []
    tops = []
    for which in range(2):
        mine = one_head(queries, which, HEAD ** (-0.5))
        near = nt(ko_ref[0, :own_keys], mine)
        far = nt(kf_ref[0], mine)
        if masked:
            near = near + jnp.concatenate([bo_ref[...]] * (rows // LANES), axis=1)
            far = far + jnp.concatenate([bf_ref[...]] * (rows // LANES), axis=1)
        top = jnp.maximum(
            jnp.max(near, axis=0, keepdims=True), jnp.max(far, axis=0, keepdims=True)
        )
        near = jnp.exp(near - top)
        far = jnp.exp(far - top)
        total = jnp.sum(near, axis=0, keepdims=True) + jnp.sum(far, axis=0, keepdims=True)
        mixed = tn(near.astype(BF), near_values) + tn(far.astype(BF), far_values)
        outs.append(mixed / jnp.transpose(jnp.broadcast_to(total, (LANES, rows))))
        log_ref[0, which : which + 1] = top + jnp.log(total)
    lane = lax.broadcasted_iota(jnp.int32, outs[0].shape, 1)
    out_ref[...] = jnp.where(lane < HEAD, outs[0], outs[1]).astype(BF)


def attend(own, far, bias, first_row, rows, prompt_rows, block):
    masked = bias is not None
    width = own.shape[2]
    q = own[0, first_row : first_row + rows][None]

    def kind_spec(array, kind):
        return pl.BlockSpec((1, array.shape[1], LANES), lambda p, r: (kind, 0, p))

    specs = [
        pl.BlockSpec((1, block, LANES), lambda p, r: (0, r, p)),
        kind_spec(own, 1),
        kind_spec(own, 2),
        kind_spec(far, 0),
        kind_spec(far, 1),
    ]
    args = [q, own, own, far, far]
    if masked:
        specs += [pl.BlockSpec(b.shape, lambda p, r: (0, 0)) for b in bias]
        args += list(bias)
    keys = far.shape[1] + (own.shape[1] if masked else prompt_rows)
    return pl.pallas_call(
        functools.partial(attend_kernel, masked=masked, prompt_rows=prompt_rows),
        grid=(width // LANES, rows // block),
        in_specs=specs,
        out_specs=[
            pl.BlockSpec((block, LANES), lambda p, r: (r, p)),
            pl.BlockSpec((1, 8, block), lambda p, r: (p, 0, r)),
        ],
        out_shape=[
            jax.ShapeDtypeStruct((rows, width), BF),
            jax.ShapeDtypeStruct((width // LANES, 8, rows), F32),
        ],
        compiler_params=pltpu.CompilerParams(vmem_limit_bytes=BUDGET),
        cost_estimate=pl.CostEstimate(
            flops=8 * rows * keys * width, transcendentals=rows * keys * width // HEAD, bytes_accessed=4 * keys * width
        ),
    )(*args)


def pull_kernel(*refs, masked, prompt_rows, chunk):
    if masked:
        (q_ref, ko_ref, vo_ref, kf_ref, vf_ref, bo_ref, bf_ref, do_ref, out_ref, lse_ref,
         dq_ref, dko_ref, dvo_ref, dkf_ref, dvf_ref, dkc_ref, dvc_ref) = refs
    else:
        (q_ref, ko_ref, vo_ref, kf_ref, vf_ref, do_ref, out_ref, lse_ref, pko_ref, pvo_ref, pkf_ref, pvf_ref,
         dq_ref, dko_ref, dvo_ref, dkf_ref, dvf_ref) = refs
    upstream = do_ref[...]
    inner = jnp.transpose(upstream.astype(F32) * out_ref[...].astype(F32))
    queries = q_ref[0]
    rows = upstream.shape[0]
    heads = []
    for which in range(2):
        heads.append(
            (
                one_head(queries, which, HEAD ** (-0.5)),
                one_head(upstream, which),
                jnp.sum(inner[which * HEAD : (which + 1) * HEAD], axis=0, keepdims=True),
                lse_ref[0, which : which + 1],
            )
        )

    def piece(keys, values, bias):
        key_grad = None
        query_grads = []
        for mine, grad, delta, log in heads:
            scores = nt(keys, mine)
            if bias is not None:
                scores = scores + jnp.concatenate([bias] * (rows // LANES), axis=1)
            probs = jnp.exp(scores - log)
            spread = probs * (nt(values, grad) - delta)
            low = spread.astype(BF)
            dv = nn(probs.astype(BF), grad)
            dk = nn(low, mine)
            key_grad = dk if key_grad is None else key_grad + dk
            value_grad = dv if len(query_grads) == 0 else value_grad + dv
            query_grads.append(tn(low, keys))
        return key_grad, value_grad, query_grads

    dk, dv, acc = piece(
        ko_ref[0, :prompt_rows], vo_ref[0, :prompt_rows], bo_ref[:prompt_rows] if masked else None
    )
    if masked:
        dko_ref[...] = dk
        dvo_ref[...] = dv
        dk, dv, more = piece(ko_ref[0, prompt_rows:], vo_ref[0, prompt_rows:], None)
        dkc_ref[...] = dk.astype(BF)
        dvc_ref[...] = dv.astype(BF)
        acc = [a + b for a, b in zip(acc, more)]
    else:
        dko_ref[...] = (dk + pko_ref[...]).astype(BF)
        dvo_ref[...] = (dv + pvo_ref[...]).astype(BF)

    def far_step(at, acc):
        span = pl.ds(at, chunk)
        dk, dv, more = piece(kf_ref[0, span], vf_ref[0, span], bf_ref[span] if masked else None)
        if masked:
            dkf_ref[span] = dk
            dvf_ref[span] = dv
        else:
            dkf_ref[span] = (dk + pkf_ref[span]).astype(BF)
            dvf_ref[span] = (dv + pvf_ref[span]).astype(BF)
        return [a + b for a, b in zip(acc, more)]

    count = kf_ref.shape[1] // chunk
    if count <= 4:
        for step in range(count):
            acc = far_step(step * chunk, acc)
    else:
        acc = lax.fori_loop(
            0, count, lambda i, a: far_step(pl.multiple_of(i * chunk, chunk), a), acc
        )
    lane = lax.broadcasted_iota(jnp.int32, acc[0].shape, 1)
    dq_ref[...] = (jnp.where(lane < HEAD, acc[0], acc[1]) * HEAD ** (-0.5)).astype(BF)


def pull(own, far, bias, first_row, rows, grad, out, lse, before, prompt_rows):
    masked = bias is not None
    width = own.shape[2]
    far_n = far.shape[1]
    q = own[0, first_row : first_row + rows][None]

    def full(array_rows):
        return pl.BlockSpec((array_rows, LANES), lambda p: (0, p))

    def kind_spec(array, kind):
        return pl.BlockSpec((1, array.shape[1], LANES), lambda p: (kind, 0, p))

    specs = [kind_spec(q, 0), kind_spec(own, 1), kind_spec(own, 2), kind_spec(far, 0), kind_spec(far, 1)]
    args = [q, own, own, far, far]
    if masked:
        specs += [pl.BlockSpec(b.shape, lambda p: (0, 0)) for b in bias]
        args += list(bias)
    specs += [full(rows)] * 2 + [pl.BlockSpec((1, 8, rows), lambda p: (p, 0, 0))]
    args += [grad, out, lse]
    kind = F32 if masked else BF
    outs = [(rows, BF), (prompt_rows, kind), (prompt_rows, kind), (far_n, kind), (far_n, kind)]
    if masked:
        outs += [(own.shape[1] - prompt_rows, BF)] * 2
    else:
        specs += [full(b.shape[0]) for b in before]
        args += list(before)
    keys = far_n + (own.shape[1] if masked else prompt_rows)
    return pl.pallas_call(
        functools.partial(pull_kernel, masked=masked, prompt_rows=prompt_rows, chunk=prompt_rows),
        grid=(width // LANES,),
        in_specs=specs,
        out_specs=[full(n) for n, _ in outs],
        out_shape=[jax.ShapeDtypeStruct((n, width), t) for n, t in outs],
        compiler_params=pltpu.CompilerParams(vmem_limit_bytes=BUDGET),
        cost_estimate=pl.CostEstimate(
            flops=20 * rows * keys * width, transcendentals=rows * keys * width // HEAD, bytes_accessed=12 * keys * width
        ),
    )(*args)
def pick(array, index, axis):
    return lax.dynamic_index_in_dim(array, index, axis, keepdims=False)


def shift_perm(count, step):
    return [(j, (j + step) % count) for j in range(count)]


def group_perm(count, core_flip, step):
    chips = count // CORES
    return [
        (x * CORES + c, ((x + step) % chips) * CORES + (c ^ core_flip))
        for x in range(chips)
        for c in range(CORES)
    ]


def tp_swap(array):
    return lax.ppermute(array, "tp", shift_perm(lax.axis_size("tp"), 1))


def tp_sum(part):
    low = lax.optimization_barrier(part.astype(BF))
    return low.astype(F32) + tp_swap(low).astype(F32)


def spread_sum(grad):
    seq_n = lax.axis_size("seq")
    grp_n = lax.axis_size("grp")
    chips = grp_n // CORES
    seq_i = lax.axis_index("seq")
    grp_i = lax.axis_index("grp")
    core_i = grp_i % CORES
    chip_i = grp_i // CORES
    rows = grad.shape[0] // (seq_n * grp_n)
    width = grad.shape[1]
    low = grad.astype(BF).reshape(seq_n, CORES, chips, rows, width)
    got = lax.ppermute(pick(low, 1 - core_i, 1), "grp", group_perm(grp_n, 1, 0))
    half = (pick(low, core_i, 1).astype(F32) + got.astype(F32)).astype(BF)
    total = pick(half, chip_i, 1).astype(F32)
    for step in range(1, chips):
        sent = pick(half, (chip_i + step) % chips, 1)
        total += lax.ppermute(sent, "grp", group_perm(grp_n, 0, step)).astype(F32)
    part = total.astype(BF)
    total = pick(part, seq_i, 0).astype(F32)
    for step in range(1, seq_n):
        sent = pick(part, (seq_i + step) % seq_n, 0)
        total += lax.ppermute(sent, "seq", shift_perm(seq_n, step)).astype(F32)
    mine = lax.optimization_barrier(total.astype(BF))
    line = jnp.zeros((chips, rows, width), BF)
    line = lax.dynamic_update_index_in_dim(line, mine, chip_i, 0)
    for step in range(1, chips):
        came = lax.ppermute(mine, "grp", group_perm(grp_n, 0, step))
        line = lax.dynamic_update_index_in_dim(line, came, (chip_i - step) % chips, 0)
    other = lax.ppermute(line, "grp", group_perm(grp_n, 1, 0))
    first = core_i == 0
    both = jnp.stack([jnp.where(first, line, other), jnp.where(first, other, line)])
    return both.reshape(CORES * chips * rows, width)


def norm_parts(tokens):
    mean = jnp.mean(tokens, axis=-1, keepdims=True)
    centred = tokens - mean
    variance = jnp.mean(centred * centred, axis=-1, keepdims=True)
    inv = lax.rsqrt(variance + norm_eps)
    return centred * inv, inv


def norm_back(normed, inv, upstream, gain):
    scaled = upstream * gain
    mean = jnp.mean(scaled, axis=-1, keepdims=True)
    inner = jnp.mean(scaled * normed, axis=-1, keepdims=True)
    return inv * (scaled - mean - normed * inner)


def exact_gelu(upper):
    return jax.nn.gelu(upper, approximate=False)


def in_order(earlier, later):
    return lax.optimization_barrier((earlier, later))[1]


def body(
    prompt_in,
    cont_in,
    prompt_cot,
    cont_cot,
    prompt_len,
    qkv_weight,
    out_weight,
    ffn_in,
    ffn_out,
    norm_gain,
    norm_shift,
):
    rows_p = prompt_in.shape[1]
    half = rows_p // 2
    width = prompt_in.shape[2]
    local_width = qkv_weight.shape[2]
    seq_n = lax.axis_size("seq")
    seq_i = lax.axis_index("seq")
    tp_n = lax.axis_size("tp")
    tp_i = lax.axis_index("tp")
    gains = norm_gain.astype(F32)
    shifts = norm_shift.astype(F32)

    sent = lax.dynamic_slice_in_dim(prompt_in[0], tp_i * half, half, 0)
    pieces = []
    starts = []
    for step in range(1, seq_n):
        came = lax.ppermute(sent, "seq", shift_perm(seq_n, step))
        pieces += [came, tp_swap(came)]
        block = (seq_i - step) % seq_n * rows_p
        starts += [block + tp_i * half, block + (1 - tp_i) * half]
    far_in = jnp.concatenate(pieces, axis=0)
    inside = jnp.arange(half, dtype=jnp.int32)
    limit = prompt_len[0, 0]
    place = (jnp.stack(starts)[:, None] + inside[None, :]).reshape(-1)
    bias_far = jnp.where(place < limit, 0.0, hidden_value).astype(F32)
    place = seq_i * rows_p + jnp.arange(rows_p, dtype=jnp.int32)
    bias_own = jnp.concatenate(
        [
            jnp.where(place < limit, 0.0, hidden_value).astype(F32),
            jnp.zeros((cont_in.shape[2],), F32),
        ]
    )
    bias = tuple(jnp.broadcast_to(b[:, None], (b.shape[0], LANES)) for b in (bias_own, bias_far))

    tokens = jnp.concatenate([prompt_in[0], cont_in[0, 0]], axis=0).astype(F32)
    count = tokens.shape[0]
    rows_c = count - rows_p
    normed_one, inv_one = norm_parts(tokens)
    first_low = (normed_one * gains[0] + shifts[0]).astype(BF)
    own = jnp.einsum("nd,cde->cne", first_low, qkv_weight, preferred_element_type=F32).astype(BF)
    first_far = (norm_parts(far_in.astype(F32))[0] * gains[0] + shifts[0]).astype(BF)
    far = jnp.einsum(
        "nd,cde->cne", first_far, qkv_weight[1:], preferred_element_type=F32
    ).astype(BF)

    att_c, log_c = attend(own, far, bias, rows_p, rows_c, rows_p, rows_c)
    mixed_c = jnp.dot(att_c, out_weight, preferred_element_type=F32)
    att_p, log_p = attend(own, far, None, 0, rows_p, rows_p, rows_p)
    mixed_p = jnp.dot(att_p, out_weight, preferred_element_type=F32)

    def feed(token_rows, mixed, cot):
        resid = token_rows + tp_sum(mixed)
        normed, inv = norm_parts(resid)
        low = (normed * gains[1] + shifts[1]).astype(BF)
        upper = jnp.dot(low, ffn_in, preferred_element_type=F32)
        activated, gelu_pull = jax.vjp(exact_gelu, upper)
        act_low = activated.astype(BF)
        act_grad = jnp.einsum("nd,fd->nf", cot, ffn_out, preferred_element_type=F32)
        upper_grad = gelu_pull(act_grad)[0].astype(BF)
        terms = jnp.einsum("nf,df->nd", upper_grad, ffn_in, preferred_element_type=F32)
        return resid, normed, inv, low, act_low, upper_grad, tp_sum(terms)

    cot_c = cont_cot[0, 0]
    cot_p = prompt_cot[0]
    resid_c, normed_c, inv_c, low_c, act_c, up_c, second_c = feed(tokens[rows_p:], mixed_c, cot_c)
    resid_p, normed_p, inv_p, low_p, act_p, up_p, second_p = feed(tokens[:rows_p], mixed_p, cot_p)

    def rows_grad(left_c, right_c, left_p, right_p):
        return jnp.einsum(
            "nd,nf->df",
            jnp.concatenate([left_p, left_c]),
            jnp.concatenate([right_p, right_c]),
            preferred_element_type=F32,
        ).astype(BF)

    in_grad = rows_grad(low_c, up_c, low_p, up_p)
    down_grad = rows_grad(cot_c, act_c, cot_p, act_p)

    def rest(cot, normed, inv, second):
        return cot.astype(F32) + norm_back(normed, inv, second, gains[1])

    grad_c = rest(cot_c, normed_c, inv_c, second_c)
    grad_p = rest(cot_p, normed_p, inv_p, second_p)
    dm_c = grad_c.astype(BF)
    dm_p = grad_p.astype(BF)
    do_c = jnp.einsum("nd,ed->ne", dm_c, out_weight, preferred_element_type=F32).astype(BF)
    do_p = jnp.einsum("nd,ed->ne", dm_p, out_weight, preferred_element_type=F32).astype(BF)
    mixing_grad = rows_grad(dm_c, att_c, dm_p, att_p)
    wide_sum = spread_sum(jnp.concatenate([in_grad, down_grad, mixing_grad], axis=1))

    dq_c, *partial, dk_c, dv_c = pull(
        own, far, bias, rows_p, rows_c, do_c, att_c, log_c, None, rows_p
    )
    proj_c = jnp.stack([dq_c, dk_c, dv_c])
    terms_c = jnp.einsum("cne,cde->nd", proj_c, qkv_weight, preferred_element_type=F32)
    first_c = tp_sum(terms_c)
    dq_p, dk_p, dv_p, dk_f, dv_f = pull(
        own, far, None, 0, rows_p, do_p, att_p, log_p, partial, rows_p
    )
    proj_p = jnp.stack([dq_p, dk_p, dv_p])
    proj_f = jnp.stack([dk_f, dv_f])
    terms_p = jnp.einsum("cne,cde->nd", proj_p, qkv_weight, preferred_element_type=F32)
    terms_f = jnp.einsum("cne,cde->nd", proj_f, qkv_weight[1:], preferred_element_type=F32)
    terms_f = terms_f.astype(BF).reshape(seq_n - 1, 2, half, width)
    terms_p = terms_p.astype(BF).reshape(2, half, width)
    total = pick(terms_p, tp_i, 0).astype(F32) + tp_swap(pick(terms_p, 1 - tp_i, 0)).astype(F32)
    for step in range(1, seq_n):
        mine = terms_f[step - 1, 0].astype(F32) + tp_swap(terms_f[step - 1, 1]).astype(F32)
        back = lax.ppermute(mine.astype(BF), "seq", shift_perm(seq_n, -step))
        total += back.astype(F32)
    mine = lax.optimization_barrier(total.astype(BF))
    other = tp_swap(mine)
    first = tp_i == 0
    first_p = jnp.concatenate([jnp.where(first, mine, other), jnp.where(first, other, mine)])
    first_p = first_p.astype(F32)

    qkv_grad = jnp.einsum(
        "nd,cne->dce", first_low, jnp.concatenate([proj_p, proj_c], axis=1), preferred_element_type=F32
    )
    far_grad = jnp.einsum("nd,cne->dce", first_far, proj_f, preferred_element_type=F32)
    qkv_grad = jnp.concatenate([qkv_grad[:, :1], qkv_grad[:, 1:] + far_grad], axis=1)
    qkv_sum = spread_sum(qkv_grad.reshape(width, 3 * local_width)).astype(F32)

    ffn_terms_c = tp_sum(jnp.dot(act_c, ffn_out, preferred_element_type=F32))
    ffn_terms_p = tp_sum(jnp.dot(act_p, ffn_out, preferred_element_type=F32))
    cont_out = (resid_c + ffn_terms_c).astype(BF)[None, None]
    prompt_out = (resid_p + ffn_terms_p).astype(BF)[None]

    one_p, one_c = normed_one[:rows_p], normed_one[rows_p:]
    cont_grad = (grad_c + norm_back(one_c, inv_one[rows_p:], first_c, gains[0])).astype(BF)[None, None]
    prompt_grad = (grad_p + norm_back(one_p, inv_one[:rows_p], first_p, gains[0])).astype(BF)[None]

    def sums(a, b):
        return jnp.sum(a, axis=0) + jnp.sum(b, axis=0)

    norm_rows = jnp.stack(
        [
            sums(first_p * one_p, first_c * one_c),
            sums(second_p * normed_p, second_c * normed_c),
            sums(first_p, first_c),
            sums(second_p, second_c),
        ]
    )
    norm_blocks = norm_rows.reshape(4, seq_n, tp_n, -1)
    norm_own = pick(norm_blocks, tp_i, 2)
    total = pick(norm_own, seq_i, 1)
    for step in range(1, seq_n):
        piece = pick(norm_own, (seq_i + step) % seq_n, 1)
        total += lax.ppermute(piece, "seq", shift_perm(seq_n, step))
    grp_n = lax.axis_size("grp")
    part = total
    for step in range(1, grp_n // CORES):
        total += lax.ppermute(part, "grp", group_perm(grp_n, 0, step))
    total = lax.optimization_barrier(total)
    total = total + lax.ppermute(total, "grp", group_perm(grp_n, 1, 0))
    seq_rows = width // seq_n
    hidden = ffn_in.shape[1]
    return (
        prompt_out,
        cont_out,
        prompt_grad,
        cont_grad,
        qkv_sum.reshape(seq_rows, 3, local_width).transpose(1, 0, 2),
        wide_sum[:, 2 * hidden :].astype(F32).T,
        wide_sum[:, :hidden].astype(F32),
        wide_sum[:, hidden : 2 * hidden].astype(F32).T,
        total[:2],
        total[2:],
    )


def solution(mesh):
    placed = (
        P("grp", "seq", None),
        P("grp", "seq", None, None),
        P("grp", "seq", None),
        P("grp", "seq", None, None),
        P("grp", "seq"),
        P(None, None, "tp"),
        P("tp", None),
        P(None, "tp"),
        P("tp", None),
        P(),
        P(),
    )
    return jax.shard_map(
        body,
        mesh=mesh,
        in_specs=placed,
        out_specs=(
            P("grp", "seq", None),
            P("grp", "seq", None, None),
            P("grp", "seq", None),
            P("grp", "seq", None, None),
            P(None, "seq", "tp"),
            P("tp", "seq"),
            P("seq", "tp"),
            P("tp", "seq"),
            P(None, ("seq", "tp")),
            P(None, ("seq", "tp")),
        ),
        check_vma=False,
    )
```

```python
import functools

import jax
import jax.numpy as jnp
from jax import lax
from jax.experimental import pallas as pl
from jax.experimental.pallas import tpu as pltpu
from jax.sharding import PartitionSpec as P

HEAD = 64
CORES = 2
LANES = 128
norm_eps = 1e-05
hidden_value = -1e30
BF = jnp.bfloat16
F32 = jnp.float32
BUDGET = 56 * 1024 * 1024


def nt(left, right):
    return lax.dot_general(left, right, (((1,), (1,)), ((), ())), preferred_element_type=F32)


def tn(left, right):
    return lax.dot_general(left, right, (((0,), (0,)), ((), ())), preferred_element_type=F32)


def nn(left, right):
    return lax.dot_general(left, right, (((1,), (0,)), ((), ())), preferred_element_type=F32)


def one_head(pair, which, factor=None):
    lane = lax.broadcasted_iota(jnp.int32, pair.shape, 1)
    wide = pair.astype(F32)
    if factor is not None:
        wide = wide * factor
    return jnp.where((lane // HEAD) == which, wide, 0.0).astype(BF)


def lane_pair(pair):
    lane = lax.broadcasted_iota(jnp.int32, pair[0].shape, 1)
    return jnp.where(lane < HEAD, pair[0], pair[1])


def row_pair(pair):
    rows = pair[0].shape[1]
    return jnp.transpose(
        jnp.concatenate([jnp.broadcast_to(one, (HEAD, rows)) for one in pair], axis=0)
    )


def masked_scores(keys, mine, bias):
    scores = nt(keys, mine)
    if bias is None:
        return scores
    return scores + jnp.concatenate([bias] * (mine.shape[0] // LANES), axis=1)


def near_kernel(qp_ref, kp_ref, vp_ref, qc_ref, kc_ref, vc_ref, bias_ref, op_ref, sp_ref, oc_ref, sc_ref):
    parts = (
        (qp_ref, op_ref, sp_ref, [(kp_ref, vp_ref, None)]),
        (qc_ref, oc_ref, sc_ref, [(kp_ref, vp_ref, bias_ref), (kc_ref, vc_ref, None)]),
    )
    for q_ref, out_ref, stat_ref, sources in parts:
        outs = []
        for which in range(2):
            mine = one_head(q_ref[0], which, HEAD ** (-0.5))
            scores = [
                masked_scores(k_ref[0], mine, None if b_ref is None else b_ref[...])
                for k_ref, _, b_ref in sources
            ]
            top = functools.reduce(
                jnp.maximum, [jnp.max(s, axis=0, keepdims=True) for s in scores]
            )
            weights = [jnp.exp(s - top) for s in scores]
            stat_ref[0, which : which + 1] = top
            stat_ref[0, 2 + which : 3 + which] = sum(
                jnp.sum(w, axis=0, keepdims=True) for w in weights
            )
            outs.append(sum(tn(w.astype(BF), v_ref[0]) for w, (_, v_ref, _) in zip(weights, sources)))
        out_ref[...] = lane_pair(outs)


def kind_spec(array, kind):
    return pl.BlockSpec((1, array.shape[1], LANES), lambda p: (kind, 0, p))


def full_spec(rows):
    return pl.BlockSpec((rows, LANES), lambda p: (0, p))


def slab_spec(count, rows):
    return pl.BlockSpec((count, rows, LANES), lambda p: (0, 0, p))


def stat_spec(rows):
    return pl.BlockSpec((1, 8, rows), lambda p: (p, 0, 0))


def bias_spec(bias):
    return pl.BlockSpec(bias.shape, lambda p: (0, 0))


def params():
    return pltpu.CompilerParams(vmem_limit_bytes=BUDGET)


def cost(matmuls, pairs, width, moved):
    return pl.CostEstimate(flops=matmuls * pairs, transcendentals=0, bytes_accessed=moved)


def attend_near(own_p, own_c, bias):
    width = own_p.shape[2]
    outs = []
    for own in (own_p, own_c):
        rows = own.shape[1]
        outs += [
            jax.ShapeDtypeStruct((rows, width), F32),
            jax.ShapeDtypeStruct((width // LANES, 8, rows), F32),
        ]
    rows_p, rows_c = own_p.shape[1], own_c.shape[1]
    return pl.pallas_call(
        near_kernel,
        grid=(width // LANES,),
        in_specs=[kind_spec(own_p, c) for c in range(3)]
        + [kind_spec(own_c, c) for c in range(3)]
        + [bias_spec(bias)],
        out_specs=[full_spec(rows_p), stat_spec(rows_p), full_spec(rows_c), stat_spec(rows_c)],
        out_shape=outs,
        compiler_params=params(),
        cost_estimate=cost(2, rows_p * rows_p + rows_c * (rows_p + rows_c), width, 10 * rows_c),
    )(own_p, own_p, own_p, own_c, own_c, own_c, bias)


def far_kernel(*refs, masked):
    if masked:
        q_ref, k_ref, v_ref, bias_ref, part_ref, stat_ref, out_ref, log_ref = refs
    else:
        q_ref, k_ref, v_ref, part_ref, stat_ref, out_ref, log_ref = refs
    outs = []
    olds = []
    news = []
    for which in range(2):
        mine = one_head(q_ref[0], which, HEAD ** (-0.5))
        scores = masked_scores(k_ref[0], mine, bias_ref[...] if masked else None)
        old = stat_ref[0, which : which + 1]
        top = jnp.maximum(old, jnp.max(scores, axis=0, keepdims=True))
        weights = jnp.exp(scores - top)
        shrink = jnp.exp(old - top)
        total = shrink * stat_ref[0, 2 + which : 3 + which] + jnp.sum(
            weights, axis=0, keepdims=True
        )
        outs.append(tn(weights.astype(BF), v_ref[0]))
        olds.append(shrink / total)
        news.append(1.0 / total)
        log_ref[0, which : which + 1] = top + jnp.log(total)
    out = lane_pair(outs) * row_pair(news) + part_ref[...] * row_pair(olds)
    out_ref[...] = out.astype(BF)


def attend_far(own, far, bias, part, stat):
    masked = bias is not None
    rows = own.shape[1]
    width = own.shape[2]
    specs = [kind_spec(own, 0), kind_spec(far, 0), kind_spec(far, 1)]
    args = [own, far, far]
    if masked:
        specs.append(bias_spec(bias))
        args.append(bias)
    return pl.pallas_call(
        functools.partial(far_kernel, masked=masked),
        grid=(width // LANES,),
        in_specs=specs + [full_spec(rows), stat_spec(rows)],
        out_specs=[full_spec(rows), stat_spec(rows)],
        out_shape=[
            jax.ShapeDtypeStruct((rows, width), BF),
            jax.ShapeDtypeStruct((width // LANES, 8, rows), F32),
        ],
        compiler_params=params(),
        cost_estimate=cost(2, rows * far.shape[1], width, 4 * far.shape[1]),
    )(*args, part, stat)


def pull_heads(q_ref, do_ref, out_ref, log_ref):
    upstream = do_ref[...]
    inner = jnp.transpose(upstream.astype(F32) * out_ref[...].astype(F32))
    return [
        (
            one_head(q_ref[0], which, HEAD ** (-0.5)),
            one_head(upstream, which),
            jnp.sum(inner[which * HEAD : (which + 1) * HEAD], axis=0, keepdims=True),
            log_ref[0, which : which + 1],
        )
        for which in range(2)
    ]


def pull_piece(keys, values, bias, heads):
    key_grads = []
    value_grads = []
    query_grads = []
    for mine, grad, delta, log in heads:
        probs = jnp.exp(masked_scores(keys, mine, bias) - log)
        spread = probs * (nt(values, grad) - delta)
        low = spread.astype(BF)
        value_grads.append(nn(probs.astype(BF), grad))
        key_grads.append(nn(low, mine))
        query_grads.append(tn(low, keys))
    return key_grads[0] + key_grads[1], value_grads[0] + value_grads[1], query_grads


def pull_far_kernel(*refs, masked, chunk):
    if masked:
        q_ref, k_ref, v_ref, bias_ref, do_ref, out_ref, log_ref, dq_ref, dkv_ref = refs
    else:
        q_ref, k_ref, v_ref, do_ref, out_ref, log_ref, old_ref, dq_ref, dkv_ref = refs
    heads = pull_heads(q_ref, do_ref, out_ref, log_ref)

    def step(at, acc):
        span = pl.ds(at, chunk)
        bias = bias_ref[span] if masked else None
        dk, dv, more = pull_piece(k_ref[0, span], v_ref[0, span], bias, heads)
        if not masked:
            dk += old_ref[0, span]
            dv += old_ref[1, span]
        dkv_ref[0, span] = dk.astype(dkv_ref.dtype)
        dkv_ref[1, span] = dv.astype(dkv_ref.dtype)
        return more if acc is None else [a + b for a, b in zip(acc, more)]

    acc = step(0, None)
    count = k_ref.shape[1] // chunk
    if count <= 4:
        for i in range(1, count):
            acc = step(i * chunk, acc)
    else:
        acc = lax.fori_loop(
            1, count, lambda i, a: step(pl.multiple_of(i * chunk, chunk), a), acc
        )
    dq_ref[...] = lane_pair(acc) * HEAD ** (-0.5)


def pull_far(own, far, bias, grad, out, log, before, chunk):
    masked = bias is not None
    rows = own.shape[1]
    width = own.shape[2]
    keys = far.shape[1]
    specs = [kind_spec(own, 0), kind_spec(far, 0), kind_spec(far, 1)]
    args = [own, far, far]
    if masked:
        specs.append(bias_spec(bias))
        args.append(bias)
    specs += [full_spec(rows), full_spec(rows), stat_spec(rows)]
    args += [grad, out, log]
    if not masked:
        specs.append(slab_spec(2, keys))
        args.append(before)
    kind = F32 if masked else BF
    return pl.pallas_call(
        functools.partial(pull_far_kernel, masked=masked, chunk=chunk),
        grid=(width // LANES,),
        in_specs=specs,
        out_specs=[full_spec(rows), slab_spec(2, keys)],
        out_shape=[
            jax.ShapeDtypeStruct((rows, width), F32),
            jax.ShapeDtypeStruct((2, keys, width), kind),
        ],
        compiler_params=params(),
        cost_estimate=cost(5, rows * keys, width, 8 * keys),
    )(*args)


def pull_near_kernel(
    qp_ref, kp_ref, vp_ref, qc_ref, kc_ref, vc_ref, bias_ref,
    dop_ref, outp_ref, logp_ref, oldp_ref, doc_ref, outc_ref, logc_ref, oldc_ref,
    grad_ref,
):
    heads_p = pull_heads(qp_ref, dop_ref, outp_ref, logp_ref)
    heads_c = pull_heads(qc_ref, doc_ref, outc_ref, logc_ref)
    dk_p, dv_p, dq_p = pull_piece(kp_ref[0], vp_ref[0], None, heads_p)
    dk_pc, dv_pc, dq_pc = pull_piece(kp_ref[0], vp_ref[0], bias_ref[...], heads_c)
    dk_c, dv_c, dq_c = pull_piece(kc_ref[0], vc_ref[0], None, heads_c)
    split = qp_ref.shape[1]
    both = [a + b for a, b in zip(dq_pc, dq_c)]
    grad_ref[0, :split] = (lane_pair(dq_p) * HEAD ** (-0.5) + oldp_ref[...]).astype(BF)
    grad_ref[1, :split] = (dk_p + dk_pc).astype(BF)
    grad_ref[2, :split] = (dv_p + dv_pc).astype(BF)
    grad_ref[0, split:] = (lane_pair(both) * HEAD ** (-0.5) + oldc_ref[...]).astype(BF)
    grad_ref[1, split:] = dk_c.astype(BF)
    grad_ref[2, split:] = dv_c.astype(BF)


def pull_near(own_p, own_c, bias, part_p, part_c):
    width = own_p.shape[2]
    rows_p, rows_c = own_p.shape[1], own_c.shape[1]
    specs = [kind_spec(own_p, c) for c in range(3)] + [kind_spec(own_c, c) for c in range(3)]
    specs.append(bias_spec(bias))
    for rows in (rows_p, rows_c):
        specs += [full_spec(rows), full_spec(rows), stat_spec(rows), full_spec(rows)]
    return pl.pallas_call(
        pull_near_kernel,
        grid=(width // LANES,),
        in_specs=specs,
        out_specs=slab_spec(3, rows_p + rows_c),
        out_shape=jax.ShapeDtypeStruct((3, rows_p + rows_c, width), BF),
        compiler_params=params(),
        cost_estimate=cost(5, rows_p * rows_p + rows_c * (rows_p + rows_c), width, 10 * rows_c),
    )(own_p, own_p, own_p, own_c, own_c, own_c, bias, *part_p, *part_c)


def swap(array, axis, bit):
    count = lax.axis_size(axis)
    return lax.ppermute(array, axis, [(j, j ^ (1 << bit)) for j in range(count)])


def own_bit(axis, bit):
    return lax.axis_index(axis) // (1 << bit) % 2


def bits_of(count):
    return count.bit_length() - 1


def halve(part, axis, bit, dim):
    mine = own_bit(axis, bit)
    sent = lax.dynamic_index_in_dim(part, 1 - mine, dim, keepdims=False)
    kept = lax.dynamic_index_in_dim(part, mine, dim, keepdims=False)
    return kept, swap(sent, axis, bit)


def add_low(pair):
    return (pair[0].astype(F32) + pair[1].astype(F32)).astype(BF)


def double(mine, axis, bit, dim):
    other = swap(mine, axis, bit)
    first = own_bit(axis, bit) == 0
    return jnp.concatenate([jnp.where(first, mine, other), jnp.where(first, other, mine)], axis=dim)


def after(value, *earlier):
    return lax.optimization_barrier((value,) + earlier)[0]


def all_after(values, *earlier):
    return list(lax.optimization_barrier(tuple(values) + earlier)[: len(values)])


def tp_sum(low):
    return low.astype(F32) + swap(low, "tp", 0).astype(F32)


def wide_dot(left, right):
    return jnp.dot(left, right, preferred_element_type=F32)


def back_dot(left, right):
    return jnp.einsum("ne,de->nd", left, right, preferred_element_type=F32)


def rows_dot(left, right):
    return jnp.einsum("nd,nf->df", left, right, preferred_element_type=F32)


def cut(slabs):
    seq_bits = bits_of(lax.axis_size("seq"))
    grp_bits = bits_of(lax.axis_size("grp"))
    return slabs.reshape(
        (slabs.shape[0],) + (2,) * (seq_bits + grp_bits) + (-1, slabs.shape[2])
    )


def gather_group(mine):
    for bit in reversed(range(1, bits_of(lax.axis_size("grp")))):
        mine = double(lax.optimization_barrier(mine), "grp", bit, 1)
    return double(lax.optimization_barrier(mine), "grp", 0, 1)


def norm_parts(tokens):
    mean = jnp.mean(tokens, axis=-1, keepdims=True)
    centred = tokens - mean
    variance = jnp.mean(centred * centred, axis=-1, keepdims=True)
    inv = lax.rsqrt(variance + norm_eps)
    return centred * inv, inv


def norm_back(normed, inv, upstream, gain):
    scaled = upstream * gain
    mean = jnp.mean(scaled, axis=-1, keepdims=True)
    inner = jnp.mean(scaled * normed, axis=-1, keepdims=True)
    return inv * (scaled - mean - normed * inner)


def exact_gelu(upper):
    return jax.nn.gelu(upper, approximate=False)


def body(
    prompt_in,
    cont_in,
    prompt_cot,
    cont_cot,
    prompt_len,
    qkv_weight,
    out_weight,
    ffn_in,
    ffn_out,
    norm_gain,
    norm_shift,
):
    rows_p = prompt_in.shape[1]
    half = rows_p // 2
    width = prompt_in.shape[2]
    local_width = qkv_weight.shape[2]
    seq_n = lax.axis_size("seq")
    seq_i = lax.axis_index("seq")
    tp_n = lax.axis_size("tp")
    tp_i = lax.axis_index("tp")
    grp_n = lax.axis_size("grp")
    gains = norm_gain.astype(F32)
    shifts = norm_shift.astype(F32)

    seq_bits = bits_of(seq_n)
    grp_bits = bits_of(grp_n)
    held = lax.dynamic_slice_in_dim(prompt_in[0], tp_i * half, half, 0)
    direct = []
    for at in range(1, seq_n):
        direct.append(lax.ppermute(held, "seq", [(j, j ^ at) for j in range(seq_n)]))
    pieces = direct + [swap(came, "tp", 0) for came in direct]
    starts = [
        (seq_i ^ at) * rows_p + part * half for part in (tp_i, 1 - tp_i) for at in range(1, seq_n)
    ]
    inside = jnp.arange(half, dtype=jnp.int32)
    limit = prompt_len[0, 0]

    def bias_of(place):
        bias = jnp.where(place < limit, 0.0, hidden_value).astype(F32)
        return jnp.broadcast_to(bias[:, None], (place.shape[0], LANES))

    bias_far = bias_of((jnp.stack(starts)[:, None] + inside[None, :]).reshape(-1))
    bias_own = bias_of(seq_i * rows_p + jnp.arange(rows_p, dtype=jnp.int32))

    def project(rows):
        tokens = rows.astype(F32)
        normed, inv = norm_parts(tokens)
        return tokens, normed, inv, (normed * gains[0] + shifts[0]).astype(BF)

    def qkv(low, first):
        return jnp.einsum(
            "nd,cde->cne", low, qkv_weight[first:], preferred_element_type=F32
        ).astype(BF)

    tokens_c, one_c, inv_c, low_c = project(cont_in[0, 0])
    tokens_p, one_p, inv_p, low_p = project(prompt_in[0])
    own_c = qkv(low_c, 0)
    own_p = qkv(low_p, 0)
    part_p, stat_p, part_c, stat_c = attend_near(own_p, own_c, bias_own)
    _, one_f, _, low_f = project(after(jnp.concatenate(pieces, axis=0), part_c))
    far = qkv(low_f, 1)

    att_c, log_c = attend_far(own_c, far, bias_far, part_c, stat_c)
    mixed_c = wide_dot(att_c, out_weight).astype(BF)
    att_p, log_p = attend_far(own_p, far, None, after(part_p, mixed_c), stat_p)
    mixed_p = wide_dot(att_p, out_weight).astype(BF)

    def feed(tokens, mixed, cot):
        resid = tokens + tp_sum(mixed)
        normed, inv = norm_parts(resid)
        low = (normed * gains[1] + shifts[1]).astype(BF)
        upper = wide_dot(low, ffn_in)
        activated, gelu_pull = jax.vjp(exact_gelu, upper)
        act_grad = back_dot(cot, ffn_out)
        upper_grad = gelu_pull(act_grad)[0].astype(BF)
        terms = back_dot(upper_grad, ffn_in).astype(BF)
        return resid, normed, inv, low, activated.astype(BF), upper_grad, terms

    cot_c = cont_cot[0, 0]
    cot_p = prompt_cot[0]
    resid_c, two_c, inv_two_c, mid_c, act_c, up_c, terms_two_c = feed(tokens_c, mixed_c, cot_c)
    resid_p, two_p, inv_two_p, mid_p, act_p, up_p, terms_two_p = feed(
        after(tokens_p, terms_two_c), mixed_p, cot_p
    )
    second_other = swap(terms_two_c, "tp", 0)
    second_other_p = swap(terms_two_p, "tp", 0)

    def joined(first, second):
        return jnp.concatenate([first, second], axis=0)

    up_p = after(up_p, second_other)
    in_grad = rows_dot(joined(mid_p, mid_c), joined(up_p, up_c)).astype(BF)
    down_grad = rows_dot(joined(cot_p, cot_c), joined(act_p, act_c)).astype(BF)
    ffn_grad = cut(jnp.stack([in_grad, down_grad]))
    ffn_part = add_low(halve(ffn_grad, "grp", 0, seq_bits + 1))
    second_other = after(second_other, ffn_part)

    def rest(cot, normed, inv, second):
        grad = cot.astype(F32) + norm_back(normed, inv, second, gains[1])
        low = grad.astype(BF)
        return grad, low, back_dot(low, out_weight).astype(BF)

    second_c = terms_two_c.astype(F32) + second_other.astype(F32)
    grad_c, dm_c, do_c = rest(cot_c, two_c, inv_two_c, second_c)
    for bit in range(1, grp_bits):
        ffn_pair = halve(ffn_part, "grp", bit, seq_bits + 1)
        if bit + 1 < grp_bits:
            ffn_part = add_low(ffn_pair)
    dq_c, partial = pull_far(own_c, far, bias_far, do_c, att_c, log_c, None, rows_p)
    second_p = terms_two_p.astype(F32) + after(second_other_p, dq_c).astype(F32)
    grad_p, dm_p, do_p = rest(cot_p, two_p, inv_two_p, second_p)
    ffn_pair = all_after(ffn_pair, dq_c)
    ffn_part = add_low(ffn_pair)
    do_p = after(do_p, ffn_part)
    for bit in range(seq_bits - 1):
        ffn_pair = halve(ffn_part, "seq", bit, seq_bits - bit)
        if bit + 2 < seq_bits:
            ffn_part = add_low(ffn_pair)
    out_terms_c = wide_dot(after(act_c, dq_c), ffn_out).astype(BF)
    dq_p, dkv_f = pull_far(
        own_p, far, None, after(do_p, out_terms_c), att_p, log_p, partial, rows_p
    )

    def kv_terms(grads, weights):
        return jnp.einsum("cne,cde->nd", grads, weights, preferred_element_type=F32)

    terms_f = kv_terms(dkv_f, qkv_weight[1:])
    gain_f = jnp.sum(terms_f * one_f, axis=0)
    shift_f = jnp.sum(terms_f, axis=0)
    terms_f = lax.optimization_barrier(terms_f.astype(BF))
    away_rows = (seq_n - 1) * half
    swapped = swap(terms_f[away_rows:], "tp", 0)
    ffn_pair = all_after(ffn_pair, dkv_f)
    dq_p = after(dq_p, terms_f, *ffn_pair)
    ffn_part = add_low(ffn_pair)
    ffn_pair = halve(ffn_part, "seq", seq_bits - 1, 1)
    own_grads = pull_near(
        own_p, own_c, bias_own, (do_p, att_p, log_p, dq_p), (do_c, att_c, log_c, dq_c)
    )
    swapped, *ffn_pair, own_grads = all_after([swapped, *ffn_pair, own_grads])
    ffn_mine = add_low(ffn_pair)
    low_pc = joined(low_p, low_c)
    own_wide = jnp.einsum("nd,cne->cde", low_pc, own_grads, preferred_element_type=F32)
    far_wide = jnp.einsum("nd,cne->cde", low_f, dkv_f, preferred_element_type=F32)
    mixing_grad = rows_dot(joined(dm_p, dm_c), joined(att_p, att_c)).astype(BF)
    last_grad = jnp.concatenate(
        [
            own_wide[:1].astype(BF),
            (own_wide[1:] + far_wide).astype(BF),
            mixing_grad[None],
        ]
    )
    last_core = add_low(halve(cut(last_grad), "grp", 0, seq_bits + 1))
    last_part = last_core
    for bit in range(1, grp_bits):
        last_part = add_low(halve(last_part, "grp", bit, seq_bits + 1))

    terms = kv_terms(own_grads, qkv_weight)
    terms_p, terms_c = terms[:rows_p], terms[rows_p:]
    gain_one = gain_f + jnp.sum(terms_c * one_c, axis=0) + jnp.sum(terms_p * one_p, axis=0)
    shift_one = shift_f + jnp.sum(terms, axis=0)
    both = add_low((terms_f[:away_rows], swapped)).reshape(seq_n - 1, half, width)
    blocks = {at: both[at - 1] for at in range(1, seq_n)}
    for bit in range(seq_bits):
        away = [name for name in sorted(blocks) if name >> bit & 1]
        came = swap(jnp.stack([blocks.pop(name) for name in away]), "seq", bit)
        for i, name in enumerate(away):
            near = name ^ (1 << bit)
            blocks[near] = came[i] if near not in blocks else add_low((blocks[near], came[i]))
    halves_p = lax.optimization_barrier(terms_p.astype(BF)).reshape(2, half, width)
    first_p = halve(halves_p, "tp", 0, 0)
    first_p = first_p[0].astype(F32) + first_p[1].astype(F32) + blocks[0].astype(F32)
    first_c = tp_sum(lax.optimization_barrier(terms_c.astype(BF)))
    first_p = double(after(first_p.astype(BF), last_part), "tp", 0, 0).astype(F32)

    two = (terms_two_c.astype(F32), terms_two_p.astype(F32))
    norm_rows = jnp.stack(
        [
            gain_one,
            jnp.sum(two[0] * two_c, axis=0) + jnp.sum(two[1] * two_p, axis=0),
            shift_one,
            jnp.sum(two[0], axis=0) + jnp.sum(two[1], axis=0),
        ]
    )
    def norm_hops(axis):
        total = norm_rows
        for bit in range(bits_of(lax.axis_size(axis))):
            total = lax.optimization_barrier(total)
            total = total + swap(total, axis, bit)
        return total

    norm_rows = norm_hops("tp")
    norm_rows = norm_hops("seq")
    last_part = after(last_part, norm_rows)
    norm_rows = norm_hops("grp")
    columns = width // (seq_n * tp_n)
    norm_sum = lax.dynamic_slice_in_dim(norm_rows, (seq_i * tp_n + tp_i) * columns, columns, 1)

    ffn_sum = gather_group(ffn_mine).astype(F32)
    for bit in range(seq_bits):
        last_part = add_low(halve(last_part, "seq", bit, seq_bits - bit))
    out_terms_p = lax.optimization_barrier(wide_dot(after(act_p, last_core), ffn_out).astype(BF))
    out_other_p = swap(out_terms_p, "tp", 0)
    last_sum = gather_group(after(last_part, norm_rows, out_other_p)).astype(F32)
    cont_out = (resid_c + tp_sum(out_terms_c)).astype(BF)[None, None]
    out_p = out_terms_p.astype(F32) + out_other_p.astype(F32)
    prompt_out = (resid_p + out_p).astype(BF)[None]
    cont_grad = (grad_c + norm_back(one_c, inv_c, first_c, gains[0])).astype(BF)[None, None]
    prompt_grad = (grad_p + norm_back(one_p, inv_p, first_p, gains[0])).astype(BF)[None]
    return (
        prompt_out,
        cont_out,
        prompt_grad,
        cont_grad,
        last_sum[:3],
        last_sum[3].T,
        ffn_sum[0],
        ffn_sum[1].T,
        norm_sum[:2],
        norm_sum[2:],
    )


def solution(mesh):
    placed = (
        P("grp", "seq", None),
        P("grp", "seq", None, None),
        P("grp", "seq", None),
        P("grp", "seq", None, None),
        P("grp", "seq"),
        P(None, None, "tp"),
        P("tp", None),
        P(None, "tp"),
        P("tp", None),
        P(),
        P(),
    )
    return jax.shard_map(
        body,
        mesh=mesh,
        in_specs=placed,
        out_specs=(
            P("grp", "seq", None),
            P("grp", "seq", None, None),
            P("grp", "seq", None),
            P("grp", "seq", None, None),
            P(None, "seq", "tp"),
            P("tp", "seq"),
            P("seq", "tp"),
            P("tp", "seq"),
            P(None, ("seq", "tp")),
            P(None, ("seq", "tp")),
        ),
        check_vma=False,
    )
```

```python
import functools

import jax
import jax.numpy as jnp
from jax import lax
from jax.experimental import pallas as pl
from jax.experimental.pallas import tpu as pltpu
from jax.sharding import PartitionSpec as P

HEAD = 64
CORES = 2
LANES = 128
norm_eps = 1e-05
hidden_value = -1e30
BF = jnp.bfloat16
F32 = jnp.float32
BUDGET = 56 * 1024 * 1024


def nt(left, right):
    return lax.dot_general(left, right, (((1,), (1,)), ((), ())), preferred_element_type=F32)


def tn(left, right):
    return lax.dot_general(left, right, (((0,), (0,)), ((), ())), preferred_element_type=F32)


def nn(left, right):
    return lax.dot_general(left, right, (((1,), (0,)), ((), ())), preferred_element_type=F32)


def one_head(pair, which, factor=None):
    lane = lax.broadcasted_iota(jnp.int32, pair.shape, 1)
    wide = pair.astype(F32)
    if factor is not None:
        wide = wide * factor
    return jnp.where((lane // HEAD) == which, wide, 0.0).astype(BF)


def lane_pair(pair):
    lane = lax.broadcasted_iota(jnp.int32, pair[0].shape, 1)
    return jnp.where(lane < HEAD, pair[0], pair[1])


def row_pair(pair):
    rows = pair[0].shape[1]
    return jnp.transpose(
        jnp.concatenate([jnp.broadcast_to(one, (HEAD, rows)) for one in pair], axis=0)
    )


def masked_scores(keys, mine, bias):
    scores = nt(keys, mine)
    if bias is None:
        return scores
    return scores + jnp.concatenate([bias] * (mine.shape[0] // LANES), axis=1)


def near_kernel(qp_ref, kp_ref, vp_ref, qc_ref, kc_ref, vc_ref, bias_ref, op_ref, sp_ref, oc_ref, sc_ref):
    parts = (
        (qp_ref, op_ref, sp_ref, [(kp_ref, vp_ref, None)]),
        (qc_ref, oc_ref, sc_ref, [(kp_ref, vp_ref, bias_ref), (kc_ref, vc_ref, None)]),
    )
    for q_ref, out_ref, stat_ref, sources in parts:
        outs = []
        for which in range(2):
            mine = one_head(q_ref[0], which, HEAD ** (-0.5))
            scores = [
                masked_scores(k_ref[0], mine, None if b_ref is None else b_ref[...])
                for k_ref, _, b_ref in sources
            ]
            top = functools.reduce(
                jnp.maximum, [jnp.max(s, axis=0, keepdims=True) for s in scores]
            )
            weights = [jnp.exp(s - top) for s in scores]
            stat_ref[0, which : which + 1] = top
            stat_ref[0, 2 + which : 3 + which] = sum(
                jnp.sum(w, axis=0, keepdims=True) for w in weights
            )
            outs.append(sum(tn(w.astype(BF), v_ref[0]) for w, (_, v_ref, _) in zip(weights, sources)))
        out_ref[...] = lane_pair(outs)


def kind_spec(array, kind):
    return pl.BlockSpec((1, array.shape[1], LANES), lambda p: (kind, 0, p))


def full_spec(rows):
    return pl.BlockSpec((rows, LANES), lambda p: (0, p))


def slab_spec(count, rows):
    return pl.BlockSpec((count, rows, LANES), lambda p: (0, 0, p))


def stat_spec(rows):
    return pl.BlockSpec((1, 8, rows), lambda p: (p, 0, 0))


def bias_spec(bias):
    return pl.BlockSpec(bias.shape, lambda p: (0, 0))


def params():
    return pltpu.CompilerParams(vmem_limit_bytes=BUDGET)


def cost(matmuls, pairs, width, moved):
    return pl.CostEstimate(flops=matmuls * pairs, transcendentals=0, bytes_accessed=moved)


def attend_near(own_p, own_c, bias):
    width = own_p.shape[2]
    outs = []
    for own in (own_p, own_c):
        rows = own.shape[1]
        outs += [
            jax.ShapeDtypeStruct((rows, width), F32),
            jax.ShapeDtypeStruct((width // LANES, 8, rows), F32),
        ]
    rows_p, rows_c = own_p.shape[1], own_c.shape[1]
    return pl.pallas_call(
        near_kernel,
        grid=(width // LANES,),
        in_specs=[kind_spec(own_p, c) for c in range(3)]
        + [kind_spec(own_c, c) for c in range(3)]
        + [bias_spec(bias)],
        out_specs=[full_spec(rows_p), stat_spec(rows_p), full_spec(rows_c), stat_spec(rows_c)],
        out_shape=outs,
        compiler_params=params(),
        cost_estimate=cost(2, rows_p * rows_p + rows_c * (rows_p + rows_c), width, 10 * rows_c),
    )(own_p, own_p, own_p, own_c, own_c, own_c, bias)


def far_kernel(*refs, masked):
    if masked:
        q_ref, k_ref, v_ref, bias_ref, part_ref, stat_ref, out_ref, log_ref = refs
    else:
        q_ref, k_ref, v_ref, part_ref, stat_ref, out_ref, log_ref = refs
    outs = []
    olds = []
    news = []
    for which in range(2):
        mine = one_head(q_ref[0], which, HEAD ** (-0.5))
        scores = masked_scores(k_ref[0], mine, bias_ref[...] if masked else None)
        old = stat_ref[0, which : which + 1]
        top = jnp.maximum(old, jnp.max(scores, axis=0, keepdims=True))
        weights = jnp.exp(scores - top)
        shrink = jnp.exp(old - top)
        total = shrink * stat_ref[0, 2 + which : 3 + which] + jnp.sum(
            weights, axis=0, keepdims=True
        )
        outs.append(tn(weights.astype(BF), v_ref[0]))
        olds.append(shrink / total)
        news.append(1.0 / total)
        log_ref[0, which : which + 1] = top + jnp.log(total)
    out = lane_pair(outs) * row_pair(news) + part_ref[...] * row_pair(olds)
    out_ref[...] = out.astype(BF)


def attend_far(own, far, bias, part, stat):
    masked = bias is not None
    rows = own.shape[1]
    width = own.shape[2]
    specs = [kind_spec(own, 0), kind_spec(far, 0), kind_spec(far, 1)]
    args = [own, far, far]
    if masked:
        specs.append(bias_spec(bias))
        args.append(bias)
    return pl.pallas_call(
        functools.partial(far_kernel, masked=masked),
        grid=(width // LANES,),
        in_specs=specs + [full_spec(rows), stat_spec(rows)],
        out_specs=[full_spec(rows), stat_spec(rows)],
        out_shape=[
            jax.ShapeDtypeStruct((rows, width), BF),
            jax.ShapeDtypeStruct((width // LANES, 8, rows), F32),
        ],
        compiler_params=params(),
        cost_estimate=cost(2, rows * far.shape[1], width, 4 * far.shape[1]),
    )(*args, part, stat)


def pull_heads(q_ref, do_ref, out_ref, log_ref):
    upstream = do_ref[...]
    inner = jnp.transpose(upstream.astype(F32) * out_ref[...].astype(F32))
    return [
        (
            one_head(q_ref[0], which, HEAD ** (-0.5)),
            one_head(upstream, which),
            jnp.sum(inner[which * HEAD : (which + 1) * HEAD], axis=0, keepdims=True),
            log_ref[0, which : which + 1],
        )
        for which in range(2)
    ]


def pull_piece(keys, values, bias, heads):
    key_grads = []
    value_grads = []
    query_grads = []
    for mine, grad, delta, log in heads:
        probs = jnp.exp(masked_scores(keys, mine, bias) - log)
        spread = probs * (nt(values, grad) - delta)
        low = spread.astype(BF)
        value_grads.append(nn(probs.astype(BF), grad))
        key_grads.append(nn(low, mine))
        query_grads.append(tn(low, keys))
    return key_grads[0] + key_grads[1], value_grads[0] + value_grads[1], query_grads


def pull_far_kernel(*refs, masked, chunk):
    if masked:
        q_ref, k_ref, v_ref, bias_ref, do_ref, out_ref, log_ref, dq_ref, dkv_ref = refs
    else:
        q_ref, k_ref, v_ref, do_ref, out_ref, log_ref, old_ref, dq_ref, dkv_ref = refs
    heads = pull_heads(q_ref, do_ref, out_ref, log_ref)

    def step(at, acc):
        span = pl.ds(at, chunk)
        bias = bias_ref[span] if masked else None
        dk, dv, more = pull_piece(k_ref[0, span], v_ref[0, span], bias, heads)
        if not masked:
            dk += old_ref[0, span]
            dv += old_ref[1, span]
        dkv_ref[0, span] = dk.astype(dkv_ref.dtype)
        dkv_ref[1, span] = dv.astype(dkv_ref.dtype)
        return more if acc is None else [a + b for a, b in zip(acc, more)]

    acc = step(0, None)
    count = k_ref.shape[1] // chunk
    if count <= 4:
        for i in range(1, count):
            acc = step(i * chunk, acc)
    else:
        acc = lax.fori_loop(
            1, count, lambda i, a: step(pl.multiple_of(i * chunk, chunk), a), acc
        )
    dq_ref[...] = lane_pair(acc) * HEAD ** (-0.5)


def pull_far(own, far, bias, grad, out, log, before, chunk):
    masked = bias is not None
    rows = own.shape[1]
    width = own.shape[2]
    keys = far.shape[1]
    specs = [kind_spec(own, 0), kind_spec(far, 0), kind_spec(far, 1)]
    args = [own, far, far]
    if masked:
        specs.append(bias_spec(bias))
        args.append(bias)
    specs += [full_spec(rows), full_spec(rows), stat_spec(rows)]
    args += [grad, out, log]
    if not masked:
        specs.append(slab_spec(2, keys))
        args.append(before)
    kind = F32 if masked else BF
    return pl.pallas_call(
        functools.partial(pull_far_kernel, masked=masked, chunk=chunk),
        grid=(width // LANES,),
        in_specs=specs,
        out_specs=[full_spec(rows), slab_spec(2, keys)],
        out_shape=[
            jax.ShapeDtypeStruct((rows, width), F32),
            jax.ShapeDtypeStruct((2, keys, width), kind),
        ],
        compiler_params=params(),
        cost_estimate=cost(5, rows * keys, width, 8 * keys),
    )(*args)


def pull_near_kernel(
    qp_ref, kp_ref, vp_ref, qc_ref, kc_ref, vc_ref, bias_ref,
    dop_ref, outp_ref, logp_ref, oldp_ref, doc_ref, outc_ref, logc_ref, oldc_ref,
    grad_ref,
):
    heads_p = pull_heads(qp_ref, dop_ref, outp_ref, logp_ref)
    heads_c = pull_heads(qc_ref, doc_ref, outc_ref, logc_ref)
    dk_p, dv_p, dq_p = pull_piece(kp_ref[0], vp_ref[0], None, heads_p)
    dk_pc, dv_pc, dq_pc = pull_piece(kp_ref[0], vp_ref[0], bias_ref[...], heads_c)
    dk_c, dv_c, dq_c = pull_piece(kc_ref[0], vc_ref[0], None, heads_c)
    split = qp_ref.shape[1]
    both = [a + b for a, b in zip(dq_pc, dq_c)]
    grad_ref[0, :split] = (lane_pair(dq_p) * HEAD ** (-0.5) + oldp_ref[...]).astype(BF)
    grad_ref[1, :split] = (dk_p + dk_pc).astype(BF)
    grad_ref[2, :split] = (dv_p + dv_pc).astype(BF)
    grad_ref[0, split:] = (lane_pair(both) * HEAD ** (-0.5) + oldc_ref[...]).astype(BF)
    grad_ref[1, split:] = dk_c.astype(BF)
    grad_ref[2, split:] = dv_c.astype(BF)


def pull_near(own_p, own_c, bias, part_p, part_c):
    width = own_p.shape[2]
    rows_p, rows_c = own_p.shape[1], own_c.shape[1]
    specs = [kind_spec(own_p, c) for c in range(3)] + [kind_spec(own_c, c) for c in range(3)]
    specs.append(bias_spec(bias))
    for rows in (rows_p, rows_c):
        specs += [full_spec(rows), full_spec(rows), stat_spec(rows), full_spec(rows)]
    return pl.pallas_call(
        pull_near_kernel,
        grid=(width // LANES,),
        in_specs=specs,
        out_specs=slab_spec(3, rows_p + rows_c),
        out_shape=jax.ShapeDtypeStruct((3, rows_p + rows_c, width), BF),
        compiler_params=params(),
        cost_estimate=cost(5, rows_p * rows_p + rows_c * (rows_p + rows_c), width, 10 * rows_c),
    )(own_p, own_p, own_p, own_c, own_c, own_c, bias, *part_p, *part_c)


def swap(array, axis, bit):
    count = lax.axis_size(axis)
    return lax.ppermute(array, axis, [(j, j ^ (1 << bit)) for j in range(count)])


def own_bit(axis, bit):
    return lax.axis_index(axis) // (1 << bit) % 2


def bits_of(count):
    return count.bit_length() - 1


def halve(part, axis, bit, dim):
    mine = own_bit(axis, bit)
    sent = lax.dynamic_index_in_dim(part, 1 - mine, dim, keepdims=False)
    kept = lax.dynamic_index_in_dim(part, mine, dim, keepdims=False)
    return kept, swap(sent, axis, bit)


def add_low(pair):
    return (pair[0].astype(F32) + pair[1].astype(F32)).astype(BF)


def double(mine, axis, bit, dim):
    other = swap(mine, axis, bit)
    first = own_bit(axis, bit) == 0
    return jnp.concatenate([jnp.where(first, mine, other), jnp.where(first, other, mine)], axis=dim)


def after(value, *earlier):
    return lax.optimization_barrier((value,) + earlier)[0]


def all_after(values, *earlier):
    return list(lax.optimization_barrier(tuple(values) + earlier)[: len(values)])


def tp_sum(low):
    return low.astype(F32) + swap(low, "tp", 0).astype(F32)


def wide_dot(left, right):
    return jnp.dot(left, right, preferred_element_type=F32)


def back_dot(left, right):
    return jnp.einsum("ne,de->nd", left, right, preferred_element_type=F32)


def rows_dot(left, right):
    return jnp.einsum("nd,nf->df", left, right, preferred_element_type=F32)


def cut(slabs):
    seq_bits = bits_of(lax.axis_size("seq"))
    grp_bits = bits_of(lax.axis_size("grp"))
    return slabs.reshape(
        (slabs.shape[0],) + (2,) * (seq_bits + grp_bits) + (-1, slabs.shape[2])
    )


def gather_group(mine):
    for bit in reversed(range(1, bits_of(lax.axis_size("grp")))):
        mine = double(lax.optimization_barrier(mine), "grp", bit, 1)
    return double(lax.optimization_barrier(mine), "grp", 0, 1)


def gather_last(mine, slab_rows, slabs, hold):
    grp_n = lax.axis_size("grp")
    mine = lax.optimization_barrier(mine)

    def slabs_of(rows):
        return rows[:slab_rows].reshape(slabs, -1, rows.shape[1])

    if grp_n != 2 * CORES:
        total = mine[slab_rows:].astype(F32)
        for bit in range(bits_of(grp_n)):
            total = total + swap(total, "grp", bit)
        return gather_group(slabs_of(mine)).astype(F32), total
    came = [mine] + [
        lax.ppermute(mine, "grp", [(j, j ^ at) for j in range(grp_n)]) for at in range(1, grp_n)
    ]
    came = all_after(came, *hold)
    total = sum(rows[slab_rows:].astype(F32) for rows in came)
    came = [slabs_of(rows) for rows in came]
    swapped_core = lax.axis_index("grp") % CORES == 1
    swapped_chip = lax.axis_index("grp") // CORES == 1
    came = [jnp.where(swapped_core, came[at ^ 1], came[at]) for at in range(grp_n)]
    came = [jnp.where(swapped_chip, came[at ^ 2], came[at]) for at in range(grp_n)]
    return jnp.concatenate([came[0], came[2], came[1], came[3]], axis=1).astype(F32), total


def norm_parts(tokens):
    mean = jnp.mean(tokens, axis=-1, keepdims=True)
    centred = tokens - mean
    variance = jnp.mean(centred * centred, axis=-1, keepdims=True)
    inv = lax.rsqrt(variance + norm_eps)
    return centred * inv, inv


def norm_back(normed, inv, upstream, gain):
    scaled = upstream * gain
    mean = jnp.mean(scaled, axis=-1, keepdims=True)
    inner = jnp.mean(scaled * normed, axis=-1, keepdims=True)
    return inv * (scaled - mean - normed * inner)


def exact_gelu(upper):
    return jax.nn.gelu(upper, approximate=False)


def body(
    prompt_in,
    cont_in,
    prompt_cot,
    cont_cot,
    prompt_len,
    qkv_weight,
    out_weight,
    ffn_in,
    ffn_out,
    norm_gain,
    norm_shift,
):
    rows_p = prompt_in.shape[1]
    rows_c = cont_in.shape[2]
    half = rows_p // 2
    width = prompt_in.shape[2]
    local_width = qkv_weight.shape[2]
    seq_n = lax.axis_size("seq")
    seq_i = lax.axis_index("seq")
    tp_n = lax.axis_size("tp")
    tp_i = lax.axis_index("tp")
    grp_n = lax.axis_size("grp")
    gains = norm_gain.astype(F32)
    shifts = norm_shift.astype(F32)

    seq_bits = bits_of(seq_n)
    grp_bits = bits_of(grp_n)
    held = lax.dynamic_slice_in_dim(prompt_in[0], tp_i * half, half, 0)
    direct = []
    for at in range(1, seq_n):
        direct.append(lax.ppermute(held, "seq", [(j, j ^ at) for j in range(seq_n)]))
    pieces = direct + [swap(came, "tp", 0) for came in direct]
    starts = [
        (seq_i ^ at) * rows_p + part * half for part in (tp_i, 1 - tp_i) for at in range(1, seq_n)
    ]
    inside = jnp.arange(half, dtype=jnp.int32)
    limit = prompt_len[0, 0]

    def bias_of(place):
        bias = jnp.where(place < limit, 0.0, hidden_value).astype(F32)
        return jnp.broadcast_to(bias[:, None], (place.shape[0], LANES))

    bias_far = bias_of((jnp.stack(starts)[:, None] + inside[None, :]).reshape(-1))
    bias_own = bias_of(seq_i * rows_p + jnp.arange(rows_p, dtype=jnp.int32))

    def project(rows):
        tokens = rows.astype(F32)
        normed, inv = norm_parts(tokens)
        return tokens, normed, inv, (normed * gains[0] + shifts[0]).astype(BF)

    def qkv(low, first):
        return jnp.einsum(
            "nd,cde->cne", low, qkv_weight[first:], preferred_element_type=F32
        ).astype(BF)

    tokens_c, one_c, inv_c, low_c = project(cont_in[0, 0])
    tokens_p, one_p, inv_p, low_p = project(prompt_in[0])
    own_c = qkv(low_c, 0)
    own_p = qkv(low_p, 0)
    part_p, stat_p, part_c, stat_c = attend_near(own_p, own_c, bias_own)
    _, one_f, _, low_f = project(after(jnp.concatenate(pieces, axis=0), part_c))
    far = qkv(low_f, 1)

    att_c, log_c = attend_far(own_c, far, bias_far, part_c, stat_c)
    mixed_c = wide_dot(att_c, out_weight).astype(BF)
    att_p, log_p = attend_far(own_p, far, None, after(part_p, mixed_c), stat_p)
    mixed_p = wide_dot(att_p, out_weight).astype(BF)

    def feed(tokens, mixed, cot):
        resid = tokens + tp_sum(mixed)
        normed, inv = norm_parts(resid)
        low = (normed * gains[1] + shifts[1]).astype(BF)
        upper = wide_dot(low, ffn_in)
        activated, gelu_pull = jax.vjp(exact_gelu, upper)
        act_grad = back_dot(cot, ffn_out)
        upper_grad = gelu_pull(act_grad)[0].astype(BF)
        terms = back_dot(upper_grad, ffn_in).astype(BF)
        return resid, normed, inv, low, activated.astype(BF), upper_grad, terms

    cot_c = cont_cot[0, 0]
    cot_p = prompt_cot[0]
    resid_c, two_c, inv_two_c, mid_c, act_c, up_c, terms_two_c = feed(tokens_c, mixed_c, cot_c)
    resid_p, two_p, inv_two_p, mid_p, act_p, up_p, terms_two_p = feed(
        after(tokens_p, terms_two_c), mixed_p, cot_p
    )
    second_other = swap(terms_two_c, "tp", 0)
    second_other_p = swap(terms_two_p, "tp", 0)

    def joined(first, second):
        return jnp.concatenate([first, second], axis=0)

    up_p = after(up_p, second_other)
    in_grad = rows_dot(joined(mid_p, mid_c), joined(up_p, up_c)).astype(BF)
    down_grad = rows_dot(joined(cot_p, cot_c), joined(act_p, act_c)).astype(BF)
    ffn_grad = cut(jnp.stack([in_grad, down_grad]))
    ffn_part = add_low(halve(ffn_grad, "grp", 0, seq_bits + 1))
    second_other = after(second_other, ffn_part)

    def rest(cot, normed, inv, second):
        grad = cot.astype(F32) + norm_back(normed, inv, second, gains[1])
        low = grad.astype(BF)
        return grad, low, back_dot(low, out_weight).astype(BF)

    second_c = terms_two_c.astype(F32) + second_other.astype(F32)
    grad_c, dm_c, do_c = rest(cot_c, two_c, inv_two_c, second_c)
    for bit in range(1, grp_bits):
        ffn_pair = halve(ffn_part, "grp", bit, seq_bits + 1)
        if bit + 1 < grp_bits:
            ffn_part = add_low(ffn_pair)
    dq_c, partial = pull_far(own_c, far, bias_far, do_c, att_c, log_c, None, rows_p)
    ffn_pair = all_after(ffn_pair, dq_c)
    ffn_part = add_low(ffn_pair)
    second_other_p = after(second_other_p, ffn_part)
    second_p = terms_two_p.astype(F32) + second_other_p.astype(F32)
    grad_p, dm_p, do_p = rest(cot_p, two_p, inv_two_p, second_p)
    for bit in range(seq_bits - 1):
        ffn_pair = halve(ffn_part, "seq", bit, seq_bits - bit)
        if bit + 2 < seq_bits:
            ffn_part = add_low(ffn_pair)
    out_terms_c = wide_dot(after(act_c, dq_c), ffn_out).astype(BF)
    out_other_c = swap(out_terms_c, "tp", 0)
    dq_p, dkv_f = pull_far(
        own_p, far, None, after(do_p, out_terms_c), att_p, log_p, partial, rows_p
    )

    def kv_terms(grads, weights):
        return jnp.einsum("cne,cde->nd", grads, weights, preferred_element_type=F32)

    terms_f = kv_terms(dkv_f, qkv_weight[1:])
    gain_f = jnp.sum(terms_f * one_f, axis=0)
    shift_f = jnp.sum(terms_f, axis=0)
    terms_f = lax.optimization_barrier(terms_f.astype(BF))
    away_rows = (seq_n - 1) * half
    swapped = swap(terms_f[away_rows:], "tp", 0)
    ffn_pair = all_after(ffn_pair, dkv_f)
    out_other_c = after(out_other_c, dkv_f)
    dq_p = after(dq_p, terms_f, out_other_c, *ffn_pair)
    ffn_part = add_low(ffn_pair)
    ffn_pair = halve(ffn_part, "seq", seq_bits - 1, 1)
    own_grads = pull_near(
        own_p, own_c, bias_own, (do_p, att_p, log_p, dq_p), (do_c, att_c, log_c, dq_c)
    )
    swapped, *ffn_pair, own_grads = all_after([swapped, *ffn_pair, own_grads])
    ffn_mine = lax.optimization_barrier(add_low(ffn_pair))
    for bit in reversed(range(1, grp_bits)):
        ffn_mine = lax.optimization_barrier(double(ffn_mine, "grp", bit, 1))
    low_pc = joined(low_p, low_c)
    last_grads = [rows_dot(low_pc, own_grads[0])]
    for c in range(2):
        last_grads.append(rows_dot(low_pc, own_grads[1 + c]) + rows_dot(low_f, dkv_f[c]))
    mixing_grad = rows_dot(joined(dm_p, dm_c), joined(att_p, att_c))
    last_cut = [cut(grad.astype(BF)[None]) for grad in last_grads + [mixing_grad]]
    core_i = own_bit("grp", 0)

    def core_half(which):
        return jnp.concatenate(
            [lax.dynamic_index_in_dim(g, which, seq_bits + 1, keepdims=False) for g in last_cut]
        )

    sent = lax.optimization_barrier(core_half(1 - core_i))
    last_core = add_low((core_half(core_i), swap(sent, "grp", 0)))
    ffn_mine = after(ffn_mine, sent)
    ffn_other = swap(ffn_mine, "grp", 0)
    out_other_c = after(out_other_c, last_core)
    out_c = out_terms_c.astype(F32) + out_other_c.astype(F32)
    cont_out = (resid_c + out_c).astype(BF)[None, None]
    last_part = last_core
    for bit in range(1, grp_bits):
        last_pair = halve(last_part, "grp", bit, seq_bits + 1)
        if bit + 1 < grp_bits:
            last_part = add_low(last_pair)

    terms = kv_terms(after(own_grads, sent), qkv_weight)
    terms_p, terms_c = terms[:rows_p], terms[rows_p:]
    gain_one = gain_f + jnp.sum(terms * joined(one_p, one_c), axis=0)
    shift_one = shift_f + jnp.sum(terms, axis=0)
    both = add_low((terms_f[:away_rows], swapped)).reshape(seq_n - 1, half, width)
    blocks = {at: both[at - 1] for at in range(1, seq_n)}
    for bit in range(seq_bits):
        away = [name for name in sorted(blocks) if name >> bit & 1]
        came = swap(jnp.stack([blocks.pop(name) for name in away]), "seq", bit)
        if bit == 0:
            came = after(came, last_core)
        for i, name in enumerate(away):
            near = name ^ (1 << bit)
            blocks[near] = came[i] if near not in blocks else add_low((blocks[near], came[i]))
    halves_p = lax.optimization_barrier(terms_p.astype(BF)).reshape(2, half, width)
    mine_p, other_p = halve(halves_p, "tp", 0, 0)
    two = (terms_two_c.astype(F32), terms_two_p.astype(F32))
    norm_rows = jnp.stack(
        [
            gain_one,
            jnp.sum(two[0] * two_c, axis=0) + jnp.sum(two[1] * two_p, axis=0),
            shift_one,
            jnp.sum(two[0], axis=0) + jnp.sum(two[1], axis=0),
        ]
    )
    low_norm = jnp.pad(norm_rows.astype(BF), ((0, 12), (0, 0)))
    low_terms_c = lax.optimization_barrier(joined(terms_c.astype(BF), low_norm))
    other_c = swap(low_terms_c, "tp", 0)

    last_pair = all_after(last_pair, cont_out)
    last_part = add_low(last_pair)
    late = [other_p, other_c, blocks[0], ffn_mine, ffn_other]
    other_p, other_c, home, ffn_mine, ffn_other = all_after(late, last_part)
    first = core_i == 0
    ffn_sum = jnp.concatenate(
        [jnp.where(first, ffn_mine, ffn_other), jnp.where(first, ffn_other, ffn_mine)], axis=1
    ).astype(F32)
    ffn_sums = lax.optimization_barrier((ffn_sum[0], ffn_sum[1].T))
    norm_rows = norm_rows + other_c[rows_c : rows_c + 4].astype(F32)
    norm_cut = norm_rows.reshape(4, seq_n, tp_n, -1)
    norm_cut = lax.dynamic_index_in_dim(norm_cut, tp_i, 2, keepdims=False)
    columns = norm_cut.shape[2]
    norm_cut = norm_cut.transpose(1, 0, 2).reshape(seq_n, -1)
    norm_pad = jnp.pad(norm_cut, ((0, 0), (0, 16 * local_width - norm_cut.shape[1])))
    norm_pad = norm_pad.astype(BF).reshape(seq_n, 16, local_width)
    slab_rows = last_part.shape[0] * last_part.shape[-2]
    last_part = last_part.reshape(last_part.shape[0], seq_n, -1, local_width)

    def block(at):
        slabs = lax.dynamic_index_in_dim(last_part, at, 1, keepdims=False)
        norms = lax.dynamic_index_in_dim(norm_pad, at, 0, keepdims=False)
        return jnp.concatenate([slabs.reshape(slab_rows, local_width), norms])

    last_pieces = [block(seq_i)] + [
        lax.ppermute(block(seq_i ^ at), "seq", [(j, j ^ at) for j in range(seq_n)])
        for at in range(1, seq_n)
    ]

    first_p = mine_p.astype(F32) + other_p.astype(F32) + home.astype(F32)
    first_p = lax.optimization_barrier(first_p.astype(BF))
    gathered_p = swap(first_p, "tp", 0)
    first_c = low_terms_c[:rows_c].astype(F32) + other_c[:rows_c].astype(F32)
    out_terms_p = lax.optimization_barrier(wide_dot(after(act_p, first_p), ffn_out).astype(BF))
    out_other_p = swap(out_terms_p, "tp", 0)

    last_pieces = all_after(last_pieces, *ffn_sums)
    last_mine = sum(piece.astype(F32) for piece in last_pieces).astype(BF)
    gathered_p, out_other_p = all_after([gathered_p, out_other_p], last_mine)
    first = tp_i == 0
    first_p = jnp.concatenate(
        [jnp.where(first, first_p, gathered_p), jnp.where(first, gathered_p, first_p)]
    ).astype(F32)
    out_p = out_terms_p.astype(F32) + out_other_p.astype(F32)
    prompt_out = (resid_p + out_p).astype(BF)[None]
    cont_grad = (grad_c + norm_back(one_c, inv_c, first_c, gains[0])).astype(BF)[None, None]
    prompt_grad = (grad_p + norm_back(one_p, inv_p, first_p, gains[0])).astype(BF)[None]
    last_sum, norm_sum = gather_last(last_mine, slab_rows, last_part.shape[0], (prompt_grad, cont_grad))
    norm_sum = norm_sum.reshape(-1)[: 4 * columns].reshape(4, columns)
    return (
        prompt_out,
        cont_out,
        prompt_grad,
        cont_grad,
        last_sum[:3],
        last_sum[3].T,
        *ffn_sums,
        norm_sum[:2],
        norm_sum[2:],
    )


def solution(mesh):
    placed = (
        P("grp", "seq", None),
        P("grp", "seq", None, None),
        P("grp", "seq", None),
        P("grp", "seq", None, None),
        P("grp", "seq"),
        P(None, None, "tp"),
        P("tp", None),
        P(None, "tp"),
        P("tp", None),
        P(),
        P(),
    )
    return jax.shard_map(
        body,
        mesh=mesh,
        in_specs=placed,
        out_specs=(
            P("grp", "seq", None),
            P("grp", "seq", None, None),
            P("grp", "seq", None),
            P("grp", "seq", None, None),
            P(None, "seq", "tp"),
            P("tp", "seq"),
            P("seq", "tp"),
            P("tp", "seq"),
            P(None, ("seq", "tp")),
            P(None, ("seq", "tp")),
        ),
        check_vma=False,
    )
```

```python
import functools

import jax
import jax.numpy as jnp
from jax import lax
from jax.experimental import pallas as pl
from jax.experimental.pallas import tpu as pltpu
from jax.sharding import PartitionSpec as P

HEAD = 64
CORES = 2
LANES = 128
norm_eps = 1e-05
hidden_value = -1e30
BF = jnp.bfloat16
F32 = jnp.float32
BUDGET = 56 * 1024 * 1024


def nt(left, right):
    return lax.dot_general(left, right, (((1,), (1,)), ((), ())), preferred_element_type=F32)


def tn(left, right):
    return lax.dot_general(left, right, (((0,), (0,)), ((), ())), preferred_element_type=F32)


def nn(left, right):
    return lax.dot_general(left, right, (((1,), (0,)), ((), ())), preferred_element_type=F32)


def one_head(pair, which, factor=None):
    lane = lax.broadcasted_iota(jnp.int32, pair.shape, 1)
    wide = pair.astype(F32)
    if factor is not None:
        wide = wide * factor
    return jnp.where((lane // HEAD) == which, wide, 0.0).astype(BF)


def lane_pair(pair):
    lane = lax.broadcasted_iota(jnp.int32, pair[0].shape, 1)
    return jnp.where(lane < HEAD, pair[0], pair[1])


def row_pair(pair):
    rows = pair[0].shape[1]
    return jnp.transpose(
        jnp.concatenate([jnp.broadcast_to(one, (HEAD, rows)) for one in pair], axis=0)
    )


def masked_scores(keys, mine, bias):
    scores = nt(keys, mine)
    if bias is None:
        return scores
    return scores + jnp.concatenate([bias] * (mine.shape[0] // LANES), axis=1)


def near_kernel(qp_ref, kp_ref, vp_ref, qc_ref, kc_ref, vc_ref, bias_ref, op_ref, sp_ref, oc_ref, sc_ref):
    parts = (
        (qp_ref, op_ref, sp_ref, [(kp_ref, vp_ref, None)]),
        (qc_ref, oc_ref, sc_ref, [(kp_ref, vp_ref, bias_ref), (kc_ref, vc_ref, None)]),
    )
    for q_ref, out_ref, stat_ref, sources in parts:
        outs = []
        for which in range(2):
            mine = one_head(q_ref[0], which, HEAD ** (-0.5))
            scores = [
                masked_scores(k_ref[0], mine, None if b_ref is None else b_ref[...])
                for k_ref, _, b_ref in sources
            ]
            top = functools.reduce(
                jnp.maximum, [jnp.max(s, axis=0, keepdims=True) for s in scores]
            )
            weights = [jnp.exp(s - top) for s in scores]
            stat_ref[0, which : which + 1] = top
            stat_ref[0, 2 + which : 3 + which] = sum(
                jnp.sum(w, axis=0, keepdims=True) for w in weights
            )
            outs.append(sum(tn(w.astype(BF), v_ref[0]) for w, (_, v_ref, _) in zip(weights, sources)))
        out_ref[...] = lane_pair(outs)


def kind_spec(array, kind):
    return pl.BlockSpec((1, array.shape[1], LANES), lambda p: (kind, 0, p))


def full_spec(rows):
    return pl.BlockSpec((rows, LANES), lambda p: (0, p))


def slab_spec(count, rows):
    return pl.BlockSpec((count, rows, LANES), lambda p: (0, 0, p))


def stat_spec(rows):
    return pl.BlockSpec((1, 8, rows), lambda p: (p, 0, 0))


def bias_spec(bias):
    return pl.BlockSpec(bias.shape, lambda p: (0, 0))


def params():
    return pltpu.CompilerParams(vmem_limit_bytes=BUDGET)


def cost(matmuls, pairs, width, moved):
    return pl.CostEstimate(flops=matmuls * pairs, transcendentals=0, bytes_accessed=moved)


def attend_near(own_p, own_c, bias):
    width = own_p.shape[2]
    outs = []
    for own in (own_p, own_c):
        rows = own.shape[1]
        outs += [
            jax.ShapeDtypeStruct((rows, width), F32),
            jax.ShapeDtypeStruct((width // LANES, 8, rows), F32),
        ]
    rows_p, rows_c = own_p.shape[1], own_c.shape[1]
    return pl.pallas_call(
        near_kernel,
        grid=(width // LANES,),
        in_specs=[kind_spec(own_p, c) for c in range(3)]
        + [kind_spec(own_c, c) for c in range(3)]
        + [bias_spec(bias)],
        out_specs=[full_spec(rows_p), stat_spec(rows_p), full_spec(rows_c), stat_spec(rows_c)],
        out_shape=outs,
        compiler_params=params(),
        cost_estimate=cost(2, rows_p * rows_p + rows_c * (rows_p + rows_c), width, 10 * rows_c),
    )(own_p, own_p, own_p, own_c, own_c, own_c, bias)


def middle_kernel(
    k_ref, v_ref, bias_ref, qp_ref, partp_ref, statp_ref, qc_ref, partc_ref, statc_ref,
    outp_ref, newp_ref, outc_ref, newc_ref,
):
    parts = (
        (qp_ref, None, partp_ref, statp_ref, outp_ref, newp_ref),
        (qc_ref, bias_ref, partc_ref, statc_ref, outc_ref, newc_ref),
    )
    for q_ref, b_ref, part_ref, stat_ref, out_ref, new_ref in parts:
        outs = []
        shrinks = []
        for which in range(2):
            mine = one_head(q_ref[0], which, HEAD ** (-0.5))
            scores = masked_scores(k_ref[0], mine, None if b_ref is None else b_ref[...])
            old = stat_ref[0, which : which + 1]
            top = jnp.maximum(old, jnp.max(scores, axis=0, keepdims=True))
            weights = jnp.exp(scores - top)
            shrink = jnp.exp(old - top)
            new_ref[0, which : which + 1] = top
            new_ref[0, 2 + which : 3 + which] = shrink * stat_ref[
                0, 2 + which : 3 + which
            ] + jnp.sum(weights, axis=0, keepdims=True)
            outs.append(tn(weights.astype(BF), v_ref[0]))
            shrinks.append(shrink)
        out_ref[...] = lane_pair(outs) + part_ref[...] * row_pair(shrinks)


def attend_middle(own_p, own_c, far, bias, part_p, stat_p, part_c, stat_c):
    width = own_p.shape[2]
    specs = [kind_spec(far, 0), kind_spec(far, 1), bias_spec(bias)]
    out_specs = []
    outs = []
    for own in (own_p, own_c):
        rows = own.shape[1]
        specs += [kind_spec(own, 0), full_spec(rows), stat_spec(rows)]
        out_specs += [full_spec(rows), stat_spec(rows)]
        outs += [
            jax.ShapeDtypeStruct((rows, width), F32),
            jax.ShapeDtypeStruct((width // LANES, 8, rows), F32),
        ]
    rows = own_p.shape[1] + own_c.shape[1]
    return pl.pallas_call(
        middle_kernel,
        grid=(width // LANES,),
        in_specs=specs,
        out_specs=out_specs,
        out_shape=outs,
        compiler_params=params(),
        cost_estimate=cost(2, rows * far.shape[1], width, 4 * far.shape[1]),
    )(far, far, bias, own_p, part_p, stat_p, own_c, part_c, stat_c)


def far_kernel(*refs, masked):
    if masked:
        q_ref, k_ref, v_ref, bias_ref, part_ref, stat_ref, out_ref, log_ref = refs
    else:
        q_ref, k_ref, v_ref, part_ref, stat_ref, out_ref, log_ref = refs
    outs = []
    olds = []
    news = []
    for which in range(2):
        mine = one_head(q_ref[0], which, HEAD ** (-0.5))
        scores = masked_scores(k_ref[0], mine, bias_ref[...] if masked else None)
        old = stat_ref[0, which : which + 1]
        top = jnp.maximum(old, jnp.max(scores, axis=0, keepdims=True))
        weights = jnp.exp(scores - top)
        shrink = jnp.exp(old - top)
        total = shrink * stat_ref[0, 2 + which : 3 + which] + jnp.sum(
            weights, axis=0, keepdims=True
        )
        outs.append(tn(weights.astype(BF), v_ref[0]))
        olds.append(shrink / total)
        news.append(1.0 / total)
        log_ref[0, which : which + 1] = top + jnp.log(total)
    out = lane_pair(outs) * row_pair(news) + part_ref[...] * row_pair(olds)
    out_ref[...] = out.astype(BF)


def attend_far(own, far, bias, part, stat):
    masked = bias is not None
    rows = own.shape[1]
    width = own.shape[2]
    specs = [kind_spec(own, 0), kind_spec(far, 0), kind_spec(far, 1)]
    args = [own, far, far]
    if masked:
        specs.append(bias_spec(bias))
        args.append(bias)
    return pl.pallas_call(
        functools.partial(far_kernel, masked=masked),
        grid=(width // LANES,),
        in_specs=specs + [full_spec(rows), stat_spec(rows)],
        out_specs=[full_spec(rows), stat_spec(rows)],
        out_shape=[
            jax.ShapeDtypeStruct((rows, width), BF),
            jax.ShapeDtypeStruct((width // LANES, 8, rows), F32),
        ],
        compiler_params=params(),
        cost_estimate=cost(2, rows * far.shape[1], width, 4 * far.shape[1]),
    )(*args, part, stat)


def pull_heads(q_ref, do_ref, out_ref, log_ref):
    upstream = do_ref[...]
    inner = jnp.transpose(upstream.astype(F32) * out_ref[...].astype(F32))
    return [
        (
            one_head(q_ref[0], which, HEAD ** (-0.5)),
            one_head(upstream, which),
            jnp.sum(inner[which * HEAD : (which + 1) * HEAD], axis=0, keepdims=True),
            log_ref[0, which : which + 1],
        )
        for which in range(2)
    ]


def pull_piece(keys, values, bias, heads):
    key_grads = []
    value_grads = []
    query_grads = []
    for mine, grad, delta, log in heads:
        probs = jnp.exp(masked_scores(keys, mine, bias) - log)
        spread = probs * (nt(values, grad) - delta)
        low = spread.astype(BF)
        value_grads.append(nn(probs.astype(BF), grad))
        key_grads.append(nn(low, mine))
        query_grads.append(tn(low, keys))
    return key_grads[0] + key_grads[1], value_grads[0] + value_grads[1], query_grads


def pull_far_kernel(*refs, masked, chunk):
    if masked:
        q_ref, k_ref, v_ref, bias_ref, do_ref, out_ref, log_ref, dq_ref, dkv_ref = refs
    else:
        q_ref, k_ref, v_ref, do_ref, out_ref, log_ref, old_ref, dq_ref, dkv_ref = refs
    heads = pull_heads(q_ref, do_ref, out_ref, log_ref)

    def step(at, acc):
        span = pl.ds(at, chunk)
        bias = bias_ref[span] if masked else None
        dk, dv, more = pull_piece(k_ref[0, span], v_ref[0, span], bias, heads)
        if not masked:
            dk += old_ref[0, span]
            dv += old_ref[1, span]
        dkv_ref[0, span] = dk.astype(dkv_ref.dtype)
        dkv_ref[1, span] = dv.astype(dkv_ref.dtype)
        return more if acc is None else [a + b for a, b in zip(acc, more)]

    acc = step(0, None)
    count = k_ref.shape[1] // chunk
    if count <= 4:
        for i in range(1, count):
            acc = step(i * chunk, acc)
    else:
        acc = lax.fori_loop(
            1, count, lambda i, a: step(pl.multiple_of(i * chunk, chunk), a), acc
        )
    dq_ref[...] = lane_pair(acc) * HEAD ** (-0.5)


def pull_far(own, far, bias, grad, out, log, before, chunk):
    masked = bias is not None
    rows = own.shape[1]
    width = own.shape[2]
    keys = far.shape[1]
    specs = [kind_spec(own, 0), kind_spec(far, 0), kind_spec(far, 1)]
    args = [own, far, far]
    if masked:
        specs.append(bias_spec(bias))
        args.append(bias)
    specs += [full_spec(rows), full_spec(rows), stat_spec(rows)]
    args += [grad, out, log]
    if not masked:
        specs.append(slab_spec(2, keys))
        args.append(before)
    kind = F32 if masked else BF
    return pl.pallas_call(
        functools.partial(pull_far_kernel, masked=masked, chunk=chunk),
        grid=(width // LANES,),
        in_specs=specs,
        out_specs=[full_spec(rows), slab_spec(2, keys)],
        out_shape=[
            jax.ShapeDtypeStruct((rows, width), F32),
            jax.ShapeDtypeStruct((2, keys, width), kind),
        ],
        compiler_params=params(),
        cost_estimate=cost(5, rows * keys, width, 8 * keys),
    )(*args)


def pull_near_kernel(
    qp_ref, kp_ref, vp_ref, qc_ref, kc_ref, vc_ref, bias_ref,
    dop_ref, outp_ref, logp_ref, oldp_ref, doc_ref, outc_ref, logc_ref, oldc_ref,
    grad_ref,
):
    heads_p = pull_heads(qp_ref, dop_ref, outp_ref, logp_ref)
    heads_c = pull_heads(qc_ref, doc_ref, outc_ref, logc_ref)
    dk_p, dv_p, dq_p = pull_piece(kp_ref[0], vp_ref[0], None, heads_p)
    dk_pc, dv_pc, dq_pc = pull_piece(kp_ref[0], vp_ref[0], bias_ref[...], heads_c)
    dk_c, dv_c, dq_c = pull_piece(kc_ref[0], vc_ref[0], None, heads_c)
    split = qp_ref.shape[1]
    both = [a + b for a, b in zip(dq_pc, dq_c)]
    grad_ref[0, :split] = (lane_pair(dq_p) * HEAD ** (-0.5) + oldp_ref[...]).astype(BF)
    grad_ref[1, :split] = (dk_p + dk_pc).astype(BF)
    grad_ref[2, :split] = (dv_p + dv_pc).astype(BF)
    grad_ref[0, split:] = (lane_pair(both) * HEAD ** (-0.5) + oldc_ref[...]).astype(BF)
    grad_ref[1, split:] = dk_c.astype(BF)
    grad_ref[2, split:] = dv_c.astype(BF)


def pull_near(own_p, own_c, bias, part_p, part_c):
    width = own_p.shape[2]
    rows_p, rows_c = own_p.shape[1], own_c.shape[1]
    specs = [kind_spec(own_p, c) for c in range(3)] + [kind_spec(own_c, c) for c in range(3)]
    specs.append(bias_spec(bias))
    for rows in (rows_p, rows_c):
        specs += [full_spec(rows), full_spec(rows), stat_spec(rows), full_spec(rows)]
    return pl.pallas_call(
        pull_near_kernel,
        grid=(width // LANES,),
        in_specs=specs,
        out_specs=slab_spec(3, rows_p + rows_c),
        out_shape=jax.ShapeDtypeStruct((3, rows_p + rows_c, width), BF),
        compiler_params=params(),
        cost_estimate=cost(5, rows_p * rows_p + rows_c * (rows_p + rows_c), width, 10 * rows_c),
    )(own_p, own_p, own_p, own_c, own_c, own_c, bias, *part_p, *part_c)


def swap(array, axis, bit):
    count = lax.axis_size(axis)
    return lax.ppermute(array, axis, [(j, j ^ (1 << bit)) for j in range(count)])


def own_bit(axis, bit):
    return lax.axis_index(axis) // (1 << bit) % 2


def bits_of(count):
    return count.bit_length() - 1


def halve(part, axis, bit, dim):
    mine = own_bit(axis, bit)
    sent = lax.dynamic_index_in_dim(part, 1 - mine, dim, keepdims=False)
    kept = lax.dynamic_index_in_dim(part, mine, dim, keepdims=False)
    return kept, swap(sent, axis, bit)


def add_low(pair):
    return (pair[0].astype(F32) + pair[1].astype(F32)).astype(BF)


def double(mine, axis, bit, dim):
    other = swap(mine, axis, bit)
    first = own_bit(axis, bit) == 0
    return jnp.concatenate([jnp.where(first, mine, other), jnp.where(first, other, mine)], axis=dim)


def after(value, *earlier):
    return lax.optimization_barrier((value,) + earlier)[0]


def all_after(values, *earlier):
    return list(lax.optimization_barrier(tuple(values) + earlier)[: len(values)])


def tp_sum(low):
    return low.astype(F32) + swap(low, "tp", 0).astype(F32)


def wide_dot(left, right):
    return jnp.dot(left, right, preferred_element_type=F32)


def back_dot(left, right):
    return jnp.einsum("ne,de->nd", left, right, preferred_element_type=F32)


def rows_dot(left, right):
    return jnp.einsum("nd,nf->df", left, right, preferred_element_type=F32)


def cut(slabs):
    seq_bits = bits_of(lax.axis_size("seq"))
    grp_bits = bits_of(lax.axis_size("grp"))
    return slabs.reshape(
        (slabs.shape[0],) + (2,) * (seq_bits + grp_bits) + (-1, slabs.shape[2])
    )


def gather_group(mine):
    for bit in reversed(range(1, bits_of(lax.axis_size("grp")))):
        mine = double(lax.optimization_barrier(mine), "grp", bit, 1)
    return double(lax.optimization_barrier(mine), "grp", 0, 1)


def gather_last(mine, slab_rows, slabs, hold):
    grp_n = lax.axis_size("grp")
    mine = lax.optimization_barrier(mine)

    def slabs_of(rows):
        return rows[:slab_rows].reshape(slabs, -1, rows.shape[1])

    if grp_n != 2 * CORES:
        total = mine[slab_rows:].astype(F32)
        for bit in range(bits_of(grp_n)):
            total = total + swap(total, "grp", bit)
        return gather_group(slabs_of(mine)).astype(F32), total
    came = [mine] + [
        lax.ppermute(mine, "grp", [(j, j ^ at) for j in range(grp_n)]) for at in range(1, grp_n)
    ]
    came = all_after(came, *hold)
    total = sum(rows[slab_rows:].astype(F32) for rows in came)
    came = [slabs_of(rows) for rows in came]
    swapped_core = lax.axis_index("grp") % CORES == 1
    swapped_chip = lax.axis_index("grp") // CORES == 1
    came = [jnp.where(swapped_core, came[at ^ 1], came[at]) for at in range(grp_n)]
    came = [jnp.where(swapped_chip, came[at ^ 2], came[at]) for at in range(grp_n)]
    return jnp.concatenate([came[0], came[2], came[1], came[3]], axis=1).astype(F32), total


def norm_parts(tokens):
    mean = jnp.mean(tokens, axis=-1, keepdims=True)
    centred = tokens - mean
    variance = jnp.mean(centred * centred, axis=-1, keepdims=True)
    inv = lax.rsqrt(variance + norm_eps)
    return centred * inv, inv


def norm_back(normed, inv, upstream, gain):
    scaled = upstream * gain
    mean = jnp.mean(scaled, axis=-1, keepdims=True)
    inner = jnp.mean(scaled * normed, axis=-1, keepdims=True)
    return inv * (scaled - mean - normed * inner)


def exact_gelu(upper):
    return jax.nn.gelu(upper, approximate=False)


def body(
    prompt_in,
    cont_in,
    prompt_cot,
    cont_cot,
    prompt_len,
    qkv_weight,
    out_weight,
    ffn_in,
    ffn_out,
    norm_gain,
    norm_shift,
):
    rows_p = prompt_in.shape[1]
    rows_c = cont_in.shape[2]
    half = rows_p // 2
    width = prompt_in.shape[2]
    local_width = qkv_weight.shape[2]
    seq_n = lax.axis_size("seq")
    seq_i = lax.axis_index("seq")
    tp_n = lax.axis_size("tp")
    tp_i = lax.axis_index("tp")
    grp_n = lax.axis_size("grp")
    gains = norm_gain.astype(F32)
    shifts = norm_shift.astype(F32)

    seq_bits = bits_of(seq_n)
    grp_bits = bits_of(grp_n)
    held = lax.dynamic_slice_in_dim(prompt_in[0], tp_i * half, half, 0)
    direct = []
    for at in range(1, seq_n):
        direct.append(lax.ppermute(held, "seq", [(j, j ^ at) for j in range(seq_n)]))
    direct = lax.optimization_barrier(jnp.concatenate(direct, axis=0))
    swapped = swap(direct, "tp", 0)
    starts = [
        (seq_i ^ at) * rows_p + part * half for part in (tp_i, 1 - tp_i) for at in range(1, seq_n)
    ]
    inside = jnp.arange(half, dtype=jnp.int32)
    limit = prompt_len[0, 0]

    def bias_of(place):
        bias = jnp.where(place < limit, 0.0, hidden_value).astype(F32)
        return jnp.broadcast_to(bias[:, None], (place.shape[0], LANES))

    bias_far = bias_of((jnp.stack(starts)[:, None] + inside[None, :]).reshape(-1))
    away_rows = (seq_n - 1) * half
    bias_own = bias_of(seq_i * rows_p + jnp.arange(rows_p, dtype=jnp.int32))

    def project(rows):
        tokens = rows.astype(F32)
        normed, inv = norm_parts(tokens)
        return tokens, normed, inv, (normed * gains[0] + shifts[0]).astype(BF)

    def qkv(low, first):
        return jnp.einsum(
            "nd,cde->cne", low, qkv_weight[first:], preferred_element_type=F32
        ).astype(BF)

    tokens_c, one_c, inv_c, low_c = project(cont_in[0, 0])
    tokens_p, one_p, inv_p, low_p = project(prompt_in[0])
    own_c = qkv(low_c, 0)
    own_p = qkv(low_p, 0)
    part_p, stat_p, part_c, stat_c = attend_near(own_p, own_c, bias_own)
    _, one_a, _, low_a = project(after(direct, part_c))
    far_a = qkv(low_a, 1)
    part_p, stat_p, part_c, stat_c = attend_middle(
        own_p, own_c, far_a, bias_far[:away_rows], part_p, stat_p, part_c, stat_c
    )
    _, one_b, _, low_b = project(after(swapped, part_c))
    far_b = qkv(low_b, 1)

    att_c, log_c = attend_far(own_c, far_b, bias_far[away_rows:], part_c, stat_c)
    mixed_c = wide_dot(att_c, out_weight).astype(BF)
    att_p, log_p = attend_far(own_p, far_b, None, after(part_p, mixed_c), stat_p)
    mixed_p = wide_dot(att_p, out_weight).astype(BF)
    cot_c = cont_cot[0, 0]
    cot_p = prompt_cot[0]
    mixed_other_c = swap(mixed_c, "tp", 0)
    mixed_other_p = swap(mixed_p, "tp", 0)
    held = [far_a, far_b, low_a, low_b, cot_c, cot_p]
    far_a, far_b, low_a, low_b, early_c, early_p = all_after(held, mixed_p)
    far = jnp.concatenate([far_a, far_b], axis=1)
    low_f = jnp.concatenate([low_a, low_b], axis=0)
    act_grad_c = back_dot(early_c, ffn_out)
    act_grad_p = back_dot(early_p, ffn_out)
    held = [mixed_other_c, far, low_f, act_grad_c, act_grad_p, bias_far]
    mixed_other_c, far, low_f, act_grad_c, act_grad_p, bias_far = all_after(held)

    def feed(tokens, mixed, mixed_other, act_grad):
        resid = tokens + (mixed.astype(F32) + mixed_other.astype(F32))
        normed, inv = norm_parts(resid)
        low = (normed * gains[1] + shifts[1]).astype(BF)
        upper = wide_dot(low, ffn_in)
        activated, gelu_pull = jax.vjp(exact_gelu, upper)
        upper_grad = gelu_pull(act_grad)[0].astype(BF)
        terms = back_dot(upper_grad, ffn_in).astype(BF)
        return resid, normed, inv, low, activated.astype(BF), upper_grad, terms

    resid_c, two_c, inv_two_c, mid_c, act_c, up_c, terms_two_c = feed(
        tokens_c, mixed_c, mixed_other_c, act_grad_c
    )
    resid_p, two_p, inv_two_p, mid_p, act_p, up_p, terms_two_p = feed(
        after(tokens_p, terms_two_c), mixed_p, mixed_other_p, act_grad_p
    )
    second_other = swap(terms_two_c, "tp", 0)
    second_other_p = swap(terms_two_p, "tp", 0)

    def joined(first, second):
        return jnp.concatenate([first, second], axis=0)

    up_p = after(up_p, second_other)
    in_grad = rows_dot(joined(mid_p, mid_c), joined(up_p, up_c)).astype(BF)
    down_grad = rows_dot(joined(cot_p, cot_c), joined(act_p, act_c)).astype(BF)
    ffn_grad = cut(jnp.stack([in_grad, down_grad]))
    ffn_part = add_low(halve(ffn_grad, "grp", 0, seq_bits + 1))
    second_other = after(second_other, ffn_part)

    def rest(cot, normed, inv, second):
        grad = cot.astype(F32) + norm_back(normed, inv, second, gains[1])
        low = grad.astype(BF)
        return grad, low, back_dot(low, out_weight).astype(BF)

    second_c = terms_two_c.astype(F32) + second_other.astype(F32)
    grad_c, dm_c, do_c = rest(cot_c, two_c, inv_two_c, second_c)
    for bit in range(1, grp_bits):
        ffn_pair = halve(ffn_part, "grp", bit, seq_bits + 1)
        if bit + 1 < grp_bits:
            ffn_part = add_low(ffn_pair)
    dq_c, partial = pull_far(own_c, far, bias_far, do_c, att_c, log_c, None, rows_p)
    ffn_pair = all_after(ffn_pair, dq_c)
    ffn_part = add_low(ffn_pair)
    second_other_p = after(second_other_p, ffn_part)
    second_p = terms_two_p.astype(F32) + second_other_p.astype(F32)
    grad_p, dm_p, do_p = rest(cot_p, two_p, inv_two_p, second_p)
    for bit in range(seq_bits - 1):
        ffn_pair = halve(ffn_part, "seq", bit, seq_bits - bit)
        if bit + 2 < seq_bits:
            ffn_part = add_low(ffn_pair)
    out_terms_c = wide_dot(after(act_c, dq_c), ffn_out).astype(BF)
    out_other_c = swap(out_terms_c, "tp", 0)
    dq_p, dkv_f = pull_far(
        own_p, far, None, after(do_p, out_terms_c), att_p, log_p, partial, rows_p
    )

    def kv_terms(grads, weights):
        return jnp.einsum("cne,cde->nd", grads, weights, preferred_element_type=F32)

    terms_f = kv_terms(dkv_f, qkv_weight[1:])
    gain_f = jnp.sum(terms_f[:away_rows] * one_a, axis=0)
    gain_f += jnp.sum(terms_f[away_rows:] * one_b, axis=0)
    shift_f = jnp.sum(terms_f, axis=0)
    terms_f = lax.optimization_barrier(terms_f.astype(BF))
    swapped = swap(terms_f[away_rows:], "tp", 0)
    ffn_pair = all_after(ffn_pair, dkv_f)
    out_other_c = after(out_other_c, dkv_f)
    dq_p = after(dq_p, terms_f, out_other_c, *ffn_pair)
    ffn_part = add_low(ffn_pair)
    ffn_pair = halve(ffn_part, "seq", seq_bits - 1, 1)
    own_grads = pull_near(
        own_p, own_c, bias_own, (do_p, att_p, log_p, dq_p), (do_c, att_c, log_c, dq_c)
    )
    swapped, *ffn_pair, own_grads = all_after([swapped, *ffn_pair, own_grads])
    ffn_mine = lax.optimization_barrier(add_low(ffn_pair))
    for bit in reversed(range(1, grp_bits)):
        ffn_mine = lax.optimization_barrier(double(ffn_mine, "grp", bit, 1))
    low_pc = joined(low_p, low_c)
    last_grads = [rows_dot(low_pc, own_grads[0])]
    for c in range(2):
        last_grads.append(rows_dot(low_pc, own_grads[1 + c]) + rows_dot(low_f, dkv_f[c]))
    mixing_grad = rows_dot(joined(dm_p, dm_c), joined(att_p, att_c))
    last_cut = [cut(grad.astype(BF)[None]) for grad in last_grads + [mixing_grad]]
    core_i = own_bit("grp", 0)

    def core_half(which):
        return jnp.concatenate(
            [lax.dynamic_index_in_dim(g, which, seq_bits + 1, keepdims=False) for g in last_cut]
        )

    sent = lax.optimization_barrier(core_half(1 - core_i))
    last_core = add_low((core_half(core_i), swap(sent, "grp", 0)))
    ffn_mine = after(ffn_mine, sent)
    ffn_other = swap(ffn_mine, "grp", 0)
    out_other_c = after(out_other_c, last_core)
    out_c = out_terms_c.astype(F32) + out_other_c.astype(F32)
    cont_out = (resid_c + out_c).astype(BF)[None, None]
    last_part = last_core
    for bit in range(1, grp_bits):
        last_pair = halve(last_part, "grp", bit, seq_bits + 1)
        if bit + 1 < grp_bits:
            last_part = add_low(last_pair)

    terms = kv_terms(after(own_grads, sent), qkv_weight)
    terms_p, terms_c = terms[:rows_p], terms[rows_p:]
    gain_one = gain_f + jnp.sum(terms * joined(one_p, one_c), axis=0)
    shift_one = shift_f + jnp.sum(terms, axis=0)
    both = add_low((terms_f[:away_rows], swapped)).reshape(seq_n - 1, half, width)
    blocks = {at: both[at - 1] for at in range(1, seq_n)}
    for bit in range(seq_bits):
        away = [name for name in sorted(blocks) if name >> bit & 1]
        came = swap(jnp.stack([blocks.pop(name) for name in away]), "seq", bit)
        if bit == 0:
            came = after(came, last_core)
        for i, name in enumerate(away):
            near = name ^ (1 << bit)
            blocks[near] = came[i] if near not in blocks else add_low((blocks[near], came[i]))
    halves_p = lax.optimization_barrier(terms_p.astype(BF)).reshape(2, half, width)
    mine_p, other_p = halve(halves_p, "tp", 0, 0)
    two = (terms_two_c.astype(F32), terms_two_p.astype(F32))
    norm_rows = jnp.stack(
        [
            gain_one,
            jnp.sum(two[0] * two_c, axis=0) + jnp.sum(two[1] * two_p, axis=0),
            shift_one,
            jnp.sum(two[0], axis=0) + jnp.sum(two[1], axis=0),
        ]
    )
    low_norm = jnp.pad(norm_rows.astype(BF), ((0, 12), (0, 0)))
    low_terms_c = lax.optimization_barrier(joined(terms_c.astype(BF), low_norm))
    other_c = swap(low_terms_c, "tp", 0)

    last_pair = all_after(last_pair, cont_out)
    last_part = add_low(last_pair)
    late = [other_p, other_c, blocks[0], ffn_mine, ffn_other]
    other_p, other_c, home, ffn_mine, ffn_other = all_after(late, last_part)
    first = core_i == 0
    ffn_sum = jnp.concatenate(
        [jnp.where(first, ffn_mine, ffn_other), jnp.where(first, ffn_other, ffn_mine)], axis=1
    ).astype(F32)
    ffn_sums = lax.optimization_barrier((ffn_sum[0], ffn_sum[1].T))
    norm_rows = norm_rows + other_c[rows_c : rows_c + 4].astype(F32)
    norm_cut = norm_rows.reshape(4, seq_n, tp_n, -1)
    norm_cut = lax.dynamic_index_in_dim(norm_cut, tp_i, 2, keepdims=False)
    columns = norm_cut.shape[2]
    norm_cut = norm_cut.transpose(1, 0, 2).reshape(seq_n, -1)
    norm_pad = jnp.pad(norm_cut, ((0, 0), (0, 16 * local_width - norm_cut.shape[1])))
    norm_pad = norm_pad.astype(BF).reshape(seq_n, 16, local_width)
    slab_rows = last_part.shape[0] * last_part.shape[-2]
    last_part = last_part.reshape(last_part.shape[0], seq_n, -1, local_width)

    def block(at):
        slabs = lax.dynamic_index_in_dim(last_part, at, 1, keepdims=False)
        norms = lax.dynamic_index_in_dim(norm_pad, at, 0, keepdims=False)
        return jnp.concatenate([slabs.reshape(slab_rows, local_width), norms])

    last_pieces = [block(seq_i)] + [
        lax.ppermute(block(seq_i ^ at), "seq", [(j, j ^ at) for j in range(seq_n)])
        for at in range(1, seq_n)
    ]

    first_p = mine_p.astype(F32) + other_p.astype(F32) + home.astype(F32)
    first_p = lax.optimization_barrier(first_p.astype(BF))
    gathered_p = swap(first_p, "tp", 0)
    first_c = low_terms_c[:rows_c].astype(F32) + other_c[:rows_c].astype(F32)
    out_terms_p = lax.optimization_barrier(wide_dot(after(act_p, first_p), ffn_out).astype(BF))
    out_other_p = swap(out_terms_p, "tp", 0)

    last_pieces = all_after(last_pieces, *ffn_sums)
    last_mine = sum(piece.astype(F32) for piece in last_pieces).astype(BF)
    gathered_p, out_other_p = all_after([gathered_p, out_other_p], last_mine)
    first = tp_i == 0
    first_p = jnp.concatenate(
        [jnp.where(first, first_p, gathered_p), jnp.where(first, gathered_p, first_p)]
    ).astype(F32)
    out_p = out_terms_p.astype(F32) + out_other_p.astype(F32)
    prompt_out = (resid_p + out_p).astype(BF)[None]
    cont_grad = (grad_c + norm_back(one_c, inv_c, first_c, gains[0])).astype(BF)[None, None]
    prompt_grad = (grad_p + norm_back(one_p, inv_p, first_p, gains[0])).astype(BF)[None]
    last_sum, norm_sum = gather_last(last_mine, slab_rows, last_part.shape[0], (prompt_grad, cont_grad))
    norm_sum = norm_sum.reshape(-1)[: 4 * columns].reshape(4, columns)
    return (
        prompt_out,
        cont_out,
        prompt_grad,
        cont_grad,
        last_sum[:3],
        last_sum[3].T,
        *ffn_sums,
        norm_sum[:2],
        norm_sum[2:],
    )


def solution(mesh):
    placed = (
        P("grp", "seq", None),
        P("grp", "seq", None, None),
        P("grp", "seq", None),
        P("grp", "seq", None, None),
        P("grp", "seq"),
        P(None, None, "tp"),
        P("tp", None),
        P(None, "tp"),
        P("tp", None),
        P(),
        P(),
    )
    return jax.shard_map(
        body,
        mesh=mesh,
        in_specs=placed,
        out_specs=(
            P("grp", "seq", None),
            P("grp", "seq", None, None),
            P("grp", "seq", None),
            P("grp", "seq", None, None),
            P(None, "seq", "tp"),
            P("tp", "seq"),
            P("seq", "tp"),
            P("tp", "seq"),
            P(None, ("seq", "tp")),
            P(None, ("seq", "tp")),
        ),
        check_vma=False,
    )
```

```python
import functools

import jax
import jax.numpy as jnp
from jax import lax
from jax.experimental import pallas as pl
from jax.experimental.pallas import tpu as pltpu
from jax.sharding import PartitionSpec as P

HEAD = 64
CORES = 2
LANES = 128
norm_eps = 1e-05
hidden_value = -1e30
BF = jnp.bfloat16
F32 = jnp.float32
BUDGET = 56 * 1024 * 1024


def nt(left, right):
    return lax.dot_general(left, right, (((1,), (1,)), ((), ())), preferred_element_type=F32)


def tn(left, right):
    return lax.dot_general(left, right, (((0,), (0,)), ((), ())), preferred_element_type=F32)


def nn(left, right):
    return lax.dot_general(left, right, (((1,), (0,)), ((), ())), preferred_element_type=F32)


def one_head(pair, which, factor=None):
    lane = lax.broadcasted_iota(jnp.int32, pair.shape, 1)
    wide = pair.astype(F32)
    if factor is not None:
        wide = wide * factor
    return jnp.where((lane // HEAD) == which, wide, 0.0).astype(BF)


def lane_pair(pair):
    lane = lax.broadcasted_iota(jnp.int32, pair[0].shape, 1)
    return jnp.where(lane < HEAD, pair[0], pair[1])


def row_pair(pair):
    rows = pair[0].shape[1]
    return jnp.transpose(
        jnp.concatenate([jnp.broadcast_to(one, (HEAD, rows)) for one in pair], axis=0)
    )


def masked_scores(keys, mine, bias):
    scores = nt(keys, mine)
    if bias is None:
        return scores
    return scores + jnp.concatenate([bias] * (mine.shape[0] // LANES), axis=1)


def near_kernel(qp_ref, kp_ref, vp_ref, qc_ref, kc_ref, vc_ref, bias_ref, op_ref, sp_ref, oc_ref, sc_ref):
    parts = (
        (qp_ref, op_ref, sp_ref, [(kp_ref, vp_ref, None)]),
        (qc_ref, oc_ref, sc_ref, [(kp_ref, vp_ref, bias_ref), (kc_ref, vc_ref, None)]),
    )
    for q_ref, out_ref, stat_ref, sources in parts:
        outs = []
        for which in range(2):
            mine = one_head(q_ref[0], which, HEAD ** (-0.5))
            scores = [
                masked_scores(k_ref[0], mine, None if b_ref is None else b_ref[...])
                for k_ref, _, b_ref in sources
            ]
            top = functools.reduce(
                jnp.maximum, [jnp.max(s, axis=0, keepdims=True) for s in scores]
            )
            weights = [jnp.exp(s - top) for s in scores]
            stat_ref[0, which : which + 1] = top
            stat_ref[0, 2 + which : 3 + which] = sum(
                jnp.sum(w, axis=0, keepdims=True) for w in weights
            )
            outs.append(sum(tn(w.astype(BF), v_ref[0]) for w, (_, v_ref, _) in zip(weights, sources)))
        out_ref[...] = lane_pair(outs)


def kind_spec(array, kind):
    return pl.BlockSpec((1, array.shape[1], LANES), lambda p: (kind, 0, p))


def full_spec(rows):
    return pl.BlockSpec((rows, LANES), lambda p: (0, p))


def slab_spec(count, rows):
    return pl.BlockSpec((count, rows, LANES), lambda p: (0, 0, p))


def stat_spec(rows):
    return pl.BlockSpec((1, 8, rows), lambda p: (p, 0, 0))


def bias_spec(bias):
    return pl.BlockSpec(bias.shape, lambda p: (0, 0))


def params():
    return pltpu.CompilerParams(vmem_limit_bytes=BUDGET)


def cost(matmuls, pairs, width, moved):
    return pl.CostEstimate(flops=matmuls * pairs, transcendentals=0, bytes_accessed=moved)


def attend_near(own_p, own_c, bias):
    width = own_p.shape[2]
    outs = []
    for own in (own_p, own_c):
        rows = own.shape[1]
        outs += [
            jax.ShapeDtypeStruct((rows, width), F32),
            jax.ShapeDtypeStruct((width // LANES, 8, rows), F32),
        ]
    rows_p, rows_c = own_p.shape[1], own_c.shape[1]
    return pl.pallas_call(
        near_kernel,
        grid=(width // LANES,),
        in_specs=[kind_spec(own_p, c) for c in range(3)]
        + [kind_spec(own_c, c) for c in range(3)]
        + [bias_spec(bias)],
        out_specs=[full_spec(rows_p), stat_spec(rows_p), full_spec(rows_c), stat_spec(rows_c)],
        out_shape=outs,
        compiler_params=params(),
        cost_estimate=cost(2, rows_p * rows_p + rows_c * (rows_p + rows_c), width, 10 * rows_c),
    )(own_p, own_p, own_p, own_c, own_c, own_c, bias)


def middle_kernel(
    k_ref, v_ref, bias_ref, qp_ref, partp_ref, statp_ref, qc_ref, partc_ref, statc_ref,
    outp_ref, newp_ref, outc_ref, newc_ref,
):
    parts = (
        (qp_ref, None, partp_ref, statp_ref, outp_ref, newp_ref),
        (qc_ref, bias_ref, partc_ref, statc_ref, outc_ref, newc_ref),
    )
    for q_ref, b_ref, part_ref, stat_ref, out_ref, new_ref in parts:
        outs = []
        shrinks = []
        for which in range(2):
            mine = one_head(q_ref[0], which, HEAD ** (-0.5))
            scores = masked_scores(k_ref[0], mine, None if b_ref is None else b_ref[...])
            old = stat_ref[0, which : which + 1]
            top = jnp.maximum(old, jnp.max(scores, axis=0, keepdims=True))
            weights = jnp.exp(scores - top)
            shrink = jnp.exp(old - top)
            new_ref[0, which : which + 1] = top
            new_ref[0, 2 + which : 3 + which] = shrink * stat_ref[
                0, 2 + which : 3 + which
            ] + jnp.sum(weights, axis=0, keepdims=True)
            outs.append(tn(weights.astype(BF), v_ref[0]))
            shrinks.append(shrink)
        out_ref[...] = lane_pair(outs) + part_ref[...] * row_pair(shrinks)


def attend_middle(own_p, own_c, far, bias, part_p, stat_p, part_c, stat_c):
    width = own_p.shape[2]
    specs = [kind_spec(far, 0), kind_spec(far, 1), bias_spec(bias)]
    out_specs = []
    outs = []
    for own in (own_p, own_c):
        rows = own.shape[1]
        specs += [kind_spec(own, 0), full_spec(rows), stat_spec(rows)]
        out_specs += [full_spec(rows), stat_spec(rows)]
        outs += [
            jax.ShapeDtypeStruct((rows, width), F32),
            jax.ShapeDtypeStruct((width // LANES, 8, rows), F32),
        ]
    rows = own_p.shape[1] + own_c.shape[1]
    return pl.pallas_call(
        middle_kernel,
        grid=(width // LANES,),
        in_specs=specs,
        out_specs=out_specs,
        out_shape=outs,
        compiler_params=params(),
        cost_estimate=cost(2, rows * far.shape[1], width, 4 * far.shape[1]),
    )(far, far, bias, own_p, part_p, stat_p, own_c, part_c, stat_c)


def far_kernel(*refs, masked):
    if masked:
        q_ref, k_ref, v_ref, bias_ref, part_ref, stat_ref, out_ref, log_ref = refs
    else:
        q_ref, k_ref, v_ref, part_ref, stat_ref, out_ref, log_ref = refs
    outs = []
    olds = []
    news = []
    for which in range(2):
        mine = one_head(q_ref[0], which, HEAD ** (-0.5))
        scores = masked_scores(k_ref[0], mine, bias_ref[...] if masked else None)
        old = stat_ref[0, which : which + 1]
        top = jnp.maximum(old, jnp.max(scores, axis=0, keepdims=True))
        weights = jnp.exp(scores - top)
        shrink = jnp.exp(old - top)
        total = shrink * stat_ref[0, 2 + which : 3 + which] + jnp.sum(
            weights, axis=0, keepdims=True
        )
        outs.append(tn(weights.astype(BF), v_ref[0]))
        olds.append(shrink / total)
        news.append(1.0 / total)
        log_ref[0, which : which + 1] = top + jnp.log(total)
    out = lane_pair(outs) * row_pair(news) + part_ref[...] * row_pair(olds)
    out_ref[...] = out.astype(BF)


def attend_far(own, far, bias, part, stat):
    masked = bias is not None
    rows = own.shape[1]
    width = own.shape[2]
    specs = [kind_spec(own, 0), kind_spec(far, 0), kind_spec(far, 1)]
    args = [own, far, far]
    if masked:
        specs.append(bias_spec(bias))
        args.append(bias)
    return pl.pallas_call(
        functools.partial(far_kernel, masked=masked),
        grid=(width // LANES,),
        in_specs=specs + [full_spec(rows), stat_spec(rows)],
        out_specs=[full_spec(rows), stat_spec(rows)],
        out_shape=[
            jax.ShapeDtypeStruct((rows, width), BF),
            jax.ShapeDtypeStruct((width // LANES, 8, rows), F32),
        ],
        compiler_params=params(),
        cost_estimate=cost(2, rows * far.shape[1], width, 4 * far.shape[1]),
    )(*args, part, stat)


def pull_heads(q_ref, do_ref, out_ref, log_ref):
    upstream = do_ref[...]
    inner = jnp.transpose(upstream.astype(F32) * out_ref[...].astype(F32))
    return [
        (
            one_head(q_ref[0], which, HEAD ** (-0.5)),
            one_head(upstream, which),
            jnp.sum(inner[which * HEAD : (which + 1) * HEAD], axis=0, keepdims=True),
            log_ref[0, which : which + 1],
        )
        for which in range(2)
    ]


def pull_piece(keys, values, bias, heads):
    key_grads = []
    value_grads = []
    query_grads = []
    for mine, grad, delta, log in heads:
        probs = jnp.exp(masked_scores(keys, mine, bias) - log)
        spread = probs * (nt(values, grad) - delta)
        low = spread.astype(BF)
        value_grads.append(nn(probs.astype(BF), grad))
        key_grads.append(nn(low, mine))
        query_grads.append(tn(low, keys))
    return key_grads[0] + key_grads[1], value_grads[0] + value_grads[1], query_grads


def pull_far_kernel(*refs, masked, chunk):
    if masked:
        q_ref, k_ref, v_ref, bias_ref, do_ref, out_ref, log_ref, dq_ref, dkv_ref = refs
    else:
        q_ref, k_ref, v_ref, do_ref, out_ref, log_ref, old_ref, dq_ref, dkv_ref = refs
    heads = pull_heads(q_ref, do_ref, out_ref, log_ref)

    def step(at, acc):
        span = pl.ds(at, chunk)
        bias = bias_ref[span] if masked else None
        dk, dv, more = pull_piece(k_ref[0, span], v_ref[0, span], bias, heads)
        if not masked:
            dk += old_ref[0, span]
            dv += old_ref[1, span]
        dkv_ref[0, span] = dk.astype(dkv_ref.dtype)
        dkv_ref[1, span] = dv.astype(dkv_ref.dtype)
        return more if acc is None else [a + b for a, b in zip(acc, more)]

    acc = step(0, None)
    count = k_ref.shape[1] // chunk
    if count <= 4:
        for i in range(1, count):
            acc = step(i * chunk, acc)
    else:
        acc = lax.fori_loop(
            1, count, lambda i, a: step(pl.multiple_of(i * chunk, chunk), a), acc
        )
    dq_ref[...] = lane_pair(acc) * HEAD ** (-0.5)


def pull_far(own, far, bias, grad, out, log, before, chunk):
    masked = bias is not None
    rows = own.shape[1]
    width = own.shape[2]
    keys = far.shape[1]
    specs = [kind_spec(own, 0), kind_spec(far, 0), kind_spec(far, 1)]
    args = [own, far, far]
    if masked:
        specs.append(bias_spec(bias))
        args.append(bias)
    specs += [full_spec(rows), full_spec(rows), stat_spec(rows)]
    args += [grad, out, log]
    if not masked:
        specs.append(slab_spec(2, keys))
        args.append(before)
    kind = F32 if masked else BF
    return pl.pallas_call(
        functools.partial(pull_far_kernel, masked=masked, chunk=chunk),
        grid=(width // LANES,),
        in_specs=specs,
        out_specs=[full_spec(rows), slab_spec(2, keys)],
        out_shape=[
            jax.ShapeDtypeStruct((rows, width), F32),
            jax.ShapeDtypeStruct((2, keys, width), kind),
        ],
        compiler_params=params(),
        cost_estimate=cost(5, rows * keys, width, 8 * keys),
    )(*args)


def pull_near_kernel(
    qp_ref, kp_ref, vp_ref, qc_ref, kc_ref, vc_ref, bias_ref,
    dop_ref, outp_ref, logp_ref, oldp_ref, doc_ref, outc_ref, logc_ref, oldc_ref,
    grad_ref,
):
    heads_p = pull_heads(qp_ref, dop_ref, outp_ref, logp_ref)
    heads_c = pull_heads(qc_ref, doc_ref, outc_ref, logc_ref)
    dk_p, dv_p, dq_p = pull_piece(kp_ref[0], vp_ref[0], None, heads_p)
    dk_pc, dv_pc, dq_pc = pull_piece(kp_ref[0], vp_ref[0], bias_ref[...], heads_c)
    dk_c, dv_c, dq_c = pull_piece(kc_ref[0], vc_ref[0], None, heads_c)
    split = qp_ref.shape[1]
    both = [a + b for a, b in zip(dq_pc, dq_c)]
    grad_ref[0, :split] = (lane_pair(dq_p) * HEAD ** (-0.5) + oldp_ref[...]).astype(BF)
    grad_ref[1, :split] = (dk_p + dk_pc).astype(BF)
    grad_ref[2, :split] = (dv_p + dv_pc).astype(BF)
    grad_ref[0, split:] = (lane_pair(both) * HEAD ** (-0.5) + oldc_ref[...]).astype(BF)
    grad_ref[1, split:] = dk_c.astype(BF)
    grad_ref[2, split:] = dv_c.astype(BF)


def pull_near(own_p, own_c, bias, part_p, part_c):
    width = own_p.shape[2]
    rows_p, rows_c = own_p.shape[1], own_c.shape[1]
    specs = [kind_spec(own_p, c) for c in range(3)] + [kind_spec(own_c, c) for c in range(3)]
    specs.append(bias_spec(bias))
    for rows in (rows_p, rows_c):
        specs += [full_spec(rows), full_spec(rows), stat_spec(rows), full_spec(rows)]
    return pl.pallas_call(
        pull_near_kernel,
        grid=(width // LANES,),
        in_specs=specs,
        out_specs=slab_spec(3, rows_p + rows_c),
        out_shape=jax.ShapeDtypeStruct((3, rows_p + rows_c, width), BF),
        compiler_params=params(),
        cost_estimate=cost(5, rows_p * rows_p + rows_c * (rows_p + rows_c), width, 10 * rows_c),
    )(own_p, own_p, own_p, own_c, own_c, own_c, bias, *part_p, *part_c)


def swap(array, axis, bit):
    count = lax.axis_size(axis)
    return lax.ppermute(array, axis, [(j, j ^ (1 << bit)) for j in range(count)])


def own_bit(axis, bit):
    return lax.axis_index(axis) // (1 << bit) % 2


def bits_of(count):
    return count.bit_length() - 1


def halve(part, axis, bit, dim):
    mine = own_bit(axis, bit)
    sent = lax.dynamic_index_in_dim(part, 1 - mine, dim, keepdims=False)
    kept = lax.dynamic_index_in_dim(part, mine, dim, keepdims=False)
    return kept, swap(sent, axis, bit)


def add_low(pair):
    return (pair[0].astype(F32) + pair[1].astype(F32)).astype(BF)


def double(mine, axis, bit, dim):
    other = swap(mine, axis, bit)
    first = own_bit(axis, bit) == 0
    return jnp.concatenate([jnp.where(first, mine, other), jnp.where(first, other, mine)], axis=dim)


def after(value, *earlier):
    return lax.optimization_barrier((value,) + earlier)[0]


def all_after(values, *earlier):
    return list(lax.optimization_barrier(tuple(values) + earlier)[: len(values)])


def tp_sum(low):
    return low.astype(F32) + swap(low, "tp", 0).astype(F32)


def wide_dot(left, right):
    return jnp.dot(left, right, preferred_element_type=F32)


def back_dot(left, right):
    return jnp.einsum("ne,de->nd", left, right, preferred_element_type=F32)


def rows_dot(left, right):
    return jnp.einsum("nd,nf->df", left, right, preferred_element_type=F32)


def cut(slabs):
    seq_bits = bits_of(lax.axis_size("seq"))
    grp_bits = bits_of(lax.axis_size("grp"))
    return slabs.reshape(
        (slabs.shape[0],) + (2,) * (seq_bits + grp_bits) + (-1, slabs.shape[2])
    )


def gather_group(mine):
    for bit in reversed(range(1, bits_of(lax.axis_size("grp")))):
        mine = double(lax.optimization_barrier(mine), "grp", bit, 1)
    return double(lax.optimization_barrier(mine), "grp", 0, 1)


def gather_last(mine, slab_rows, slabs, hold):
    grp_n = lax.axis_size("grp")
    mine = lax.optimization_barrier(mine)

    def slabs_of(rows):
        return rows[:slab_rows].reshape(slabs, -1, rows.shape[1])

    if grp_n != 2 * CORES:
        total = mine[slab_rows:].astype(F32)
        for bit in range(bits_of(grp_n)):
            total = total + swap(total, "grp", bit)
        return gather_group(slabs_of(mine)).astype(F32), total
    came = [mine] + [
        lax.ppermute(mine, "grp", [(j, j ^ at) for j in range(grp_n)]) for at in range(1, grp_n)
    ]
    came = all_after(came, *hold)
    total = sum(rows[slab_rows:].astype(F32) for rows in came)
    came = [slabs_of(rows) for rows in came]
    swapped_core = lax.axis_index("grp") % CORES == 1
    swapped_chip = lax.axis_index("grp") // CORES == 1
    came = [jnp.where(swapped_core, came[at ^ 1], came[at]) for at in range(grp_n)]
    came = [jnp.where(swapped_chip, came[at ^ 2], came[at]) for at in range(grp_n)]
    return jnp.concatenate([came[0], came[2], came[1], came[3]], axis=1).astype(F32), total


def norm_parts(tokens):
    mean = jnp.mean(tokens, axis=-1, keepdims=True)
    centred = tokens - mean
    variance = jnp.mean(centred * centred, axis=-1, keepdims=True)
    inv = lax.rsqrt(variance + norm_eps)
    return centred * inv, inv


def norm_back(normed, inv, upstream, gain):
    scaled = upstream * gain
    mean = jnp.mean(scaled, axis=-1, keepdims=True)
    inner = jnp.mean(scaled * normed, axis=-1, keepdims=True)
    return inv * (scaled - mean - normed * inner)


def gelu_parts(upper):
    half = 0.5 + 0.5 * lax.erf(upper * 0.5**0.5)
    bell = jnp.exp(-0.5 * upper * upper) * (2.0 * jnp.pi) ** -0.5
    return upper * half, half + upper * bell


def body(
    prompt_in,
    cont_in,
    prompt_cot,
    cont_cot,
    prompt_len,
    qkv_weight,
    out_weight,
    ffn_in,
    ffn_out,
    norm_gain,
    norm_shift,
):
    rows_p = prompt_in.shape[1]
    rows_c = cont_in.shape[2]
    half = rows_p // 2
    width = prompt_in.shape[2]
    local_width = qkv_weight.shape[2]
    seq_n = lax.axis_size("seq")
    seq_i = lax.axis_index("seq")
    tp_n = lax.axis_size("tp")
    tp_i = lax.axis_index("tp")
    grp_n = lax.axis_size("grp")
    gains = norm_gain.astype(F32)
    shifts = norm_shift.astype(F32)

    seq_bits = bits_of(seq_n)
    grp_bits = bits_of(grp_n)
    held = lax.dynamic_slice_in_dim(prompt_in[0], tp_i * half, half, 0)
    direct = []
    for at in range(1, seq_n):
        direct.append(lax.ppermute(held, "seq", [(j, j ^ at) for j in range(seq_n)]))
    direct = lax.optimization_barrier(jnp.concatenate(direct, axis=0))
    swapped = swap(direct, "tp", 0)
    starts = [
        (seq_i ^ at) * rows_p + part * half for part in (tp_i, 1 - tp_i) for at in range(1, seq_n)
    ]
    inside = jnp.arange(half, dtype=jnp.int32)
    limit = prompt_len[0, 0]

    def bias_of(place):
        bias = jnp.where(place < limit, 0.0, hidden_value).astype(F32)
        return jnp.broadcast_to(bias[:, None], (place.shape[0], LANES))

    bias_far = bias_of((jnp.stack(starts)[:, None] + inside[None, :]).reshape(-1))
    away_rows = (seq_n - 1) * half
    bias_own = bias_of(seq_i * rows_p + jnp.arange(rows_p, dtype=jnp.int32))

    def project(rows):
        tokens = rows.astype(F32)
        normed, inv = norm_parts(tokens)
        return tokens, normed, inv, (normed * gains[0] + shifts[0]).astype(BF)

    def qkv(low, first):
        return jnp.einsum(
            "nd,cde->cne", low, qkv_weight[first:], preferred_element_type=F32
        ).astype(BF)

    tokens_c, one_c, inv_c, low_c = project(cont_in[0, 0])
    tokens_p, one_p, inv_p, low_p = project(prompt_in[0])
    own_c = qkv(low_c, 0)
    own_p = qkv(low_p, 0)
    part_p, stat_p, part_c, stat_c = attend_near(own_p, own_c, bias_own)
    _, one_a, _, low_a = project(after(direct, part_c))
    far_a = qkv(low_a, 1)
    part_p, stat_p, part_c, stat_c = attend_middle(
        own_p, own_c, far_a, bias_far[:away_rows], part_p, stat_p, part_c, stat_c
    )
    _, one_b, _, low_b = project(after(swapped, part_c))
    far_b = qkv(low_b, 1)

    att_c, log_c = attend_far(own_c, far_b, bias_far[away_rows:], part_c, stat_c)
    mixed_c = wide_dot(att_c, out_weight).astype(BF)
    att_p, log_p = attend_far(own_p, far_b, None, after(part_p, mixed_c), stat_p)
    mixed_p = wide_dot(att_p, out_weight).astype(BF)
    cot_c = cont_cot[0, 0]
    cot_p = prompt_cot[0]
    mixed_other_c = swap(mixed_c, "tp", 0)
    mixed_other_p = swap(mixed_p, "tp", 0)
    held = [far_a, far_b, low_a, low_b, cot_c, cot_p]
    far_a, far_b, low_a, low_b, early_c, early_p = all_after(held, mixed_p)
    far = jnp.concatenate([far_a, far_b], axis=1)
    low_f = jnp.concatenate([low_a, low_b], axis=0)
    act_grad_c = back_dot(early_c, ffn_out)
    act_grad_p = back_dot(early_p, ffn_out)
    held = [mixed_other_c, far, low_f, act_grad_c, act_grad_p, bias_far]
    mixed_other_c, far, low_f, act_grad_c, act_grad_p, bias_far = all_after(held)

    def feed(tokens, mixed, mixed_other, act_grad):
        resid = tokens + (mixed.astype(F32) + mixed_other.astype(F32))
        normed, inv = norm_parts(resid)
        low = (normed * gains[1] + shifts[1]).astype(BF)
        upper = wide_dot(low, ffn_in)
        activated, slope = gelu_parts(upper)
        upper_grad = (act_grad * slope).astype(BF)
        terms = back_dot(upper_grad, ffn_in).astype(BF)
        return resid, normed, inv, low, activated.astype(BF), upper_grad, terms

    resid_c, two_c, inv_two_c, mid_c, act_c, up_c, terms_two_c = feed(
        tokens_c, mixed_c, mixed_other_c, act_grad_c
    )
    resid_p, two_p, inv_two_p, mid_p, act_p, up_p, terms_two_p = feed(
        after(tokens_p, terms_two_c), mixed_p, mixed_other_p, act_grad_p
    )
    second_other = swap(terms_two_c, "tp", 0)
    second_other_p = swap(terms_two_p, "tp", 0)

    def joined(first, second):
        return jnp.concatenate([first, second], axis=0)

    in_grad = rows_dot(joined(mid_p, mid_c), joined(up_p, up_c)).astype(BF)
    down_grad = rows_dot(joined(cot_p, cot_c), joined(act_p, act_c)).astype(BF)
    in_grad = after(in_grad, second_other, terms_two_p)
    ffn_grad = cut(jnp.stack([in_grad, down_grad]))
    ffn_part = add_low(halve(ffn_grad, "grp", 0, seq_bits + 1))
    second_other = after(second_other, ffn_part)

    def rest(cot, normed, inv, second):
        grad = cot.astype(F32) + norm_back(normed, inv, second, gains[1])
        low = grad.astype(BF)
        return grad, low, back_dot(low, out_weight).astype(BF)

    second_c = terms_two_c.astype(F32) + second_other.astype(F32)
    grad_c, dm_c, do_c = rest(cot_c, two_c, inv_two_c, second_c)
    for bit in range(1, grp_bits):
        ffn_pair = halve(ffn_part, "grp", bit, seq_bits + 1)
        if bit + 1 < grp_bits:
            ffn_part = add_low(ffn_pair)
    dq_c, partial = pull_far(own_c, far, bias_far, do_c, att_c, log_c, None, rows_p)
    ffn_pair = all_after(ffn_pair, dq_c)
    ffn_part = add_low(ffn_pair)
    second_other_p = after(second_other_p, ffn_part)
    second_p = terms_two_p.astype(F32) + second_other_p.astype(F32)
    grad_p, dm_p, do_p = rest(cot_p, two_p, inv_two_p, second_p)
    for bit in range(seq_bits - 1):
        ffn_pair = halve(ffn_part, "seq", bit, seq_bits - bit)
        if bit + 2 < seq_bits:
            ffn_part = add_low(ffn_pair)
    out_terms_c = wide_dot(after(act_c, dq_c), ffn_out).astype(BF)
    out_other_c = swap(out_terms_c, "tp", 0)
    dq_p, dkv_f = pull_far(
        own_p, far, None, after(do_p, out_terms_c), att_p, log_p, partial, rows_p
    )

    def kv_terms(grads, weights):
        return jnp.einsum("cne,cde->nd", grads, weights, preferred_element_type=F32)

    terms_f = kv_terms(dkv_f, qkv_weight[1:])
    gain_f = jnp.sum(terms_f[:away_rows] * one_a, axis=0)
    gain_f += jnp.sum(terms_f[away_rows:] * one_b, axis=0)
    shift_f = jnp.sum(terms_f, axis=0)
    terms_f = lax.optimization_barrier(terms_f.astype(BF))
    swapped = swap(terms_f[away_rows:], "tp", 0)
    ffn_pair = all_after(ffn_pair, dkv_f)
    out_other_c = after(out_other_c, dkv_f)
    dq_p = after(dq_p, terms_f, out_other_c, *ffn_pair)
    ffn_part = add_low(ffn_pair)
    ffn_pair = halve(ffn_part, "seq", seq_bits - 1, 1)
    own_grads = pull_near(
        own_p, own_c, bias_own, (do_p, att_p, log_p, dq_p), (do_c, att_c, log_c, dq_c)
    )
    swapped, *ffn_pair, own_grads = all_after([swapped, *ffn_pair, own_grads])
    ffn_mine = lax.optimization_barrier(add_low(ffn_pair))
    for bit in reversed(range(1, grp_bits)):
        ffn_mine = lax.optimization_barrier(double(ffn_mine, "grp", bit, 1))
    low_pc = joined(low_p, low_c)
    last_grads = [rows_dot(low_pc, own_grads[0])]
    for c in range(2):
        last_grads.append(rows_dot(low_pc, own_grads[1 + c]) + rows_dot(low_f, dkv_f[c]))
    mixing_grad = rows_dot(joined(dm_p, dm_c), joined(att_p, att_c))
    last_cut = [cut(grad.astype(BF)[None]) for grad in last_grads + [mixing_grad]]
    core_i = own_bit("grp", 0)

    def core_half(which):
        return jnp.concatenate(
            [lax.dynamic_index_in_dim(g, which, seq_bits + 1, keepdims=False) for g in last_cut]
        )

    sent = lax.optimization_barrier(core_half(1 - core_i))
    last_core = add_low((core_half(core_i), swap(sent, "grp", 0)))
    ffn_mine = after(ffn_mine, sent)
    ffn_other = swap(ffn_mine, "grp", 0)
    out_other_c = after(out_other_c, last_core)
    out_c = out_terms_c.astype(F32) + out_other_c.astype(F32)
    cont_out = (resid_c + out_c).astype(BF)[None, None]
    last_part = last_core
    for bit in range(1, grp_bits):
        last_pair = halve(last_part, "grp", bit, seq_bits + 1)
        if bit + 1 < grp_bits:
            last_part = add_low(last_pair)

    terms = kv_terms(after(own_grads, sent), qkv_weight)
    terms_p, terms_c = terms[:rows_p], terms[rows_p:]
    gain_one = gain_f + jnp.sum(terms * joined(one_p, one_c), axis=0)
    shift_one = shift_f + jnp.sum(terms, axis=0)
    both = add_low((terms_f[:away_rows], swapped)).reshape(seq_n - 1, half, width)
    blocks = {at: both[at - 1] for at in range(1, seq_n)}
    for bit in range(seq_bits):
        away = [name for name in sorted(blocks) if name >> bit & 1]
        came = swap(jnp.stack([blocks.pop(name) for name in away]), "seq", bit)
        if bit == 0:
            came = after(came, last_core)
        for i, name in enumerate(away):
            near = name ^ (1 << bit)
            blocks[near] = came[i] if near not in blocks else add_low((blocks[near], came[i]))
    halves_p = lax.optimization_barrier(terms_p.astype(BF)).reshape(2, half, width)
    mine_p, other_p = halve(halves_p, "tp", 0, 0)
    two = (terms_two_c.astype(F32), terms_two_p.astype(F32))
    norm_rows = jnp.stack(
        [
            gain_one,
            jnp.sum(two[0] * two_c, axis=0) + jnp.sum(two[1] * two_p, axis=0),
            shift_one,
            jnp.sum(two[0], axis=0) + jnp.sum(two[1], axis=0),
        ]
    )
    low_norm = jnp.pad(norm_rows.astype(BF), ((0, 12), (0, 0)))
    low_terms_c = lax.optimization_barrier(joined(terms_c.astype(BF), low_norm))
    other_c = swap(low_terms_c, "tp", 0)

    last_pair = all_after(last_pair, cont_out)
    last_part = add_low(last_pair)
    late = [other_p, other_c, blocks[0], ffn_mine, ffn_other]
    other_p, other_c, home, ffn_mine, ffn_other = all_after(late, last_part)
    first = core_i == 0
    ffn_sum = jnp.concatenate(
        [jnp.where(first, ffn_mine, ffn_other), jnp.where(first, ffn_other, ffn_mine)], axis=1
    ).astype(F32)
    ffn_sums = lax.optimization_barrier((ffn_sum[0], ffn_sum[1].T))
    norm_rows = norm_rows + other_c[rows_c : rows_c + 4].astype(F32)
    norm_cut = norm_rows.reshape(4, seq_n, tp_n, -1)
    norm_cut = lax.dynamic_index_in_dim(norm_cut, tp_i, 2, keepdims=False)
    columns = norm_cut.shape[2]
    norm_cut = norm_cut.transpose(1, 0, 2).reshape(seq_n, -1)
    norm_pad = jnp.pad(norm_cut, ((0, 0), (0, 16 * local_width - norm_cut.shape[1])))
    norm_pad = norm_pad.astype(BF).reshape(seq_n, 16, local_width)
    slab_rows = last_part.shape[0] * last_part.shape[-2]
    last_part = last_part.reshape(last_part.shape[0], seq_n, -1, local_width)

    def block(at):
        slabs = lax.dynamic_index_in_dim(last_part, at, 1, keepdims=False)
        norms = lax.dynamic_index_in_dim(norm_pad, at, 0, keepdims=False)
        return jnp.concatenate([slabs.reshape(slab_rows, local_width), norms])

    last_pieces = [block(seq_i)] + [
        lax.ppermute(block(seq_i ^ at), "seq", [(j, j ^ at) for j in range(seq_n)])
        for at in range(1, seq_n)
    ]

    first_p = mine_p.astype(F32) + other_p.astype(F32) + home.astype(F32)
    first_p = lax.optimization_barrier(first_p.astype(BF))
    gathered_p = swap(first_p, "tp", 0)
    first_c = low_terms_c[:rows_c].astype(F32) + other_c[:rows_c].astype(F32)
    out_terms_p = lax.optimization_barrier(wide_dot(after(act_p, first_p), ffn_out).astype(BF))
    out_other_p = swap(out_terms_p, "tp", 0)

    last_pieces = all_after(last_pieces, *ffn_sums)
    last_mine = sum(piece.astype(F32) for piece in last_pieces).astype(BF)
    gathered_p, out_other_p = all_after([gathered_p, out_other_p], last_mine)
    first = tp_i == 0
    first_p = jnp.concatenate(
        [jnp.where(first, first_p, gathered_p), jnp.where(first, gathered_p, first_p)]
    ).astype(F32)
    out_p = out_terms_p.astype(F32) + out_other_p.astype(F32)
    prompt_out = (resid_p + out_p).astype(BF)[None]
    cont_grad = (grad_c + norm_back(one_c, inv_c, first_c, gains[0])).astype(BF)[None, None]
    prompt_grad = (grad_p + norm_back(one_p, inv_p, first_p, gains[0])).astype(BF)[None]
    last_sum, norm_sum = gather_last(last_mine, slab_rows, last_part.shape[0], (prompt_grad, cont_grad))
    norm_sum = norm_sum.reshape(-1)[: 4 * columns].reshape(4, columns)
    return (
        prompt_out,
        cont_out,
        prompt_grad,
        cont_grad,
        last_sum[:3],
        last_sum[3].T,
        *ffn_sums,
        norm_sum[:2],
        norm_sum[2:],
    )


def solution(mesh):
    placed = (
        P("grp", "seq", None),
        P("grp", "seq", None, None),
        P("grp", "seq", None),
        P("grp", "seq", None, None),
        P("grp", "seq"),
        P(None, None, "tp"),
        P("tp", None),
        P(None, "tp"),
        P("tp", None),
        P(),
        P(),
    )
    return jax.shard_map(
        body,
        mesh=mesh,
        in_specs=placed,
        out_specs=(
            P("grp", "seq", None),
            P("grp", "seq", None, None),
            P("grp", "seq", None),
            P("grp", "seq", None, None),
            P(None, "seq", "tp"),
            P("tp", "seq"),
            P("seq", "tp"),
            P("tp", "seq"),
            P(None, ("seq", "tp")),
            P(None, ("seq", "tp")),
        ),
        check_vma=False,
    )
```

```python
import functools

import jax
import jax.numpy as jnp
from jax import lax
from jax.experimental import pallas as pl
from jax.experimental.pallas import tpu as pltpu
from jax.sharding import PartitionSpec as P

HEAD = 64
CORES = 2
LANES = 128
norm_eps = 1e-05
hidden_value = -1e30
BF = jnp.bfloat16
F32 = jnp.float32
BUDGET = 56 * 1024 * 1024


def nt(left, right):
    return lax.dot_general(left, right, (((1,), (1,)), ((), ())), preferred_element_type=F32)


def tn(left, right):
    return lax.dot_general(left, right, (((0,), (0,)), ((), ())), preferred_element_type=F32)


def nn(left, right):
    return lax.dot_general(left, right, (((1,), (0,)), ((), ())), preferred_element_type=F32)


def one_head(pair, which, factor=None):
    lane = lax.broadcasted_iota(jnp.int32, pair.shape, 1)
    wide = pair.astype(F32)
    if factor is not None:
        wide = wide * factor
    return jnp.where((lane // HEAD) == which, wide, 0.0).astype(BF)


def lane_pair(pair):
    lane = lax.broadcasted_iota(jnp.int32, pair[0].shape, 1)
    return jnp.where(lane < HEAD, pair[0], pair[1])


def row_pair(pair):
    rows = pair[0].shape[1]
    return jnp.transpose(
        jnp.concatenate([jnp.broadcast_to(one, (HEAD, rows)) for one in pair], axis=0)
    )


def masked_scores(keys, mine, bias):
    scores = nt(keys, mine)
    if bias is None:
        return scores
    return scores + jnp.concatenate([bias] * (mine.shape[0] // LANES), axis=1)


def near_kernel(qp_ref, kp_ref, vp_ref, qc_ref, kc_ref, vc_ref, bias_ref, op_ref, sp_ref, oc_ref, sc_ref):
    parts = (
        (qp_ref, op_ref, sp_ref, [(kp_ref, vp_ref, None)]),
        (qc_ref, oc_ref, sc_ref, [(kp_ref, vp_ref, bias_ref), (kc_ref, vc_ref, None)]),
    )
    for q_ref, out_ref, stat_ref, sources in parts:
        outs = []
        for which in range(2):
            mine = one_head(q_ref[0], which, HEAD ** (-0.5))
            scores = [
                masked_scores(k_ref[0], mine, None if b_ref is None else b_ref[...])
                for k_ref, _, b_ref in sources
            ]
            top = functools.reduce(
                jnp.maximum, [jnp.max(s, axis=0, keepdims=True) for s in scores]
            )
            weights = [jnp.exp(s - top) for s in scores]
            stat_ref[0, which : which + 1] = top
            stat_ref[0, 2 + which : 3 + which] = sum(
                jnp.sum(w, axis=0, keepdims=True) for w in weights
            )
            outs.append(sum(tn(w.astype(BF), v_ref[0]) for w, (_, v_ref, _) in zip(weights, sources)))
        out_ref[...] = lane_pair(outs)


def kind_spec(array, kind):
    return pl.BlockSpec((1, array.shape[1], LANES), lambda p: (kind, 0, p))


def full_spec(rows):
    return pl.BlockSpec((rows, LANES), lambda p: (0, p))


def slab_spec(count, rows):
    return pl.BlockSpec((count, rows, LANES), lambda p: (0, 0, p))


def stat_spec(rows):
    return pl.BlockSpec((1, 8, rows), lambda p: (p, 0, 0))


def bias_spec(bias):
    return pl.BlockSpec(bias.shape, lambda p: (0, 0))


def params():
    return pltpu.CompilerParams(vmem_limit_bytes=BUDGET)


def cost(matmuls, pairs, width, moved):
    return pl.CostEstimate(flops=matmuls * pairs, transcendentals=0, bytes_accessed=moved)


def attend_near(own_p, own_c, bias):
    width = own_p.shape[2]
    outs = []
    for own in (own_p, own_c):
        rows = own.shape[1]
        outs += [
            jax.ShapeDtypeStruct((rows, width), F32),
            jax.ShapeDtypeStruct((width // LANES, 8, rows), F32),
        ]
    rows_p, rows_c = own_p.shape[1], own_c.shape[1]
    return pl.pallas_call(
        near_kernel,
        grid=(width // LANES,),
        in_specs=[kind_spec(own_p, c) for c in range(3)]
        + [kind_spec(own_c, c) for c in range(3)]
        + [bias_spec(bias)],
        out_specs=[full_spec(rows_p), stat_spec(rows_p), full_spec(rows_c), stat_spec(rows_c)],
        out_shape=outs,
        compiler_params=params(),
        cost_estimate=cost(2, rows_p * rows_p + rows_c * (rows_p + rows_c), width, 10 * rows_c),
    )(own_p, own_p, own_p, own_c, own_c, own_c, bias)


def middle_kernel(
    k_ref, v_ref, bias_ref, qp_ref, partp_ref, statp_ref, qc_ref, partc_ref, statc_ref,
    outp_ref, newp_ref, outc_ref, newc_ref,
):
    parts = (
        (qp_ref, None, partp_ref, statp_ref, outp_ref, newp_ref),
        (qc_ref, bias_ref, partc_ref, statc_ref, outc_ref, newc_ref),
    )
    for q_ref, b_ref, part_ref, stat_ref, out_ref, new_ref in parts:
        outs = []
        shrinks = []
        for which in range(2):
            mine = one_head(q_ref[0], which, HEAD ** (-0.5))
            scores = masked_scores(k_ref[0], mine, None if b_ref is None else b_ref[...])
            old = stat_ref[0, which : which + 1]
            top = jnp.maximum(old, jnp.max(scores, axis=0, keepdims=True))
            weights = jnp.exp(scores - top)
            shrink = jnp.exp(old - top)
            new_ref[0, which : which + 1] = top
            new_ref[0, 2 + which : 3 + which] = shrink * stat_ref[
                0, 2 + which : 3 + which
            ] + jnp.sum(weights, axis=0, keepdims=True)
            outs.append(tn(weights.astype(BF), v_ref[0]))
            shrinks.append(shrink)
        out_ref[...] = lane_pair(outs) + part_ref[...] * row_pair(shrinks)


def attend_middle(own_p, own_c, far, bias, part_p, stat_p, part_c, stat_c):
    width = own_p.shape[2]
    specs = [kind_spec(far, 0), kind_spec(far, 1), bias_spec(bias)]
    out_specs = []
    outs = []
    for own in (own_p, own_c):
        rows = own.shape[1]
        specs += [kind_spec(own, 0), full_spec(rows), stat_spec(rows)]
        out_specs += [full_spec(rows), stat_spec(rows)]
        outs += [
            jax.ShapeDtypeStruct((rows, width), F32),
            jax.ShapeDtypeStruct((width // LANES, 8, rows), F32),
        ]
    rows = own_p.shape[1] + own_c.shape[1]
    return pl.pallas_call(
        middle_kernel,
        grid=(width // LANES,),
        in_specs=specs,
        out_specs=out_specs,
        out_shape=outs,
        compiler_params=params(),
        cost_estimate=cost(2, rows * far.shape[1], width, 4 * far.shape[1]),
    )(far, far, bias, own_p, part_p, stat_p, own_c, part_c, stat_c)


def far_kernel(*refs, masked):
    if masked:
        q_ref, k_ref, v_ref, bias_ref, part_ref, stat_ref, out_ref, log_ref = refs
    else:
        q_ref, k_ref, v_ref, part_ref, stat_ref, out_ref, log_ref = refs
    outs = []
    olds = []
    news = []
    for which in range(2):
        mine = one_head(q_ref[0], which, HEAD ** (-0.5))
        scores = masked_scores(k_ref[0], mine, bias_ref[...] if masked else None)
        old = stat_ref[0, which : which + 1]
        top = jnp.maximum(old, jnp.max(scores, axis=0, keepdims=True))
        weights = jnp.exp(scores - top)
        shrink = jnp.exp(old - top)
        total = shrink * stat_ref[0, 2 + which : 3 + which] + jnp.sum(
            weights, axis=0, keepdims=True
        )
        outs.append(tn(weights.astype(BF), v_ref[0]))
        olds.append(shrink / total)
        news.append(1.0 / total)
        log_ref[0, which : which + 1] = top + jnp.log(total)
    out = lane_pair(outs) * row_pair(news) + part_ref[...] * row_pair(olds)
    out_ref[...] = out.astype(BF)


def attend_far(own, far, bias, part, stat):
    masked = bias is not None
    rows = own.shape[1]
    width = own.shape[2]
    specs = [kind_spec(own, 0), kind_spec(far, 0), kind_spec(far, 1)]
    args = [own, far, far]
    if masked:
        specs.append(bias_spec(bias))
        args.append(bias)
    return pl.pallas_call(
        functools.partial(far_kernel, masked=masked),
        grid=(width // LANES,),
        in_specs=specs + [full_spec(rows), stat_spec(rows)],
        out_specs=[full_spec(rows), stat_spec(rows)],
        out_shape=[
            jax.ShapeDtypeStruct((rows, width), BF),
            jax.ShapeDtypeStruct((width // LANES, 8, rows), F32),
        ],
        compiler_params=params(),
        cost_estimate=cost(2, rows * far.shape[1], width, 4 * far.shape[1]),
    )(*args, part, stat)


def pull_heads(q_ref, do_ref, out_ref, log_ref):
    upstream = do_ref[...]
    inner = jnp.transpose(upstream.astype(F32) * out_ref[...].astype(F32))
    return [
        (
            one_head(q_ref[0], which, HEAD ** (-0.5)),
            one_head(upstream, which),
            jnp.sum(inner[which * HEAD : (which + 1) * HEAD], axis=0, keepdims=True),
            log_ref[0, which : which + 1],
        )
        for which in range(2)
    ]


def pull_piece(keys, values, bias, heads):
    key_grads = []
    value_grads = []
    query_grads = []
    for mine, grad, delta, log in heads:
        probs = jnp.exp(masked_scores(keys, mine, bias) - log)
        spread = probs * (nt(values, grad) - delta)
        low = spread.astype(BF)
        value_grads.append(nn(probs.astype(BF), grad))
        key_grads.append(nn(low, mine))
        query_grads.append(tn(low, keys))
    return key_grads[0] + key_grads[1], value_grads[0] + value_grads[1], query_grads


def pull_far_kernel(*refs, masked, chunk):
    if masked:
        q_ref, k_ref, v_ref, bias_ref, do_ref, out_ref, log_ref, dq_ref, dkv_ref = refs
    else:
        q_ref, k_ref, v_ref, do_ref, out_ref, log_ref, old_ref, dq_ref, dkv_ref = refs
    heads = pull_heads(q_ref, do_ref, out_ref, log_ref)

    def step(at, acc):
        span = pl.ds(at, chunk)
        bias = bias_ref[span] if masked else None
        dk, dv, more = pull_piece(k_ref[0, span], v_ref[0, span], bias, heads)
        if not masked:
            dk += old_ref[0, span]
            dv += old_ref[1, span]
        dkv_ref[0, span] = dk.astype(dkv_ref.dtype)
        dkv_ref[1, span] = dv.astype(dkv_ref.dtype)
        return more if acc is None else [a + b for a, b in zip(acc, more)]

    acc = step(0, None)
    count = k_ref.shape[1] // chunk
    if count <= 4:
        for i in range(1, count):
            acc = step(i * chunk, acc)
    else:
        acc = lax.fori_loop(
            1, count, lambda i, a: step(pl.multiple_of(i * chunk, chunk), a), acc
        )
    dq_ref[...] = lane_pair(acc) * HEAD ** (-0.5)


def pull_far(own, far, bias, grad, out, log, before, chunk):
    masked = bias is not None
    rows = own.shape[1]
    width = own.shape[2]
    keys = far.shape[1]
    specs = [kind_spec(own, 0), kind_spec(far, 0), kind_spec(far, 1)]
    args = [own, far, far]
    if masked:
        specs.append(bias_spec(bias))
        args.append(bias)
    specs += [full_spec(rows), full_spec(rows), stat_spec(rows)]
    args += [grad, out, log]
    if not masked:
        specs.append(slab_spec(2, keys))
        args.append(before)
    kind = F32 if masked else BF
    return pl.pallas_call(
        functools.partial(pull_far_kernel, masked=masked, chunk=chunk),
        grid=(width // LANES,),
        in_specs=specs,
        out_specs=[full_spec(rows), slab_spec(2, keys)],
        out_shape=[
            jax.ShapeDtypeStruct((rows, width), F32),
            jax.ShapeDtypeStruct((2, keys, width), kind),
        ],
        compiler_params=params(),
        cost_estimate=cost(5, rows * keys, width, 8 * keys),
    )(*args)


def pull_near_kernel(
    qp_ref, kp_ref, vp_ref, qc_ref, kc_ref, vc_ref, bias_ref,
    dop_ref, outp_ref, logp_ref, oldp_ref, doc_ref, outc_ref, logc_ref, oldc_ref,
    grad_ref,
):
    heads_p = pull_heads(qp_ref, dop_ref, outp_ref, logp_ref)
    heads_c = pull_heads(qc_ref, doc_ref, outc_ref, logc_ref)
    dk_p, dv_p, dq_p = pull_piece(kp_ref[0], vp_ref[0], None, heads_p)
    dk_pc, dv_pc, dq_pc = pull_piece(kp_ref[0], vp_ref[0], bias_ref[...], heads_c)
    dk_c, dv_c, dq_c = pull_piece(kc_ref[0], vc_ref[0], None, heads_c)
    split = qp_ref.shape[1]
    both = [a + b for a, b in zip(dq_pc, dq_c)]
    grad_ref[0, :split] = (lane_pair(dq_p) * HEAD ** (-0.5) + oldp_ref[...]).astype(BF)
    grad_ref[1, :split] = (dk_p + dk_pc).astype(BF)
    grad_ref[2, :split] = (dv_p + dv_pc).astype(BF)
    grad_ref[0, split:] = (lane_pair(both) * HEAD ** (-0.5) + oldc_ref[...]).astype(BF)
    grad_ref[1, split:] = dk_c.astype(BF)
    grad_ref[2, split:] = dv_c.astype(BF)


def pull_near(own_p, own_c, bias, part_p, part_c):
    width = own_p.shape[2]
    rows_p, rows_c = own_p.shape[1], own_c.shape[1]
    specs = [kind_spec(own_p, c) for c in range(3)] + [kind_spec(own_c, c) for c in range(3)]
    specs.append(bias_spec(bias))
    for rows in (rows_p, rows_c):
        specs += [full_spec(rows), full_spec(rows), stat_spec(rows), full_spec(rows)]
    return pl.pallas_call(
        pull_near_kernel,
        grid=(width // LANES,),
        in_specs=specs,
        out_specs=slab_spec(3, rows_p + rows_c),
        out_shape=jax.ShapeDtypeStruct((3, rows_p + rows_c, width), BF),
        compiler_params=params(),
        cost_estimate=cost(5, rows_p * rows_p + rows_c * (rows_p + rows_c), width, 10 * rows_c),
    )(own_p, own_p, own_p, own_c, own_c, own_c, bias, *part_p, *part_c)


def swap(array, axis, bit):
    count = lax.axis_size(axis)
    return lax.ppermute(array, axis, [(j, j ^ (1 << bit)) for j in range(count)])


def own_bit(axis, bit):
    return lax.axis_index(axis) // (1 << bit) % 2


def bits_of(count):
    return count.bit_length() - 1


def halve(part, axis, bit, dim):
    mine = own_bit(axis, bit)
    sent = lax.dynamic_index_in_dim(part, 1 - mine, dim, keepdims=False)
    kept = lax.dynamic_index_in_dim(part, mine, dim, keepdims=False)
    return kept, swap(sent, axis, bit)


def add_low(pair):
    return (pair[0].astype(F32) + pair[1].astype(F32)).astype(BF)


def double(mine, axis, bit, dim):
    other = swap(mine, axis, bit)
    first = own_bit(axis, bit) == 0
    return jnp.concatenate([jnp.where(first, mine, other), jnp.where(first, other, mine)], axis=dim)


def after(value, *earlier):
    return lax.optimization_barrier((value,) + earlier)[0]


def all_after(values, *earlier):
    return list(lax.optimization_barrier(tuple(values) + earlier)[: len(values)])


def tp_sum(low):
    return low.astype(F32) + swap(low, "tp", 0).astype(F32)


def wide_dot(left, right):
    return jnp.dot(left, right, preferred_element_type=F32)


def back_dot(left, right):
    return jnp.einsum("ne,de->nd", left, right, preferred_element_type=F32)


def rows_dot(left, right):
    return jnp.einsum("nd,nf->df", left, right, preferred_element_type=F32)


def cut(slabs):
    seq_bits = bits_of(lax.axis_size("seq"))
    grp_bits = bits_of(lax.axis_size("grp"))
    return slabs.reshape(
        (slabs.shape[0],) + (2,) * (seq_bits + grp_bits) + (-1, slabs.shape[2])
    )


def gather_group(mine):
    for bit in reversed(range(1, bits_of(lax.axis_size("grp")))):
        mine = double(lax.optimization_barrier(mine), "grp", bit, 1)
    return double(lax.optimization_barrier(mine), "grp", 0, 1)


def gather_last(mine, slab_rows, slabs, hold):
    grp_n = lax.axis_size("grp")
    mine = lax.optimization_barrier(mine)

    def slabs_of(rows):
        return rows[:slab_rows].reshape(slabs, -1, rows.shape[1])

    if grp_n != 2 * CORES:
        total = mine[slab_rows:].astype(F32)
        for bit in range(bits_of(grp_n)):
            total = total + swap(total, "grp", bit)
        return gather_group(slabs_of(mine)).astype(F32), total
    came = [mine] + [
        lax.ppermute(mine, "grp", [(j, j ^ at) for j in range(grp_n)]) for at in range(1, grp_n)
    ]
    came = all_after(came, *hold)
    total = sum(rows[slab_rows:].astype(F32) for rows in came)
    came = [slabs_of(rows) for rows in came]
    swapped_core = lax.axis_index("grp") % CORES == 1
    swapped_chip = lax.axis_index("grp") // CORES == 1
    came = [jnp.where(swapped_core, came[at ^ 1], came[at]) for at in range(grp_n)]
    came = [jnp.where(swapped_chip, came[at ^ 2], came[at]) for at in range(grp_n)]
    return jnp.concatenate([came[0], came[2], came[1], came[3]], axis=1).astype(F32), total


def norm_parts(tokens):
    mean = jnp.mean(tokens, axis=-1, keepdims=True)
    centred = tokens - mean
    variance = jnp.mean(centred * centred, axis=-1, keepdims=True)
    inv = lax.rsqrt(variance + norm_eps)
    return centred * inv, inv


def norm_back(normed, inv, upstream, gain):
    scaled = upstream * gain
    mean = jnp.mean(scaled, axis=-1, keepdims=True)
    inner = jnp.mean(scaled * normed, axis=-1, keepdims=True)
    return inv * (scaled - mean - normed * inner)


def gelu_parts(upper):
    half = 0.5 + 0.5 * lax.erf(upper * 0.5**0.5)
    bell = jnp.exp(-0.5 * upper * upper) * (2.0 * jnp.pi) ** -0.5
    return upper * half, half + upper * bell


def body(
    prompt_in,
    cont_in,
    prompt_cot,
    cont_cot,
    prompt_len,
    qkv_weight,
    out_weight,
    ffn_in,
    ffn_out,
    norm_gain,
    norm_shift,
):
    rows_p = prompt_in.shape[1]
    rows_c = cont_in.shape[2]
    half = rows_p // 2
    width = prompt_in.shape[2]
    local_width = qkv_weight.shape[2]
    seq_n = lax.axis_size("seq")
    seq_i = lax.axis_index("seq")
    tp_n = lax.axis_size("tp")
    tp_i = lax.axis_index("tp")
    grp_n = lax.axis_size("grp")
    gains = norm_gain.astype(F32)
    shifts = norm_shift.astype(F32)

    seq_bits = bits_of(seq_n)
    grp_bits = bits_of(grp_n)
    held = lax.dynamic_slice_in_dim(prompt_in[0], tp_i * half, half, 0)
    direct = []
    for at in range(1, seq_n):
        direct.append(lax.ppermute(held, "seq", [(j, j ^ at) for j in range(seq_n)]))
    direct = lax.optimization_barrier(jnp.concatenate(direct, axis=0))
    swapped = swap(direct, "tp", 0)
    starts = [
        (seq_i ^ at) * rows_p + part * half for part in (tp_i, 1 - tp_i) for at in range(1, seq_n)
    ]
    inside = jnp.arange(half, dtype=jnp.int32)
    limit = prompt_len[0, 0]

    def bias_of(place):
        bias = jnp.where(place < limit, 0.0, hidden_value).astype(F32)
        return jnp.broadcast_to(bias[:, None], (place.shape[0], LANES))

    bias_far = bias_of((jnp.stack(starts)[:, None] + inside[None, :]).reshape(-1))
    away_rows = (seq_n - 1) * half
    bias_own = bias_of(seq_i * rows_p + jnp.arange(rows_p, dtype=jnp.int32))

    def project(rows):
        tokens = rows.astype(F32)
        normed, inv = norm_parts(tokens)
        return tokens, normed, inv, (normed * gains[0] + shifts[0]).astype(BF)

    def qkv(low, first):
        return jnp.einsum(
            "nd,cde->cne", low, qkv_weight[first:], preferred_element_type=F32
        ).astype(BF)

    tokens_c, one_c, inv_c, low_c = project(cont_in[0, 0])
    tokens_p, one_p, inv_p, low_p = project(prompt_in[0])
    own_c = qkv(low_c, 0)
    own_p = qkv(low_p, 0)
    part_p, stat_p, part_c, stat_c = attend_near(own_p, own_c, bias_own)
    _, one_a, _, low_a = project(after(direct, part_c))
    far_a = qkv(low_a, 1)
    part_p, stat_p, part_c, stat_c = attend_middle(
        own_p, own_c, far_a, bias_far[:away_rows], part_p, stat_p, part_c, stat_c
    )
    _, one_b, _, low_b = project(after(swapped, part_c))
    far_b = qkv(low_b, 1)

    att_c, log_c = attend_far(own_c, far_b, bias_far[away_rows:], part_c, stat_c)
    mixed_c = wide_dot(att_c, out_weight).astype(BF)
    att_p, log_p = attend_far(own_p, far_b, None, after(part_p, mixed_c), stat_p)
    mixed_p = wide_dot(att_p, out_weight).astype(BF)
    cot_c = cont_cot[0, 0]
    cot_p = prompt_cot[0]
    mixed_other_c = swap(mixed_c, "tp", 0)
    mixed_other_p = swap(mixed_p, "tp", 0)
    held = [far_a, far_b, low_a, low_b, cot_c, cot_p]
    far_a, far_b, low_a, low_b, early_c, early_p = all_after(held, mixed_p)
    far = jnp.concatenate([far_a, far_b], axis=1)
    low_f = jnp.concatenate([low_a, low_b], axis=0)
    act_grad_c = back_dot(early_c, ffn_out)
    act_grad_p = back_dot(early_p, ffn_out)
    held = [mixed_other_c, far, low_f, act_grad_c, act_grad_p, bias_far]
    mixed_other_c, far, low_f, act_grad_c, act_grad_p, bias_far = all_after(held)

    def feed(tokens, mixed, mixed_other, act_grad):
        resid = tokens + (mixed.astype(F32) + mixed_other.astype(F32))
        normed, inv = norm_parts(resid)
        low = (normed * gains[1] + shifts[1]).astype(BF)
        upper = wide_dot(low, ffn_in)
        activated, slope = gelu_parts(upper)
        upper_grad = (act_grad * slope).astype(BF)
        terms = back_dot(upper_grad, ffn_in).astype(BF)
        return resid, normed, inv, low, activated.astype(BF), upper_grad, terms

    resid_c, two_c, inv_two_c, mid_c, act_c, up_c, terms_two_c = feed(
        tokens_c, mixed_c, mixed_other_c, act_grad_c
    )
    resid_p, two_p, inv_two_p, mid_p, act_p, up_p, terms_two_p = feed(
        after(tokens_p, terms_two_c), mixed_p, mixed_other_p, act_grad_p
    )
    second_other = swap(terms_two_c, "tp", 0)
    second_other_p = swap(terms_two_p, "tp", 0)

    def joined(first, second):
        return jnp.concatenate([first, second], axis=0)

    in_grad = rows_dot(joined(mid_p, mid_c), joined(up_p, up_c)).astype(BF)
    down_grad = rows_dot(joined(cot_p, cot_c), joined(act_p, act_c)).astype(BF)
    in_grad = after(in_grad, second_other, terms_two_p)
    ffn_grad = cut(jnp.stack([in_grad, down_grad]))
    ffn_part = add_low(halve(ffn_grad, "grp", 0, seq_bits + 1))
    second_other = after(second_other, ffn_part)

    def rest(cot, normed, inv, second):
        grad = cot.astype(F32) + norm_back(normed, inv, second, gains[1])
        low = grad.astype(BF)
        return grad, low, back_dot(low, out_weight).astype(BF)

    second_c = terms_two_c.astype(F32) + second_other.astype(F32)
    grad_c, dm_c, do_c = rest(cot_c, two_c, inv_two_c, second_c)
    for bit in range(1, grp_bits):
        ffn_pair = halve(ffn_part, "grp", bit, seq_bits + 1)
        if bit + 1 < grp_bits:
            ffn_part = add_low(ffn_pair)
    dq_c, partial = pull_far(own_c, far, bias_far, do_c, att_c, log_c, None, rows_p)
    second_p = terms_two_p.astype(F32) + after(second_other_p, dq_c).astype(F32)
    second_p = lax.optimization_barrier(second_p)
    ffn_pair = all_after(ffn_pair, second_p)
    ffn_part = add_low(ffn_pair)
    grad_p, dm_p, do_p = rest(cot_p, two_p, inv_two_p, second_p)
    for bit in range(seq_bits - 1):
        ffn_pair = halve(ffn_part, "seq", bit, seq_bits - bit)
        if bit + 2 < seq_bits:
            ffn_part = add_low(ffn_pair)
    out_terms_c = wide_dot(after(act_c, dq_c), ffn_out).astype(BF)
    out_other_c = swap(out_terms_c, "tp", 0)
    dq_p, dkv_f = pull_far(
        own_p, far, None, after(do_p, out_terms_c), att_p, log_p, partial, rows_p
    )

    def kv_terms(grads, weights):
        return jnp.einsum("cne,cde->nd", grads, weights, preferred_element_type=F32)

    terms_f = kv_terms(dkv_f, qkv_weight[1:])
    gain_f = jnp.sum(terms_f[:away_rows] * one_a, axis=0)
    gain_f += jnp.sum(terms_f[away_rows:] * one_b, axis=0)
    shift_f = jnp.sum(terms_f, axis=0)
    terms_f = lax.optimization_barrier(terms_f.astype(BF))
    swapped = swap(terms_f[away_rows:], "tp", 0)
    ffn_pair = all_after(ffn_pair, dkv_f)
    out_other_c = after(out_other_c, dkv_f)
    dq_p = after(dq_p, terms_f, out_other_c, *ffn_pair)
    ffn_part = add_low(ffn_pair)
    ffn_pair = halve(ffn_part, "seq", seq_bits - 1, 1)
    own_grads = pull_near(
        own_p, own_c, bias_own, (do_p, att_p, log_p, dq_p), (do_c, att_c, log_c, dq_c)
    )
    swapped, *ffn_pair, own_grads = all_after([swapped, *ffn_pair, own_grads])
    ffn_mine = lax.optimization_barrier(add_low(ffn_pair))
    for bit in reversed(range(1, grp_bits)):
        ffn_mine = lax.optimization_barrier(double(ffn_mine, "grp", bit, 1))
    low_pc = joined(low_p, low_c)
    last_grads = [rows_dot(low_pc, own_grads[0])]
    for c in range(2):
        last_grads.append(rows_dot(low_pc, own_grads[1 + c]) + rows_dot(low_f, dkv_f[c]))
    mixing_grad = rows_dot(joined(dm_p, dm_c), joined(att_p, att_c))
    last_cut = [cut(grad.astype(BF)[None]) for grad in last_grads + [mixing_grad]]
    core_i = own_bit("grp", 0)

    def core_half(which):
        return jnp.concatenate(
            [lax.dynamic_index_in_dim(g, which, seq_bits + 1, keepdims=False) for g in last_cut]
        )

    sent = lax.optimization_barrier(core_half(1 - core_i))
    last_core = add_low((core_half(core_i), swap(sent, "grp", 0)))
    ffn_mine = after(ffn_mine, sent)
    ffn_other = swap(ffn_mine, "grp", 0)
    out_other_c = after(out_other_c, last_core)
    out_c = out_terms_c.astype(F32) + out_other_c.astype(F32)
    cont_out = (resid_c + out_c).astype(BF)[None, None]
    last_part = last_core
    for bit in range(1, grp_bits):
        last_pair = halve(last_part, "grp", bit, seq_bits + 1)
        if bit + 1 < grp_bits:
            last_part = add_low(last_pair)

    terms = kv_terms(after(own_grads, sent), qkv_weight)
    terms_p, terms_c = terms[:rows_p], terms[rows_p:]
    gain_one = gain_f + jnp.sum(terms * joined(one_p, one_c), axis=0)
    shift_one = shift_f + jnp.sum(terms, axis=0)
    both = add_low((terms_f[:away_rows], swapped)).reshape(seq_n - 1, half, width)
    blocks = {at: both[at - 1] for at in range(1, seq_n)}
    for bit in range(seq_bits):
        away = [name for name in sorted(blocks) if name >> bit & 1]
        came = swap(jnp.stack([blocks.pop(name) for name in away]), "seq", bit)
        if bit == 0:
            came = after(came, last_core)
        for i, name in enumerate(away):
            near = name ^ (1 << bit)
            blocks[near] = came[i] if near not in blocks else add_low((blocks[near], came[i]))
    halves_p = lax.optimization_barrier(terms_p.astype(BF)).reshape(2, half, width)
    mine_p, other_p = halve(halves_p, "tp", 0, 0)
    two = (terms_two_c.astype(F32), terms_two_p.astype(F32))
    norm_rows = jnp.stack(
        [
            gain_one,
            jnp.sum(two[0] * two_c, axis=0) + jnp.sum(two[1] * two_p, axis=0),
            shift_one,
            jnp.sum(two[0], axis=0) + jnp.sum(two[1], axis=0),
        ]
    )
    low_norm = jnp.pad(norm_rows.astype(BF), ((0, 12), (0, 0)))
    low_terms_c = lax.optimization_barrier(joined(terms_c.astype(BF), low_norm))
    other_c = swap(low_terms_c, "tp", 0)

    last_pair = all_after(last_pair, cont_out)
    last_part = add_low(last_pair)
    late = [other_p, other_c, blocks[0], ffn_mine, ffn_other]
    other_p, other_c, home, ffn_mine, ffn_other = all_after(late, last_part)
    first = core_i == 0
    ffn_sum = jnp.concatenate(
        [jnp.where(first, ffn_mine, ffn_other), jnp.where(first, ffn_other, ffn_mine)], axis=1
    ).astype(F32)
    ffn_sums = lax.optimization_barrier((ffn_sum[0], ffn_sum[1].T))
    norm_rows = norm_rows + other_c[rows_c : rows_c + 4].astype(F32)
    norm_cut = norm_rows.reshape(4, seq_n, tp_n, -1)
    norm_cut = lax.dynamic_index_in_dim(norm_cut, tp_i, 2, keepdims=False)
    columns = norm_cut.shape[2]
    norm_cut = norm_cut.transpose(1, 0, 2).reshape(seq_n, -1)
    norm_pad = jnp.pad(norm_cut, ((0, 0), (0, 16 * local_width - norm_cut.shape[1])))
    norm_pad = norm_pad.astype(BF).reshape(seq_n, 16, local_width)
    slab_rows = last_part.shape[0] * last_part.shape[-2]
    last_part = last_part.reshape(last_part.shape[0], seq_n, -1, local_width)

    def block(at):
        slabs = lax.dynamic_index_in_dim(last_part, at, 1, keepdims=False)
        norms = lax.dynamic_index_in_dim(norm_pad, at, 0, keepdims=False)
        return jnp.concatenate([slabs.reshape(slab_rows, local_width), norms])

    last_pieces = [block(seq_i)] + [
        lax.ppermute(block(seq_i ^ at), "seq", [(j, j ^ at) for j in range(seq_n)])
        for at in range(1, seq_n)
    ]

    first_p = mine_p.astype(F32) + other_p.astype(F32) + home.astype(F32)
    first_p = lax.optimization_barrier(first_p.astype(BF))
    gathered_p = swap(first_p, "tp", 0)
    first_c = low_terms_c[:rows_c].astype(F32) + other_c[:rows_c].astype(F32)
    out_terms_p = lax.optimization_barrier(wide_dot(after(act_p, first_p), ffn_out).astype(BF))
    out_other_p = swap(out_terms_p, "tp", 0)

    last_pieces = all_after(last_pieces, *ffn_sums)
    last_mine = sum(piece.astype(F32) for piece in last_pieces).astype(BF)
    gathered_p, out_other_p = all_after([gathered_p, out_other_p], last_mine)
    first = tp_i == 0
    first_p = jnp.concatenate(
        [jnp.where(first, first_p, gathered_p), jnp.where(first, gathered_p, first_p)]
    ).astype(F32)
    out_p = out_terms_p.astype(F32) + out_other_p.astype(F32)
    prompt_out = (resid_p + out_p).astype(BF)[None]
    cont_grad = (grad_c + norm_back(one_c, inv_c, first_c, gains[0])).astype(BF)[None, None]
    prompt_grad = (grad_p + norm_back(one_p, inv_p, first_p, gains[0])).astype(BF)[None]
    last_sum, norm_sum = gather_last(last_mine, slab_rows, last_part.shape[0], (prompt_grad, cont_grad))
    norm_sum = norm_sum.reshape(-1)[: 4 * columns].reshape(4, columns)
    return (
        prompt_out,
        cont_out,
        prompt_grad,
        cont_grad,
        last_sum[:3],
        last_sum[3].T,
        *ffn_sums,
        norm_sum[:2],
        norm_sum[2:],
    )


def solution(mesh):
    placed = (
        P("grp", "seq", None),
        P("grp", "seq", None, None),
        P("grp", "seq", None),
        P("grp", "seq", None, None),
        P("grp", "seq"),
        P(None, None, "tp"),
        P("tp", None),
        P(None, "tp"),
        P("tp", None),
        P(),
        P(),
    )
    return jax.shard_map(
        body,
        mesh=mesh,
        in_specs=placed,
        out_specs=(
            P("grp", "seq", None),
            P("grp", "seq", None, None),
            P("grp", "seq", None),
            P("grp", "seq", None, None),
            P(None, "seq", "tp"),
            P("tp", "seq"),
            P("seq", "tp"),
            P("tp", "seq"),
            P(None, ("seq", "tp")),
            P(None, ("seq", "tp")),
        ),
        check_vma=False,
    )
```

```python
import functools

import jax
import jax.numpy as jnp
from jax import lax
from jax.experimental import pallas as pl
from jax.experimental.pallas import tpu as pltpu
from jax.sharding import PartitionSpec as P

HEAD = 64
CORES = 2
LANES = 128
norm_eps = 1e-05
hidden_value = -1e30
BF = jnp.bfloat16
F32 = jnp.float32
BUDGET = 56 * 1024 * 1024


def nt(left, right):
    return lax.dot_general(left, right, (((1,), (1,)), ((), ())), preferred_element_type=F32)


def tn(left, right):
    return lax.dot_general(left, right, (((0,), (0,)), ((), ())), preferred_element_type=F32)


def nn(left, right):
    return lax.dot_general(left, right, (((1,), (0,)), ((), ())), preferred_element_type=F32)


def one_head(pair, which, factor=None):
    lane = lax.broadcasted_iota(jnp.int32, pair.shape, 1)
    wide = pair.astype(F32)
    if factor is not None:
        wide = wide * factor
    return jnp.where((lane // HEAD) == which, wide, 0.0).astype(BF)


def lane_pair(pair):
    lane = lax.broadcasted_iota(jnp.int32, pair[0].shape, 1)
    return jnp.where(lane < HEAD, pair[0], pair[1])


def row_pair(pair):
    rows = pair[0].shape[1]
    return jnp.transpose(
        jnp.concatenate([jnp.broadcast_to(one, (HEAD, rows)) for one in pair], axis=0)
    )


def masked_scores(keys, mine, bias):
    scores = nt(keys, mine)
    if bias is None:
        return scores
    return scores + jnp.concatenate([bias] * (mine.shape[0] // LANES), axis=1)


def near_kernel(qp_ref, kp_ref, vp_ref, qc_ref, kc_ref, vc_ref, bias_ref, op_ref, sp_ref, oc_ref, sc_ref):
    parts = (
        (qp_ref, op_ref, sp_ref, [(kp_ref, vp_ref, None)]),
        (qc_ref, oc_ref, sc_ref, [(kp_ref, vp_ref, bias_ref), (kc_ref, vc_ref, None)]),
    )
    for q_ref, out_ref, stat_ref, sources in parts:
        outs = []
        for which in range(2):
            mine = one_head(q_ref[0], which, HEAD ** (-0.5))
            scores = [
                masked_scores(k_ref[0], mine, None if b_ref is None else b_ref[...])
                for k_ref, _, b_ref in sources
            ]
            top = functools.reduce(
                jnp.maximum, [jnp.max(s, axis=0, keepdims=True) for s in scores]
            )
            weights = [jnp.exp(s - top) for s in scores]
            stat_ref[0, which : which + 1] = top
            stat_ref[0, 2 + which : 3 + which] = sum(
                jnp.sum(w, axis=0, keepdims=True) for w in weights
            )
            outs.append(sum(tn(w.astype(BF), v_ref[0]) for w, (_, v_ref, _) in zip(weights, sources)))
        out_ref[...] = lane_pair(outs)


def kind_spec(array, kind):
    return pl.BlockSpec((1, array.shape[1], LANES), lambda p: (kind, 0, p))


def full_spec(rows):
    return pl.BlockSpec((rows, LANES), lambda p: (0, p))


def slab_spec(count, rows):
    return pl.BlockSpec((count, rows, LANES), lambda p: (0, 0, p))


def stat_spec(rows):
    return pl.BlockSpec((1, 8, rows), lambda p: (p, 0, 0))


def bias_spec(bias):
    return pl.BlockSpec(bias.shape, lambda p: (0, 0))


def params():
    return pltpu.CompilerParams(vmem_limit_bytes=BUDGET)


def cost(matmuls, pairs, width, moved):
    return pl.CostEstimate(flops=matmuls * pairs, transcendentals=0, bytes_accessed=moved)


def attend_near(own_p, own_c, bias):
    width = own_p.shape[2]
    outs = []
    for own in (own_p, own_c):
        rows = own.shape[1]
        outs += [
            jax.ShapeDtypeStruct((rows, width), F32),
            jax.ShapeDtypeStruct((width // LANES, 8, rows), F32),
        ]
    rows_p, rows_c = own_p.shape[1], own_c.shape[1]
    return pl.pallas_call(
        near_kernel,
        grid=(width // LANES,),
        in_specs=[kind_spec(own_p, c) for c in range(3)]
        + [kind_spec(own_c, c) for c in range(3)]
        + [bias_spec(bias)],
        out_specs=[full_spec(rows_p), stat_spec(rows_p), full_spec(rows_c), stat_spec(rows_c)],
        out_shape=outs,
        compiler_params=params(),
        cost_estimate=cost(2, rows_p * rows_p + rows_c * (rows_p + rows_c), width, 10 * rows_c),
    )(own_p, own_p, own_p, own_c, own_c, own_c, bias)


def middle_kernel(
    k_ref, v_ref, bias_ref, qp_ref, partp_ref, statp_ref, qc_ref, partc_ref, statc_ref,
    outp_ref, newp_ref, outc_ref, newc_ref,
):
    parts = (
        (qp_ref, None, partp_ref, statp_ref, outp_ref, newp_ref),
        (qc_ref, bias_ref, partc_ref, statc_ref, outc_ref, newc_ref),
    )
    for q_ref, b_ref, part_ref, stat_ref, out_ref, new_ref in parts:
        outs = []
        shrinks = []
        for which in range(2):
            mine = one_head(q_ref[0], which, HEAD ** (-0.5))
            scores = masked_scores(k_ref[0], mine, None if b_ref is None else b_ref[...])
            old = stat_ref[0, which : which + 1]
            top = jnp.maximum(old, jnp.max(scores, axis=0, keepdims=True))
            weights = jnp.exp(scores - top)
            shrink = jnp.exp(old - top)
            new_ref[0, which : which + 1] = top
            new_ref[0, 2 + which : 3 + which] = shrink * stat_ref[
                0, 2 + which : 3 + which
            ] + jnp.sum(weights, axis=0, keepdims=True)
            outs.append(tn(weights.astype(BF), v_ref[0]))
            shrinks.append(shrink)
        out_ref[...] = lane_pair(outs) + part_ref[...] * row_pair(shrinks)


def attend_middle(own_p, own_c, far, bias, part_p, stat_p, part_c, stat_c):
    width = own_p.shape[2]
    specs = [kind_spec(far, 0), kind_spec(far, 1), bias_spec(bias)]
    out_specs = []
    outs = []
    for own in (own_p, own_c):
        rows = own.shape[1]
        specs += [kind_spec(own, 0), full_spec(rows), stat_spec(rows)]
        out_specs += [full_spec(rows), stat_spec(rows)]
        outs += [
            jax.ShapeDtypeStruct((rows, width), F32),
            jax.ShapeDtypeStruct((width // LANES, 8, rows), F32),
        ]
    rows = own_p.shape[1] + own_c.shape[1]
    return pl.pallas_call(
        middle_kernel,
        grid=(width // LANES,),
        in_specs=specs,
        out_specs=out_specs,
        out_shape=outs,
        compiler_params=params(),
        cost_estimate=cost(2, rows * far.shape[1], width, 4 * far.shape[1]),
    )(far, far, bias, own_p, part_p, stat_p, own_c, part_c, stat_c)


def far_kernel(*refs, masked):
    if masked:
        q_ref, k_ref, v_ref, bias_ref, part_ref, stat_ref, out_ref, log_ref = refs
    else:
        q_ref, k_ref, v_ref, part_ref, stat_ref, out_ref, log_ref = refs
    outs = []
    olds = []
    news = []
    for which in range(2):
        mine = one_head(q_ref[0], which, HEAD ** (-0.5))
        scores = masked_scores(k_ref[0], mine, bias_ref[...] if masked else None)
        old = stat_ref[0, which : which + 1]
        top = jnp.maximum(old, jnp.max(scores, axis=0, keepdims=True))
        weights = jnp.exp(scores - top)
        shrink = jnp.exp(old - top)
        total = shrink * stat_ref[0, 2 + which : 3 + which] + jnp.sum(
            weights, axis=0, keepdims=True
        )
        outs.append(tn(weights.astype(BF), v_ref[0]))
        olds.append(shrink / total)
        news.append(1.0 / total)
        log_ref[0, which : which + 1] = top + jnp.log(total)
    out = lane_pair(outs) * row_pair(news) + part_ref[...] * row_pair(olds)
    out_ref[...] = out.astype(BF)


def attend_far(own, far, bias, part, stat):
    masked = bias is not None
    rows = own.shape[1]
    width = own.shape[2]
    specs = [kind_spec(own, 0), kind_spec(far, 0), kind_spec(far, 1)]
    args = [own, far, far]
    if masked:
        specs.append(bias_spec(bias))
        args.append(bias)
    return pl.pallas_call(
        functools.partial(far_kernel, masked=masked),
        grid=(width // LANES,),
        in_specs=specs + [full_spec(rows), stat_spec(rows)],
        out_specs=[full_spec(rows), stat_spec(rows)],
        out_shape=[
            jax.ShapeDtypeStruct((rows, width), BF),
            jax.ShapeDtypeStruct((width // LANES, 8, rows), F32),
        ],
        compiler_params=params(),
        cost_estimate=cost(2, rows * far.shape[1], width, 4 * far.shape[1]),
    )(*args, part, stat)


def pull_heads(q_ref, do_ref, out_ref, log_ref):
    upstream = do_ref[...]
    inner = jnp.transpose(upstream.astype(F32) * out_ref[...].astype(F32))
    return [
        (
            one_head(q_ref[0], which, HEAD ** (-0.5)),
            one_head(upstream, which),
            jnp.sum(inner[which * HEAD : (which + 1) * HEAD], axis=0, keepdims=True),
            log_ref[0, which : which + 1],
        )
        for which in range(2)
    ]


def pull_piece(keys, values, bias, heads):
    key_grads = []
    value_grads = []
    query_grads = []
    for mine, grad, delta, log in heads:
        probs = jnp.exp(masked_scores(keys, mine, bias) - log)
        spread = probs * (nt(values, grad) - delta)
        low = spread.astype(BF)
        value_grads.append(nn(probs.astype(BF), grad))
        key_grads.append(nn(low, mine))
        query_grads.append(tn(low, keys))
    return key_grads[0] + key_grads[1], value_grads[0] + value_grads[1], query_grads


def pull_far_kernel(*refs, masked, chunk):
    if masked:
        q_ref, k_ref, v_ref, bias_ref, do_ref, out_ref, log_ref, dq_ref, dkv_ref = refs
    else:
        q_ref, k_ref, v_ref, do_ref, out_ref, log_ref, old_ref, dq_ref, dkv_ref = refs
    heads = pull_heads(q_ref, do_ref, out_ref, log_ref)

    def step(at, acc):
        span = pl.ds(at, chunk)
        bias = bias_ref[span] if masked else None
        dk, dv, more = pull_piece(k_ref[0, span], v_ref[0, span], bias, heads)
        if not masked:
            dk += old_ref[0, span]
            dv += old_ref[1, span]
        dkv_ref[0, span] = dk.astype(dkv_ref.dtype)
        dkv_ref[1, span] = dv.astype(dkv_ref.dtype)
        return more if acc is None else [a + b for a, b in zip(acc, more)]

    acc = step(0, None)
    count = k_ref.shape[1] // chunk
    if count <= 4:
        for i in range(1, count):
            acc = step(i * chunk, acc)
    else:
        acc = lax.fori_loop(
            1, count, lambda i, a: step(pl.multiple_of(i * chunk, chunk), a), acc
        )
    dq_ref[...] = lane_pair(acc) * HEAD ** (-0.5)


def pull_far(own, far, bias, grad, out, log, before, chunk):
    masked = bias is not None
    rows = own.shape[1]
    width = own.shape[2]
    keys = far.shape[1]
    specs = [kind_spec(own, 0), kind_spec(far, 0), kind_spec(far, 1)]
    args = [own, far, far]
    if masked:
        specs.append(bias_spec(bias))
        args.append(bias)
    specs += [full_spec(rows), full_spec(rows), stat_spec(rows)]
    args += [grad, out, log]
    if not masked:
        specs.append(slab_spec(2, keys))
        args.append(before)
    kind = F32 if masked else BF
    return pl.pallas_call(
        functools.partial(pull_far_kernel, masked=masked, chunk=chunk),
        grid=(width // LANES,),
        in_specs=specs,
        out_specs=[full_spec(rows), slab_spec(2, keys)],
        out_shape=[
            jax.ShapeDtypeStruct((rows, width), F32),
            jax.ShapeDtypeStruct((2, keys, width), kind),
        ],
        compiler_params=params(),
        cost_estimate=cost(5, rows * keys, width, 8 * keys),
    )(*args)


def pull_near_kernel(
    qp_ref, kp_ref, vp_ref, qc_ref, kc_ref, vc_ref, bias_ref,
    dop_ref, outp_ref, logp_ref, oldp_ref, doc_ref, outc_ref, logc_ref, oldc_ref,
    grad_ref,
):
    heads_p = pull_heads(qp_ref, dop_ref, outp_ref, logp_ref)
    heads_c = pull_heads(qc_ref, doc_ref, outc_ref, logc_ref)
    dk_p, dv_p, dq_p = pull_piece(kp_ref[0], vp_ref[0], None, heads_p)
    dk_pc, dv_pc, dq_pc = pull_piece(kp_ref[0], vp_ref[0], bias_ref[...], heads_c)
    dk_c, dv_c, dq_c = pull_piece(kc_ref[0], vc_ref[0], None, heads_c)
    split = qp_ref.shape[1]
    both = [a + b for a, b in zip(dq_pc, dq_c)]
    grad_ref[0, :split] = (lane_pair(dq_p) * HEAD ** (-0.5) + oldp_ref[...]).astype(BF)
    grad_ref[1, :split] = (dk_p + dk_pc).astype(BF)
    grad_ref[2, :split] = (dv_p + dv_pc).astype(BF)
    grad_ref[0, split:] = (lane_pair(both) * HEAD ** (-0.5) + oldc_ref[...]).astype(BF)
    grad_ref[1, split:] = dk_c.astype(BF)
    grad_ref[2, split:] = dv_c.astype(BF)


def pull_near(own_p, own_c, bias, part_p, part_c):
    width = own_p.shape[2]
    rows_p, rows_c = own_p.shape[1], own_c.shape[1]
    specs = [kind_spec(own_p, c) for c in range(3)] + [kind_spec(own_c, c) for c in range(3)]
    specs.append(bias_spec(bias))
    for rows in (rows_p, rows_c):
        specs += [full_spec(rows), full_spec(rows), stat_spec(rows), full_spec(rows)]
    return pl.pallas_call(
        pull_near_kernel,
        grid=(width // LANES,),
        in_specs=specs,
        out_specs=slab_spec(3, rows_p + rows_c),
        out_shape=jax.ShapeDtypeStruct((3, rows_p + rows_c, width), BF),
        compiler_params=params(),
        cost_estimate=cost(5, rows_p * rows_p + rows_c * (rows_p + rows_c), width, 10 * rows_c),
    )(own_p, own_p, own_p, own_c, own_c, own_c, bias, *part_p, *part_c)


def swap(array, axis, bit):
    count = lax.axis_size(axis)
    return lax.ppermute(array, axis, [(j, j ^ (1 << bit)) for j in range(count)])


def own_bit(axis, bit):
    return lax.axis_index(axis) // (1 << bit) % 2


def bits_of(count):
    return count.bit_length() - 1


def halve(part, axis, bit, dim):
    mine = own_bit(axis, bit)
    sent = lax.dynamic_index_in_dim(part, 1 - mine, dim, keepdims=False)
    kept = lax.dynamic_index_in_dim(part, mine, dim, keepdims=False)
    return kept, swap(sent, axis, bit)


def add_low(pair):
    return (pair[0].astype(F32) + pair[1].astype(F32)).astype(BF)


def double(mine, axis, bit, dim):
    other = swap(mine, axis, bit)
    first = own_bit(axis, bit) == 0
    return jnp.concatenate([jnp.where(first, mine, other), jnp.where(first, other, mine)], axis=dim)


def after(value, *earlier):
    return lax.optimization_barrier((value,) + earlier)[0]


def all_after(values, *earlier):
    return list(lax.optimization_barrier(tuple(values) + earlier)[: len(values)])


def tp_sum(low):
    return low.astype(F32) + swap(low, "tp", 0).astype(F32)


def wide_dot(left, right):
    return jnp.dot(left, right, preferred_element_type=F32)


def back_dot(left, right):
    return jnp.einsum("ne,de->nd", left, right, preferred_element_type=F32)


def rows_dot(left, right):
    return jnp.einsum("nd,nf->df", left, right, preferred_element_type=F32)


def cut(slabs):
    seq_bits = bits_of(lax.axis_size("seq"))
    grp_bits = bits_of(lax.axis_size("grp"))
    return slabs.reshape(
        (slabs.shape[0],) + (2,) * (seq_bits + grp_bits) + (-1, slabs.shape[2])
    )


def gather_group(mine):
    for bit in reversed(range(1, bits_of(lax.axis_size("grp")))):
        mine = double(lax.optimization_barrier(mine), "grp", bit, 1)
    return double(lax.optimization_barrier(mine), "grp", 0, 1)


def gather_last(mine, slab_rows, slabs, hold):
    grp_n = lax.axis_size("grp")
    mine = lax.optimization_barrier(mine)

    def slabs_of(rows):
        return rows[:slab_rows].reshape(slabs, -1, rows.shape[1])

    if grp_n != 2 * CORES:
        total = mine[slab_rows:].astype(F32)
        for bit in range(bits_of(grp_n)):
            total = total + swap(total, "grp", bit)
        return gather_group(slabs_of(mine)).astype(F32), total
    came = [mine] + [
        lax.ppermute(mine, "grp", [(j, j ^ at) for j in range(grp_n)]) for at in range(1, grp_n)
    ]
    came = all_after(came, *hold)
    total = sum(rows[slab_rows:].astype(F32) for rows in came)
    came = [slabs_of(rows) for rows in came]
    swapped_core = lax.axis_index("grp") % CORES == 1
    swapped_chip = lax.axis_index("grp") // CORES == 1
    came = [jnp.where(swapped_core, came[at ^ 1], came[at]) for at in range(grp_n)]
    came = [jnp.where(swapped_chip, came[at ^ 2], came[at]) for at in range(grp_n)]
    return jnp.concatenate([came[0], came[2], came[1], came[3]], axis=1).astype(F32), total


def norm_parts(tokens):
    mean = jnp.mean(tokens, axis=-1, keepdims=True)
    centred = tokens - mean
    variance = jnp.mean(centred * centred, axis=-1, keepdims=True)
    inv = lax.rsqrt(variance + norm_eps)
    return centred * inv, inv


def norm_back(normed, inv, upstream, gain):
    scaled = upstream * gain
    mean = jnp.mean(scaled, axis=-1, keepdims=True)
    inner = jnp.mean(scaled * normed, axis=-1, keepdims=True)
    return inv * (scaled - mean - normed * inner)


def gelu_parts(upper):
    half = 0.5 + 0.5 * lax.erf(upper * 0.5**0.5)
    bell = jnp.exp(-0.5 * upper * upper) * (2.0 * jnp.pi) ** -0.5
    return upper * half, half + upper * bell


def body(
    prompt_in,
    cont_in,
    prompt_cot,
    cont_cot,
    prompt_len,
    qkv_weight,
    out_weight,
    ffn_in,
    ffn_out,
    norm_gain,
    norm_shift,
):
    rows_p = prompt_in.shape[1]
    rows_c = cont_in.shape[2]
    half = rows_p // 2
    width = prompt_in.shape[2]
    local_width = qkv_weight.shape[2]
    seq_n = lax.axis_size("seq")
    seq_i = lax.axis_index("seq")
    tp_n = lax.axis_size("tp")
    tp_i = lax.axis_index("tp")
    grp_n = lax.axis_size("grp")
    gains = norm_gain.astype(F32)
    shifts = norm_shift.astype(F32)

    seq_bits = bits_of(seq_n)
    grp_bits = bits_of(grp_n)
    held = lax.dynamic_slice_in_dim(prompt_in[0], tp_i * half, half, 0)
    direct = []
    for at in range(1, seq_n):
        direct.append(lax.ppermute(held, "seq", [(j, j ^ at) for j in range(seq_n)]))
    direct = lax.optimization_barrier(jnp.concatenate(direct, axis=0))
    swapped = swap(direct, "tp", 0)
    starts = [
        (seq_i ^ at) * rows_p + part * half for part in (tp_i, 1 - tp_i) for at in range(1, seq_n)
    ]
    inside = jnp.arange(half, dtype=jnp.int32)
    limit = prompt_len[0, 0]

    def bias_of(place):
        bias = jnp.where(place < limit, 0.0, hidden_value).astype(F32)
        return jnp.broadcast_to(bias[:, None], (place.shape[0], LANES))

    bias_far = bias_of((jnp.stack(starts)[:, None] + inside[None, :]).reshape(-1))
    away_rows = (seq_n - 1) * half
    bias_own = bias_of(seq_i * rows_p + jnp.arange(rows_p, dtype=jnp.int32))

    def project(rows):
        tokens = rows.astype(F32)
        normed, inv = norm_parts(tokens)
        return tokens, normed, inv, (normed * gains[0] + shifts[0]).astype(BF)

    def qkv(low, first):
        return jnp.einsum(
            "nd,cde->cne", low, qkv_weight[first:], preferred_element_type=F32
        ).astype(BF)

    tokens_c, one_c, inv_c, low_c = project(cont_in[0, 0])
    tokens_p, one_p, inv_p, low_p = project(prompt_in[0])
    own_c = qkv(low_c, 0)
    own_p = qkv(low_p, 0)
    part_p, stat_p, part_c, stat_c = attend_near(own_p, own_c, bias_own)
    _, one_a, _, low_a = project(after(direct, part_c))
    far_a = qkv(low_a, 1)
    part_p, stat_p, part_c, stat_c = attend_middle(
        own_p, own_c, far_a, bias_far[:away_rows], part_p, stat_p, part_c, stat_c
    )
    _, one_b, _, low_b = project(after(swapped, part_c))
    far_b = qkv(low_b, 1)

    att_c, log_c = attend_far(own_c, far_b, bias_far[away_rows:], part_c, stat_c)
    mixed_c = wide_dot(att_c, out_weight).astype(BF)
    att_p, log_p = attend_far(own_p, far_b, None, after(part_p, mixed_c), stat_p)
    mixed_p = wide_dot(att_p, out_weight).astype(BF)
    cot_c = cont_cot[0, 0]
    cot_p = prompt_cot[0]
    mixed_other_c = swap(mixed_c, "tp", 0)
    mixed_other_p = swap(mixed_p, "tp", 0)
    held = [far_a, far_b, low_a, low_b, cot_c, cot_p]
    far_a, far_b, low_a, low_b, early_c, early_p = all_after(held, mixed_p)
    far = jnp.concatenate([far_a, far_b], axis=1)
    low_f = jnp.concatenate([low_a, low_b], axis=0)
    act_grad_c = back_dot(early_c, ffn_out)
    act_grad_p = back_dot(early_p, ffn_out)
    held = [mixed_other_c, far, low_f, act_grad_c, act_grad_p, bias_far]
    mixed_other_c, far, low_f, act_grad_c, act_grad_p, bias_far = all_after(held)

    def feed(tokens, mixed, mixed_other, act_grad):
        resid = tokens + (mixed.astype(F32) + mixed_other.astype(F32))
        normed, inv = norm_parts(resid)
        low = (normed * gains[1] + shifts[1]).astype(BF)
        upper = wide_dot(low, ffn_in)
        activated, slope = gelu_parts(upper)
        upper_grad = (act_grad * slope).astype(BF)
        terms = back_dot(upper_grad, ffn_in).astype(BF)
        return resid, normed, inv, low, activated.astype(BF), upper_grad, terms

    resid_c, two_c, inv_two_c, mid_c, act_c, up_c, terms_two_c = feed(
        tokens_c, mixed_c, mixed_other_c, act_grad_c
    )
    resid_p, two_p, inv_two_p, mid_p, act_p, up_p, terms_two_p = feed(
        after(tokens_p, terms_two_c), mixed_p, mixed_other_p, act_grad_p
    )
    second_other = swap(terms_two_c, "tp", 0)
    second_other_p = swap(terms_two_p, "tp", 0)

    def joined(first, second):
        return jnp.concatenate([first, second], axis=0)

    in_grad = rows_dot(joined(mid_p, mid_c), joined(up_p, up_c)).astype(BF)
    down_grad = rows_dot(joined(cot_p, cot_c), joined(act_p, act_c)).astype(BF)
    in_grad = after(in_grad, second_other, terms_two_p)
    ffn_grad = cut(jnp.stack([in_grad, down_grad]))
    ffn_part = add_low(halve(ffn_grad, "grp", 0, seq_bits + 1))

    def rest(cot, normed, inv, second):
        grad = cot.astype(F32) + norm_back(normed, inv, second, gains[1])
        low = grad.astype(BF)
        return grad, low, back_dot(low, out_weight).astype(BF)

    second_c = terms_two_c.astype(F32) + second_other.astype(F32)
    second_c = after(second_c, ffn_part)
    grad_c, dm_c, do_c = rest(cot_c, two_c, inv_two_c, second_c)
    for bit in range(1, grp_bits):
        ffn_pair = halve(ffn_part, "grp", bit, seq_bits + 1)
        if bit + 1 < grp_bits:
            ffn_part = add_low(ffn_pair)
    dq_c, partial = pull_far(own_c, far, bias_far, do_c, att_c, log_c, None, rows_p)
    second_p = terms_two_p.astype(F32) + after(second_other_p, dq_c).astype(F32)
    second_p = lax.optimization_barrier(second_p)
    ffn_pair = all_after(ffn_pair, second_p)
    ffn_part = add_low(ffn_pair)
    grad_p, dm_p, do_p = rest(cot_p, two_p, inv_two_p, second_p)
    for bit in range(seq_bits - 1):
        ffn_pair = halve(ffn_part, "seq", bit, seq_bits - bit)
        if bit + 2 < seq_bits:
            ffn_part = add_low(ffn_pair)
    out_terms_c = wide_dot(after(act_c, dq_c), ffn_out).astype(BF)
    out_other_c = swap(out_terms_c, "tp", 0)
    dq_p, dkv_f = pull_far(
        own_p, far, None, after(do_p, out_terms_c), att_p, log_p, partial, rows_p
    )

    def kv_terms(grads, weights):
        return jnp.einsum("cne,cde->nd", grads, weights, preferred_element_type=F32)

    terms_f = kv_terms(dkv_f, qkv_weight[1:])
    gain_f = jnp.sum(terms_f[:away_rows] * one_a, axis=0)
    gain_f += jnp.sum(terms_f[away_rows:] * one_b, axis=0)
    shift_f = jnp.sum(terms_f, axis=0)
    terms_f = lax.optimization_barrier(terms_f.astype(BF))
    swapped = swap(terms_f[away_rows:], "tp", 0)
    ffn_pair = all_after(ffn_pair, dkv_f)
    out_other_c = after(out_other_c, dkv_f)
    dq_p = after(dq_p, terms_f, out_other_c, *ffn_pair)
    ffn_part = add_low(ffn_pair)
    ffn_pair = halve(ffn_part, "seq", seq_bits - 1, 1)
    own_grads = pull_near(
        own_p, own_c, bias_own, (do_p, att_p, log_p, dq_p), (do_c, att_c, log_c, dq_c)
    )
    swapped, *ffn_pair, own_grads = all_after([swapped, *ffn_pair, own_grads])
    ffn_mine = lax.optimization_barrier(add_low(ffn_pair))
    for bit in reversed(range(1, grp_bits)):
        ffn_mine = lax.optimization_barrier(double(ffn_mine, "grp", bit, 1))
    low_pc = joined(low_p, low_c)
    last_grads = [rows_dot(low_pc, own_grads[0])]
    for c in range(2):
        last_grads.append(rows_dot(low_pc, own_grads[1 + c]) + rows_dot(low_f, dkv_f[c]))
    mixing_grad = rows_dot(joined(dm_p, dm_c), joined(att_p, att_c))
    last_cut = [cut(grad.astype(BF)[None]) for grad in last_grads + [mixing_grad]]
    core_i = own_bit("grp", 0)

    def core_half(which):
        return jnp.concatenate(
            [lax.dynamic_index_in_dim(g, which, seq_bits + 1, keepdims=False) for g in last_cut]
        )

    sent = lax.optimization_barrier(core_half(1 - core_i))
    last_core = add_low((core_half(core_i), swap(sent, "grp", 0)))
    ffn_mine = after(ffn_mine, sent)
    ffn_other = swap(ffn_mine, "grp", 0)
    out_other_c = after(out_other_c, last_core)
    out_c = out_terms_c.astype(F32) + out_other_c.astype(F32)
    cont_out = (resid_c + out_c).astype(BF)[None, None]
    last_part = last_core
    for bit in range(1, grp_bits):
        last_pair = halve(last_part, "grp", bit, seq_bits + 1)
        if bit + 1 < grp_bits:
            last_part = add_low(last_pair)

    terms = kv_terms(after(own_grads, sent), qkv_weight)
    terms_p, terms_c = terms[:rows_p], terms[rows_p:]
    gain_one = gain_f + jnp.sum(terms * joined(one_p, one_c), axis=0)
    shift_one = shift_f + jnp.sum(terms, axis=0)
    both = add_low((terms_f[:away_rows], swapped)).reshape(seq_n - 1, half, width)
    blocks = {at: both[at - 1] for at in range(1, seq_n)}
    for bit in range(seq_bits):
        away = [name for name in sorted(blocks) if name >> bit & 1]
        came = swap(jnp.stack([blocks.pop(name) for name in away]), "seq", bit)
        if bit == 0:
            came = after(came, last_core)
        for i, name in enumerate(away):
            near = name ^ (1 << bit)
            blocks[near] = came[i] if near not in blocks else add_low((blocks[near], came[i]))
    halves_p = lax.optimization_barrier(terms_p.astype(BF)).reshape(2, half, width)
    mine_p, other_p = halve(halves_p, "tp", 0, 0)
    two = (terms_two_c.astype(F32), terms_two_p.astype(F32))
    norm_rows = jnp.stack(
        [
            gain_one,
            jnp.sum(two[0] * two_c, axis=0) + jnp.sum(two[1] * two_p, axis=0),
            shift_one,
            jnp.sum(two[0], axis=0) + jnp.sum(two[1], axis=0),
        ]
    )
    low_norm = jnp.pad(norm_rows.astype(BF), ((0, 12), (0, 0)))
    low_terms_c = lax.optimization_barrier(joined(terms_c.astype(BF), low_norm))
    other_c = swap(low_terms_c, "tp", 0)

    last_pair = all_after(last_pair, cont_out)
    last_part = add_low(last_pair)
    late = [other_p, other_c, blocks[0], ffn_mine, ffn_other]
    other_p, other_c, home, ffn_mine, ffn_other = all_after(late, last_part)
    first = core_i == 0
    ffn_sum = jnp.concatenate(
        [jnp.where(first, ffn_mine, ffn_other), jnp.where(first, ffn_other, ffn_mine)], axis=1
    ).astype(F32)
    ffn_sums = lax.optimization_barrier((ffn_sum[0], ffn_sum[1].T))
    norm_rows = norm_rows + other_c[rows_c : rows_c + 4].astype(F32)
    norm_cut = norm_rows.reshape(4, seq_n, tp_n, -1)
    norm_cut = lax.dynamic_index_in_dim(norm_cut, tp_i, 2, keepdims=False)
    columns = norm_cut.shape[2]
    norm_cut = norm_cut.transpose(1, 0, 2).reshape(seq_n, -1)
    norm_pad = jnp.pad(norm_cut, ((0, 0), (0, 16 * local_width - norm_cut.shape[1])))
    norm_pad = norm_pad.astype(BF).reshape(seq_n, 16, local_width)
    slab_rows = last_part.shape[0] * last_part.shape[-2]
    last_part = last_part.reshape(last_part.shape[0], seq_n, -1, local_width)

    def block(at):
        slabs = lax.dynamic_index_in_dim(last_part, at, 1, keepdims=False)
        norms = lax.dynamic_index_in_dim(norm_pad, at, 0, keepdims=False)
        return jnp.concatenate([slabs.reshape(slab_rows, local_width), norms])

    last_pieces = [block(seq_i)] + [
        lax.ppermute(block(seq_i ^ at), "seq", [(j, j ^ at) for j in range(seq_n)])
        for at in range(1, seq_n)
    ]

    first_p = mine_p.astype(F32) + other_p.astype(F32) + home.astype(F32)
    first_p = lax.optimization_barrier(first_p.astype(BF))
    gathered_p = swap(first_p, "tp", 0)
    first_c = low_terms_c[:rows_c].astype(F32) + other_c[:rows_c].astype(F32)
    out_terms_p = lax.optimization_barrier(wide_dot(after(act_p, first_p), ffn_out).astype(BF))
    out_other_p = swap(out_terms_p, "tp", 0)

    last_pieces = all_after(last_pieces, *ffn_sums)
    last_mine = sum(piece.astype(F32) for piece in last_pieces).astype(BF)
    gathered_p, out_other_p = all_after([gathered_p, out_other_p], last_mine)
    first = tp_i == 0
    first_p = jnp.concatenate(
        [jnp.where(first, first_p, gathered_p), jnp.where(first, gathered_p, first_p)]
    ).astype(F32)
    out_p = out_terms_p.astype(F32) + out_other_p.astype(F32)
    prompt_out = (resid_p + out_p).astype(BF)[None]
    cont_grad = (grad_c + norm_back(one_c, inv_c, first_c, gains[0])).astype(BF)[None, None]
    prompt_grad = (grad_p + norm_back(one_p, inv_p, first_p, gains[0])).astype(BF)[None]
    last_sum, norm_sum = gather_last(last_mine, slab_rows, last_part.shape[0], (prompt_grad, cont_grad))
    norm_sum = norm_sum.reshape(-1)[: 4 * columns].reshape(4, columns)
    return (
        prompt_out,
        cont_out,
        prompt_grad,
        cont_grad,
        last_sum[:3],
        last_sum[3].T,
        *ffn_sums,
        norm_sum[:2],
        norm_sum[2:],
    )


def solution(mesh):
    placed = (
        P("grp", "seq", None),
        P("grp", "seq", None, None),
        P("grp", "seq", None),
        P("grp", "seq", None, None),
        P("grp", "seq"),
        P(None, None, "tp"),
        P("tp", None),
        P(None, "tp"),
        P("tp", None),
        P(),
        P(),
    )
    return jax.shard_map(
        body,
        mesh=mesh,
        in_specs=placed,
        out_specs=(
            P("grp", "seq", None),
            P("grp", "seq", None, None),
            P("grp", "seq", None),
            P("grp", "seq", None, None),
            P(None, "seq", "tp"),
            P("tp", "seq"),
            P("seq", "tp"),
            P("tp", "seq"),
            P(None, ("seq", "tp")),
            P(None, ("seq", "tp")),
        ),
        check_vma=False,
    )
```
